128 devices in a mesh: lon: 16 (over x, z_lo, core), lat: 8 (over y, z_hi).
Axes of the slice: x: 4, y: 4, z: 4 (z_hi: 2, z_lo: 2; z = z_hi * 2 + z_lo), core: 2. Of those that a mesh axis runs over, the one named last changes fastest.
Arguments:
- tracers: float32 [12, 512, 8192], P(None, 'lat', 'lon'), may hold values from -6 to 6
- lon_shift: int32 [2, 12, 512], P(None, None, 'lat'), may hold values from -255 to 255, as said below
- lon_frac: float32 [2, 12, 512], P(None, None, 'lat'), may hold values from 0 to 1
- lat_shift: int32 [2, 12, 512], P(None, None, 'lat'), may hold values from -1 to 1
- lat_frac: float32 [2, 12, 512], P(None, None, 'lat'), may hold values from 0 to 1
- remap_frac: float32 [2, 12, 512], P(None, None, 'lat'), may hold values from 0 to 1
- diffusivity: float32 [12, 512], P(None, 'lat'), may hold values from 0.1 to 3
Outputs:
- advected: float32 [12, 512, 8192], P(None, 'lat', 'lon')
The draws below stay inside these ranges and needn't reach their ends.
Inputs may be any that keep to these rules, and one draw needn't show every extreme that they name: In latitude row j, with e = |2 * j - 511|, |lon_shift| is at most min(255, 64 * 512 // (513 - e)).
All inputs are finite; a program needn't handle non-finite values.
Results may differ from the reference program's by a relative error of at most 0.00002.
Values sent between devices are 32-bit elements; how exact they have to be, the bound alone decides.
A program may use at most 64 MiB of HBM per device.

```python
import math
import jax
import jax.numpy as jnp

NTR = 8
LEV = 12
STEPS = 2
CLON = 64
NLON = 1024
NLAT = 512


def draw_lon_shift(key, part):
    row_index = jnp.arange(NLAT, dtype=jnp.int32)
    distance = jnp.abs(2 * row_index + 1 - NLAT)
    ceiling = NLON // 4 - 1
    limits = jnp.minimum(ceiling, CLON * NLAT // (NLAT + 1 - distance))
    limits = jnp.broadcast_to(limits[None, None, :], (STEPS, LEV, NLAT)).astype(jnp.int32)
    drawn = jax.random.randint(key, (STEPS, LEV, NLAT), -limits, limits + 1, dtype=jnp.int32)
    drawn = drawn.at[0, 0, 0].set(ceiling)
    drawn = drawn.at[0, 0, NLAT - 1].set(-ceiling)
    return drawn


def with_ends(values, own_key, least, high):
    longest = values.shape.index(max(values.shape))
    spots = []
    for shift in (0, 1):
        where = [jax.random.randint(jax.random.fold_in(own_key, axis), (), 0, length) for axis, length in enumerate(values.shape)]
        where[longest] = (where[longest] + shift) % values.shape[longest]
        spots.append(tuple(where))
    return values.at[spots[0]].set(least).at[spots[1]].set(high)


def block_levels(own_key, shape, pieces, smallest, largest):
    factor_of, own = 1.0, jax.random.fold_in(own_key, 6)
    for dim, blocks in pieces:
        steps = jnp.exp(jax.random.uniform(jax.random.fold_in(own, dim), (blocks,), jnp.float32, smallest / len(pieces), largest / len(pieces)))
        factor_of = factor_of * jnp.repeat(steps, shape[dim] // blocks).reshape([-1 if axis == dim else 1 for axis in range(len(shape))])
    return factor_of


def normal_values(key, shape, spread, most, cuts=(), held_as=jnp.bfloat16):
    loudness = block_levels(key, shape, cuts, -0.22, 0.18) if cuts else 1.0
    array = jax.random.normal(key, shape, jnp.float32) * spread * loudness
    return jnp.minimum(jnp.maximum(array, -most), most).astype(held_as)


def setup_inputs(seed: int = 0) -> dict:
    seeds = jax.random.split(jax.random.key(seed), 8)
    return {
        "tracers": normal_values(seeds[0], (LEV, NLAT, NLON * NTR), 1.0, 6.0, ((1, 8), (2, 16)), jnp.float32),
        "lon_shift": draw_lon_shift(jax.random.fold_in(seeds[7], 71), 0),
        "lon_frac": jnp.clip(1.0 * jax.random.uniform(seeds[2], (STEPS, LEV, NLAT), jnp.float32) ** block_levels(seeds[2], (STEPS, LEV, NLAT), ((2, 8),), -0.2, 0.2), 0.0, 1.0),
        "lat_shift": with_ends(jax.random.randint(seeds[3], (STEPS, LEV, NLAT), -1, 2), jax.random.fold_in(seeds[3], 1), -1, 1).astype(jnp.int32),
        "lat_frac": jnp.clip(1.0 * jax.random.uniform(seeds[4], (STEPS, LEV, NLAT), jnp.float32) ** block_levels(seeds[4], (STEPS, LEV, NLAT), ((2, 8),), -0.2, 0.2), 0.0, 1.0),
        "remap_frac": jnp.clip(1.0 * jax.random.uniform(seeds[5], (STEPS, LEV, NLAT), jnp.float32) ** block_levels(seeds[5], (STEPS, LEV, NLAT), ((2, 8),), -0.2, 0.2), 0.0, 1.0),
        "diffusivity": jnp.clip(jnp.exp(math.log(3.0) - 3.4011974 * jax.random.uniform(seeds[6], (LEV, NLAT), jnp.float32) ** block_levels(seeds[6], (LEV, NLAT), ((1, 8),), -0.2, 0.2)), 0.1, 3.0),
    }


def cubic_weights(fraction):
    w_zero = -fraction * (fraction - 1.0) * (fraction - 2.0) / 6.0
    w_one = (fraction + 1.0) * (fraction - 1.0) * (fraction - 2.0) / 2.0
    w_two = -(fraction + 1.0) * fraction * (fraction - 2.0) / 2.0
    w_three = (fraction + 1.0) * fraction * (fraction - 1.0) / 6.0
    return (w_zero, w_one, w_two, w_three)


def lat_step(padded, offset, fraction, row_count):
    weights = cubic_weights(fraction)
    summed = None
    for place_index in range(6):
        row_delta = place_index - 2
        coeff = jnp.zeros_like(fraction)
        for tap_index in range(4):
            coeff = coeff + jnp.where(offset == (tap_index - 1) - row_delta, weights[tap_index], 0.0)
        addend = coeff[:, :, None] * padded[:, 1 + place_index: 1 + place_index + row_count, :]
        summed = addend if summed is None else summed + addend
    return summed


def lon_step(wrapped, fraction, tracer_count):
    weights = cubic_weights(fraction)
    width_cols = wrapped.shape[2] - 4 * tracer_count
    summed = None
    for tap_index in range(4):
        offset_cols = (1 + tap_index) * tracer_count
        addend = weights[tap_index][:, :, None] * wrapped[:, :, offset_cols: offset_cols + width_cols]
        summed = addend if summed is None else summed + addend
    return summed


def remap(tracer_field, fraction):
    level_above = jnp.concatenate([tracer_field[1:], tracer_field[-1:]], axis=0)
    return (1.0 - fraction)[:, :, None] * tracer_field + fraction[:, :, None] * level_above


def diffuse(tracer_field, kappa):
    levels = tracer_field.shape[0]
    face_kappa = 0.5 * (kappa[:-1] + kappa[1:])
    zero_face = jnp.zeros_like(kappa[:1])
    face_below = jnp.concatenate([zero_face, face_kappa], axis=0)
    face_above = jnp.concatenate([face_kappa, zero_face], axis=0)
    ratio_prev = jnp.zeros_like(kappa[0])
    solved_prev = jnp.zeros_like(tracer_field[0])
    ratios = []
    solveds = []
    for level_index in range(levels):
        below = face_below[level_index]
        above = face_above[level_index]
        pivot_value = 1.0 + below + above + below * ratio_prev
        ratio_now = -above / pivot_value
        solved_now = (tracer_field[level_index] + below[:, None] * solved_prev) / pivot_value[:, None]
        ratios.append(ratio_now)
        solveds.append(solved_now)
        ratio_prev = ratio_now
        solved_prev = solved_now
    results = [None] * levels
    results[levels - 1] = solveds[levels - 1]
    for level_index in range(levels - 2, -1, -1):
        results[level_index] = solveds[level_index] - ratios[level_index][:, None] * results[level_index + 1]
    return jnp.stack(results, axis=0)


def reference(tracers, lon_shift, lon_frac, lat_shift, lat_frac, remap_frac, diffusivity):
    tracer_field = tracers
    for time_step in range(STEPS):
        padded = jnp.pad(tracer_field, ((0, 0), (3, 3), (0, 0)))
        tracer_field = lat_step(padded, lat_shift[time_step], lat_frac[time_step], NLAT)
        split_view = tracer_field.reshape(LEV, NLAT, NLON, NTR)
        cell_index = jnp.arange(NLON, dtype=jnp.int32)
        source = jnp.remainder(cell_index[None, None, :] - lon_shift[time_step][:, :, None], NLON).astype(jnp.int32)
        source = jnp.broadcast_to(source[:, :, :, None], split_view.shape)
        shifted = jnp.take_along_axis(split_view, source, axis=2).reshape(LEV, NLAT, NLON * NTR)
        wrapped = jnp.concatenate([shifted[:, :, -2 * NTR:], shifted, shifted[:, :, :2 * NTR]], axis=2)
        tracer_field = lon_step(wrapped, lon_frac[time_step], NTR)
        tracer_field = remap(tracer_field, remap_frac[time_step])
        tracer_field = diffuse(tracer_field, diffusivity)
    return tracer_field
```

```python
import jax
import jax.numpy as jnp
from jax import lax
from jax.sharding import PartitionSpec as P

NTR = 8
STEPS = 2


def from_behind(x, axis, by):
    peers = lax.axis_size(axis)
    return lax.ppermute(x, axis, [(i, (i + by) % peers) for i in range(peers)])


def with_halo(block, sides, width, periodic):
    for axis, dim in sides:
        count = lax.axis_size(axis)
        forward = [(i, i + 1) for i in range(count - 1)]
        if periodic:
            forward.append((count - 1, 0))
        backward = [(target, source) for source, target in forward]
        low = lax.ppermute(
            lax.slice_in_dim(block, block.shape[dim] - width, None, axis=dim), axis, forward
        )
        high = lax.ppermute(lax.slice_in_dim(block, 0, width, axis=dim), axis, backward)
        block = jnp.concatenate([low, block, high], axis=dim)
    return block


def cubic_weights(fraction):
    w_zero = -fraction * (fraction - 1.0) * (fraction - 2.0) / 6.0
    w_one = (fraction + 1.0) * (fraction - 1.0) * (fraction - 2.0) / 2.0
    w_two = -(fraction + 1.0) * fraction * (fraction - 2.0) / 2.0
    w_three = (fraction + 1.0) * fraction * (fraction - 1.0) / 6.0
    return (w_zero, w_one, w_two, w_three)


def lat_step(padded, offset, fraction, row_count):
    weights = cubic_weights(fraction)
    summed = None
    for place_index in range(6):
        row_delta = place_index - 2
        coeff = jnp.zeros_like(fraction)
        for tap_index in range(4):
            coeff = coeff + jnp.where(offset == tap_index - 1 - row_delta, weights[tap_index], 0.0)
        addend = coeff[:, :, None] * padded[:, 1 + place_index : 1 + place_index + row_count, :]
        summed = addend if summed is None else summed + addend
    return summed


def lon_step(wrapped, fraction, tracer_count):
    weights = cubic_weights(fraction)
    width_cols = wrapped.shape[2] - 4 * tracer_count
    summed = None
    for tap_index in range(4):
        offset_cols = (1 + tap_index) * tracer_count
        addend = (
            weights[tap_index][:, :, None] * wrapped[:, :, offset_cols : offset_cols + width_cols]
        )
        summed = addend if summed is None else summed + addend
    return summed


def remap(tracer_field, fraction):
    level_above = jnp.concatenate([tracer_field[1:], tracer_field[-1:]], axis=0)
    return (1.0 - fraction)[:, :, None] * tracer_field + fraction[:, :, None] * level_above


def diffuse(tracer_field, kappa):
    levels = tracer_field.shape[0]
    face_kappa = 0.5 * (kappa[:-1] + kappa[1:])
    zero_face = jnp.zeros_like(kappa[:1])
    face_below = jnp.concatenate([zero_face, face_kappa], axis=0)
    face_above = jnp.concatenate([face_kappa, zero_face], axis=0)
    ratio_prev = jnp.zeros_like(kappa[0])
    solved_prev = jnp.zeros_like(tracer_field[0])
    ratios = []
    solveds = []
    for level_index in range(levels):
        below = face_below[level_index]
        above = face_above[level_index]
        pivot_value = 1.0 + below + above + below * ratio_prev
        ratio_now = -above / pivot_value
        solved_now = (tracer_field[level_index] + below[:, None] * solved_prev) / pivot_value[
            :, None
        ]
        ratios.append(ratio_now)
        solveds.append(solved_now)
        ratio_prev = ratio_now
        solved_prev = solved_now
    results = [None] * levels
    results[levels - 1] = solveds[levels - 1]
    for level_index in range(levels - 2, -1, -1):
        results[level_index] = (
            solveds[level_index] - ratios[level_index][:, None] * results[level_index + 1]
        )
    return jnp.stack(results, axis=0)


def bit_mask(amount, position):
    return (amount // 2**position % 2 == 1)[:, :, None]


def to_columns(block):
    levels, rows, width = block.shape
    cells = width // NTR
    devices = lax.axis_size("lon")
    halves = devices // NTR
    parts = block.reshape(levels, halves, rows // halves, cells, NTR)
    parts = parts.transpose(4, 1, 0, 2, 3).reshape(devices, levels, rows // halves, cells)
    got = lax.all_to_all(parts, "lon", 0, 0, tiled=True)
    return got.transpose(1, 2, 0, 3).reshape(levels, rows // halves, devices * cells)


def from_columns(field, rows):
    levels, own_rows, width = field.shape
    devices = lax.axis_size("lon")
    halves = devices // NTR
    cells = width // devices
    parts = field.reshape(levels, own_rows, devices, cells).transpose(2, 0, 1, 3)
    got = lax.all_to_all(parts, "lon", 0, 0, tiled=True)
    got = got.reshape(NTR, halves, levels, own_rows, cells).transpose(2, 1, 3, 4, 0)
    return got.reshape(levels, rows, cells * NTR)


def lat_halo(field, width):
    lon_n = lax.axis_size("lon")
    lat_n = lax.axis_size("lat")
    halves = lon_n // NTR
    up = []
    for b in range(lat_n):
        for l in range(lon_n):
            t, h = l // halves, l % halves
            g = b * halves + h
            if g + 1 < lat_n * halves:
                nb, nh = (g + 1) // halves, (g + 1) % halves
                up.append((l * lat_n + b, (t * halves + nh) * lat_n + nb))
    down = [(d, s) for s, d in up]
    rows = field.shape[1]
    below = lax.ppermute(field[:, rows - width :], ("lon", "lat"), up)
    above = lax.ppermute(field[:, :width], ("lon", "lat"), down)
    return jnp.concatenate([below, field, above], axis=1)


def roll_rows(field, amount):
    width = field.shape[2]
    current = field
    for position in range(width.bit_length() - 1):
        moved = jnp.roll(current, 2**position, axis=2)
        current = jnp.where(bit_mask(amount, position), moved, current)
    return current


def lon_cubic(shifted, fraction):
    weights = cubic_weights(fraction)
    taps = [jnp.roll(shifted, 1 - p, axis=2) for p in range(4)]
    summed = None
    for p in range(4):
        addend = weights[p][:, :, None] * taps[p]
        summed = addend if summed is None else summed + addend
    return summed


def own_rows(values, count):
    halves = lax.axis_size("lon") // NTR
    start = (lax.axis_index("lon") % halves) * count
    return lax.dynamic_slice_in_dim(values, start, count, axis=values.ndim - 1)


def per_device(tracers, lon_shift, lon_frac, lat_shift, lat_frac, remap_frac, diffusivity):
    rows = tracers.shape[1]
    field = to_columns(tracers)
    count = field.shape[1]
    width = field.shape[2]
    lon_shift, lon_frac, lat_shift, lat_frac, remap_frac, diffusivity = (
        own_rows(v, count) for v in (lon_shift, lon_frac, lat_shift, lat_frac, remap_frac, diffusivity)
    )
    for time_step in range(STEPS):
        padded = lat_halo(field, 3)
        field = lat_step(padded, lat_shift[time_step], lat_frac[time_step], count)
        amount = jnp.remainder(lon_shift[time_step], width)
        field = lon_cubic(roll_rows(field, amount), lon_frac[time_step])
        field = remap(field, remap_frac[time_step])
        field = diffuse(field, diffusivity)
    return from_columns(field, rows)


def solution(mesh):
    in_specs = (
        P(None, "lat", "lon"),
        P(None, None, "lat"),
        P(None, None, "lat"),
        P(None, None, "lat"),
        P(None, None, "lat"),
        P(None, None, "lat"),
        P(None, "lat"),
    )
    out_specs = P(None, "lat", "lon")
    return jax.shard_map(
        per_device, mesh=mesh, in_specs=in_specs, out_specs=out_specs, check_vma=False
    )
```

```python
import functools

import jax
import jax.numpy as jnp
from jax import lax
from jax.experimental import pallas as pl
from jax.experimental.pallas import tpu as pltpu
from jax.sharding import PartitionSpec as P

NTR = 8
STEPS = 2


def from_behind(x, axis, by):
    peers = lax.axis_size(axis)
    return lax.ppermute(x, axis, [(i, (i + by) % peers) for i in range(peers)])


def with_halo(block, sides, width, periodic):
    for axis, dim in sides:
        count = lax.axis_size(axis)
        forward = [(i, i + 1) for i in range(count - 1)]
        if periodic:
            forward.append((count - 1, 0))
        backward = [(target, source) for source, target in forward]
        low = lax.ppermute(
            lax.slice_in_dim(block, block.shape[dim] - width, None, axis=dim), axis, forward
        )
        high = lax.ppermute(lax.slice_in_dim(block, 0, width, axis=dim), axis, backward)
        block = jnp.concatenate([low, block, high], axis=dim)
    return block


def cubic_weights(fraction):
    w_zero = -fraction * (fraction - 1.0) * (fraction - 2.0) / 6.0
    w_one = (fraction + 1.0) * (fraction - 1.0) * (fraction - 2.0) / 2.0
    w_two = -(fraction + 1.0) * fraction * (fraction - 2.0) / 2.0
    w_three = (fraction + 1.0) * fraction * (fraction - 1.0) / 6.0
    return (w_zero, w_one, w_two, w_three)


def lat_step(padded, offset, fraction, row_count):
    weights = cubic_weights(fraction)
    summed = None
    for place_index in range(6):
        row_delta = place_index - 2
        coeff = jnp.zeros_like(fraction)
        for tap_index in range(4):
            coeff = coeff + jnp.where(offset == tap_index - 1 - row_delta, weights[tap_index], 0.0)
        addend = coeff[:, :, None] * padded[:, 1 + place_index : 1 + place_index + row_count, :]
        summed = addend if summed is None else summed + addend
    return summed


def lon_step(wrapped, fraction, tracer_count):
    weights = cubic_weights(fraction)
    width_cols = wrapped.shape[2] - 4 * tracer_count
    summed = None
    for tap_index in range(4):
        offset_cols = (1 + tap_index) * tracer_count
        addend = (
            weights[tap_index][:, :, None] * wrapped[:, :, offset_cols : offset_cols + width_cols]
        )
        summed = addend if summed is None else summed + addend
    return summed


def remap(tracer_field, fraction):
    level_above = jnp.concatenate([tracer_field[1:], tracer_field[-1:]], axis=0)
    return (1.0 - fraction)[:, :, None] * tracer_field + fraction[:, :, None] * level_above


def diffuse(tracer_field, kappa):
    levels = tracer_field.shape[0]
    face_kappa = 0.5 * (kappa[:-1] + kappa[1:])
    zero_face = jnp.zeros_like(kappa[:1])
    face_below = jnp.concatenate([zero_face, face_kappa], axis=0)
    face_above = jnp.concatenate([face_kappa, zero_face], axis=0)
    ratio_prev = jnp.zeros_like(kappa[0])
    solved_prev = jnp.zeros_like(tracer_field[0])
    ratios = []
    solveds = []
    for level_index in range(levels):
        below = face_below[level_index]
        above = face_above[level_index]
        pivot_value = 1.0 + below + above + below * ratio_prev
        ratio_now = -above / pivot_value
        solved_now = (tracer_field[level_index] + below[:, None] * solved_prev) / pivot_value[
            :, None
        ]
        ratios.append(ratio_now)
        solveds.append(solved_now)
        ratio_prev = ratio_now
        solved_prev = solved_now
    results = [None] * levels
    results[levels - 1] = solveds[levels - 1]
    for level_index in range(levels - 2, -1, -1):
        results[level_index] = (
            solveds[level_index] - ratios[level_index][:, None] * results[level_index + 1]
        )
    return jnp.stack(results, axis=0)


def bit_mask(amount, position):
    return (amount // 2**position % 2 == 1)[:, :, None]


PAIR = 2


def pair_order(cells):
    cols = jnp.arange(cells * NTR)
    cell, tracer = cols // NTR, cols % NTR
    target = (tracer // PAIR) * cells * PAIR + cell * PAIR + tracer % PAIR
    return target


def exact_permute(block, target, inverse):
    width = block.shape[-1]
    flat = block.reshape(-1, width)
    cols = jnp.arange(width)
    if inverse:
        matrix = cols[:, None] == target[None, :]
    else:
        matrix = cols[None, :] == target[:, None]
    matrix = matrix.astype(jnp.bfloat16)
    rest = flat
    total = None
    for _ in range(3):
        part = lax.reduce_precision(rest, exponent_bits=8, mantissa_bits=7)
        rest = rest - part
        piece = jnp.dot(part.astype(jnp.bfloat16), matrix, preferred_element_type=jnp.float32)
        total = piece if total is None else total + piece
    return total.reshape(block.shape)


def exchange_kernel(src_ref, dst_ref, send_sem, recv_sem, local_sem, *, src_at, dst_at):
    count = lax.axis_size("lon")
    me = lax.axis_index("lon")
    lat = lax.axis_index("lat")
    barrier = pltpu.get_barrier_semaphore()
    for offset in range(1, count):
        peer = lax.rem(me + offset, count)
        pl.semaphore_signal(barrier, 1, device_id=(peer, lat), device_id_type=pl.DeviceIdType.MESH)
    pl.semaphore_wait(barrier, count - 1)
    copies = []
    for offset in range(1, count):
        peer = lax.rem(me + offset, count)
        copy = pltpu.make_async_remote_copy(
            src_ref=src_at(src_ref, peer),
            dst_ref=dst_at(dst_ref, me),
            send_sem=send_sem.at[offset],
            recv_sem=recv_sem.at[offset],
            device_id=(peer, lat),
            device_id_type=pl.DeviceIdType.MESH,
        )
        copy.start()
        copies.append(copy)
    local = pltpu.make_async_copy(src_at(src_ref, me), dst_at(dst_ref, me), local_sem)
    local.start()
    for copy in copies:
        copy.wait_send()
    for copy in copies:
        copy.wait_recv()
    local.wait()


def exchange(block, out_shape, src_at, dst_at, ident):
    count = lax.axis_size("lon")
    return pl.pallas_call(
        functools.partial(exchange_kernel, src_at=src_at, dst_at=dst_at),
        out_shape=jax.ShapeDtypeStruct(out_shape, block.dtype),
        in_specs=[pl.BlockSpec(memory_space=pl.ANY)],
        out_specs=pl.BlockSpec(memory_space=pl.ANY),
        scratch_shapes=[
            pltpu.SemaphoreType.DMA((count,)),
            pltpu.SemaphoreType.DMA((count,)),
            pltpu.SemaphoreType.DMA,
        ],
        compiler_params=pltpu.CompilerParams(collective_id=ident, has_side_effects=True),
    )(block)


def to_columns(block):
    levels, rows, width = block.shape
    cells = width // NTR
    devices = lax.axis_size("lon")
    parts = devices // (NTR // PAIR)
    count = rows // parts
    lane = cells * PAIR
    moved = exact_permute(block, pair_order(cells), False)

    def src_at(ref, peer):
        return ref.at[:, pl.ds((peer % parts) * count, count), pl.ds((peer // parts) * lane, lane)]

    def dst_at(ref, sender):
        return ref.at[:, :, pl.ds(sender * lane, lane)]

    return exchange(moved, (levels, count, devices * lane), src_at, dst_at, 0)


def from_columns(field, rows):
    levels, count, width = field.shape
    devices = lax.axis_size("lon")
    parts = devices // (NTR // PAIR)
    lane = width // devices
    cells = lane // PAIR

    def src_at(ref, peer):
        return ref.at[:, :, pl.ds(peer * lane, lane)]

    def dst_at(ref, sender):
        return ref.at[:, pl.ds((sender % parts) * count, count), pl.ds((sender // parts) * lane, lane)]

    moved = exchange(field, (levels, rows, cells * NTR), src_at, dst_at, 1)
    return exact_permute(moved, pair_order(cells), True)


def lat_halo(field, width):
    lon_n = lax.axis_size("lon")
    lat_n = lax.axis_size("lat")
    parts = lon_n // (NTR // PAIR)
    up = []
    for b in range(lat_n):
        for l in range(lon_n):
            t, h = l // parts, l % parts
            g = b * parts + h
            if g + 1 < lat_n * parts:
                nb, nh = (g + 1) // parts, (g + 1) % parts
                up.append((l * lat_n + b, (t * parts + nh) * lat_n + nb))
    down = [(d, s) for s, d in up]
    rows = field.shape[1]
    below = lax.ppermute(field[:, rows - width :], ("lon", "lat"), up)
    above = lax.ppermute(field[:, :width], ("lon", "lat"), down)
    return jnp.concatenate([below, field, above], axis=1)


def roll_rows(field, amount):
    cells = field.shape[2] // PAIR
    current = field
    for position in range(cells.bit_length() - 1):
        moved = jnp.roll(current, PAIR * 2**position, axis=2)
        current = jnp.where(bit_mask(amount, position), moved, current)
    return current


def lon_cubic(shifted, fraction):
    weights = cubic_weights(fraction)
    taps = [jnp.roll(shifted, PAIR * (1 - p), axis=2) for p in range(4)]
    summed = None
    for p in range(4):
        addend = weights[p][:, :, None] * taps[p]
        summed = addend if summed is None else summed + addend
    return summed


def own_rows(values, count):
    parts = lax.axis_size("lon") // (NTR // PAIR)
    start = (lax.axis_index("lon") % parts) * count
    return lax.dynamic_slice_in_dim(values, start, count, axis=values.ndim - 1)


def per_device(tracers, lon_shift, lon_frac, lat_shift, lat_frac, remap_frac, diffusivity):
    rows = tracers.shape[1]
    field = to_columns(tracers)
    count = field.shape[1]
    width = field.shape[2]
    lon_shift, lon_frac, lat_shift, lat_frac, remap_frac, diffusivity = (
        own_rows(v, count) for v in (lon_shift, lon_frac, lat_shift, lat_frac, remap_frac, diffusivity)
    )
    for time_step in range(STEPS):
        padded = lat_halo(field, 3)
        field = lat_step(padded, lat_shift[time_step], lat_frac[time_step], count)
        amount = jnp.remainder(lon_shift[time_step], width // PAIR)
        field = lon_cubic(roll_rows(field, amount), lon_frac[time_step])
        field = remap(field, remap_frac[time_step])
        field = diffuse(field, diffusivity)
    return from_columns(field, rows)


def solution(mesh):
    in_specs = (
        P(None, "lat", "lon"),
        P(None, None, "lat"),
        P(None, None, "lat"),
        P(None, None, "lat"),
        P(None, None, "lat"),
        P(None, None, "lat"),
        P(None, "lat"),
    )
    out_specs = P(None, "lat", "lon")
    return jax.shard_map(
        per_device, mesh=mesh, in_specs=in_specs, out_specs=out_specs, check_vma=False
    )
```

```python
import functools

import jax
import jax.numpy as jnp
from jax import lax
from jax.experimental import pallas as pl
from jax.experimental.pallas import tpu as pltpu
from jax.sharding import PartitionSpec as P

NTR = 8
STEPS = 2


def from_behind(x, axis, by):
    peers = lax.axis_size(axis)
    return lax.ppermute(x, axis, [(i, (i + by) % peers) for i in range(peers)])


def with_halo(block, sides, width, periodic):
    for axis, dim in sides:
        count = lax.axis_size(axis)
        forward = [(i, i + 1) for i in range(count - 1)]
        if periodic:
            forward.append((count - 1, 0))
        backward = [(target, source) for source, target in forward]
        low = lax.ppermute(
            lax.slice_in_dim(block, block.shape[dim] - width, None, axis=dim), axis, forward
        )
        high = lax.ppermute(lax.slice_in_dim(block, 0, width, axis=dim), axis, backward)
        block = jnp.concatenate([low, block, high], axis=dim)
    return block


def cubic_weights(fraction):
    w_zero = -fraction * (fraction - 1.0) * (fraction - 2.0) / 6.0
    w_one = (fraction + 1.0) * (fraction - 1.0) * (fraction - 2.0) / 2.0
    w_two = -(fraction + 1.0) * fraction * (fraction - 2.0) / 2.0
    w_three = (fraction + 1.0) * fraction * (fraction - 1.0) / 6.0
    return (w_zero, w_one, w_two, w_three)


def lat_step(padded, offset, fraction, row_count):
    weights = cubic_weights(fraction)
    summed = None
    for place_index in range(6):
        row_delta = place_index - 2
        coeff = jnp.zeros_like(fraction)
        for tap_index in range(4):
            coeff = coeff + jnp.where(offset == tap_index - 1 - row_delta, weights[tap_index], 0.0)
        addend = coeff[:, :, None] * padded[:, 1 + place_index : 1 + place_index + row_count, :]
        summed = addend if summed is None else summed + addend
    return summed


def lon_step(wrapped, fraction, tracer_count):
    weights = cubic_weights(fraction)
    width_cols = wrapped.shape[2] - 4 * tracer_count
    summed = None
    for tap_index in range(4):
        offset_cols = (1 + tap_index) * tracer_count
        addend = (
            weights[tap_index][:, :, None] * wrapped[:, :, offset_cols : offset_cols + width_cols]
        )
        summed = addend if summed is None else summed + addend
    return summed


def remap(tracer_field, fraction):
    level_above = jnp.concatenate([tracer_field[1:], tracer_field[-1:]], axis=0)
    return (1.0 - fraction)[:, :, None] * tracer_field + fraction[:, :, None] * level_above


def diffuse(tracer_field, kappa):
    levels = tracer_field.shape[0]
    face_kappa = 0.5 * (kappa[:-1] + kappa[1:])
    zero_face = jnp.zeros_like(kappa[:1])
    face_below = jnp.concatenate([zero_face, face_kappa], axis=0)
    face_above = jnp.concatenate([face_kappa, zero_face], axis=0)
    ratio_prev = jnp.zeros_like(kappa[0])
    solved_prev = jnp.zeros_like(tracer_field[0])
    ratios = []
    solveds = []
    for level_index in range(levels):
        below = face_below[level_index]
        above = face_above[level_index]
        pivot_value = 1.0 + below + above + below * ratio_prev
        ratio_now = -above / pivot_value
        solved_now = (tracer_field[level_index] + below[:, None] * solved_prev) / pivot_value[
            :, None
        ]
        ratios.append(ratio_now)
        solveds.append(solved_now)
        ratio_prev = ratio_now
        solved_prev = solved_now
    results = [None] * levels
    results[levels - 1] = solveds[levels - 1]
    for level_index in range(levels - 2, -1, -1):
        results[level_index] = (
            solveds[level_index] - ratios[level_index][:, None] * results[level_index + 1]
        )
    return jnp.stack(results, axis=0)


def bit_mask(amount, position):
    return (amount // 2**position % 2 == 1)[:, :, None]


PAIR = 2


def pair_order(cells):
    cols = jnp.arange(cells * NTR)
    cell, tracer = cols // NTR, cols % NTR
    target = (tracer // PAIR) * cells * PAIR + cell * PAIR + tracer % PAIR
    return target


def exact_permute(block, target, inverse):
    width = block.shape[-1]
    flat = block.reshape(-1, width)
    cols = jnp.arange(width)
    if inverse:
        matrix = cols[:, None] == target[None, :]
    else:
        matrix = cols[None, :] == target[:, None]
    matrix = matrix.astype(jnp.bfloat16)
    rest = flat
    total = None
    for _ in range(3):
        part = lax.reduce_precision(rest, exponent_bits=8, mantissa_bits=7)
        rest = rest - part
        piece = jnp.dot(part.astype(jnp.bfloat16), matrix, preferred_element_type=jnp.float32)
        total = piece if total is None else total + piece
    return total.reshape(block.shape)


def exchange_kernel(src_ref, dst_ref, send_sem, recv_sem, local_sem, *, src_at, dst_at):
    count = lax.axis_size("lon")
    me = lax.axis_index("lon")
    lat = lax.axis_index("lat")
    barrier = pltpu.get_barrier_semaphore()
    for offset in range(1, count):
        peer = lax.rem(me + offset, count)
        pl.semaphore_signal(barrier, 1, device_id=(peer, lat), device_id_type=pl.DeviceIdType.MESH)
    pl.semaphore_wait(barrier, count - 1)
    copies = []
    for offset in range(1, count):
        peer = lax.rem(me + offset, count)
        copy = pltpu.make_async_remote_copy(
            src_ref=src_at(src_ref, peer),
            dst_ref=dst_at(dst_ref, me),
            send_sem=send_sem.at[offset],
            recv_sem=recv_sem.at[offset],
            device_id=(peer, lat),
            device_id_type=pl.DeviceIdType.MESH,
        )
        copy.start()
        copies.append(copy)
    local = pltpu.make_async_copy(src_at(src_ref, me), dst_at(dst_ref, me), local_sem)
    local.start()
    for copy in copies:
        copy.wait_send()
    for copy in copies:
        copy.wait_recv()
    local.wait()


def exchange(block, out_shape, src_at, dst_at, ident):
    count = lax.axis_size("lon")
    return pl.pallas_call(
        functools.partial(exchange_kernel, src_at=src_at, dst_at=dst_at),
        out_shape=jax.ShapeDtypeStruct(out_shape, block.dtype),
        in_specs=[pl.BlockSpec(memory_space=pl.ANY)],
        out_specs=pl.BlockSpec(memory_space=pl.ANY),
        scratch_shapes=[
            pltpu.SemaphoreType.DMA((count,)),
            pltpu.SemaphoreType.DMA((count,)),
            pltpu.SemaphoreType.DMA,
        ],
        compiler_params=pltpu.CompilerParams(collective_id=ident, has_side_effects=True),
    )(block)


def to_columns(block):
    levels, rows, width = block.shape
    cells = width // NTR
    devices = lax.axis_size("lon")
    parts = devices // (NTR // PAIR)
    count = rows // parts
    lane = cells * PAIR
    moved = exact_permute(block, pair_order(cells), False)

    def src_at(ref, peer):
        return ref.at[:, pl.ds((peer % parts) * count, count), pl.ds((peer // parts) * lane, lane)]

    def dst_at(ref, sender):
        return ref.at[:, :, pl.ds(sender * lane, lane)]

    return exchange(moved, (levels, count, devices * lane), src_at, dst_at, 0)


def from_columns(field, rows):
    levels, count, width = field.shape
    devices = lax.axis_size("lon")
    parts = devices // (NTR // PAIR)
    lane = width // devices
    cells = lane // PAIR

    def src_at(ref, peer):
        return ref.at[:, :, pl.ds(peer * lane, lane)]

    def dst_at(ref, sender):
        return ref.at[:, pl.ds((sender % parts) * count, count), pl.ds((sender // parts) * lane, lane)]

    moved = exchange(field, (levels, rows, cells * NTR), src_at, dst_at, 1)
    return exact_permute(moved, pair_order(cells), True)


def lat_halo(field, width):
    lon_n = lax.axis_size("lon")
    lat_n = lax.axis_size("lat")
    parts = lon_n // (NTR // PAIR)
    up = []
    for b in range(lat_n):
        for l in range(lon_n):
            t, h = l // parts, l % parts
            g = b * parts + h
            if g + 1 < lat_n * parts:
                nb, nh = (g + 1) // parts, (g + 1) % parts
                up.append((l * lat_n + b, (t * parts + nh) * lat_n + nb))
    down = [(d, s) for s, d in up]
    rows = field.shape[1]
    below = lax.ppermute(field[:, rows - width :], ("lon", "lat"), up)
    above = lax.ppermute(field[:, :width], ("lon", "lat"), down)
    return jnp.concatenate([below, field, above], axis=1)


def step_kernel(pad_ref, latc_ref, lonw_ref, bits_ref, keep_ref, take_ref, below_ref, pivot_ref, ratio_ref, out_ref, moved_ref):
    levels, rows, width = out_ref.shape
    stages = bits_ref.shape[0]

    def move_level(k, carry):
        summed = None
        for place in range(latc_ref.shape[0]):
            addend = latc_ref[place, k] * pad_ref[k, pl.ds(1 + place, rows), :]
            summed = addend if summed is None else summed + addend
        current = summed
        for position in range(stages):
            rolled = pltpu.roll(current, PAIR * 2**position, 1)
            current = jnp.where(bits_ref[position, k] != 0, rolled, current)
        summed = None
        for tap in range(4):
            shift = (PAIR * (1 - tap)) % width
            moved = pltpu.roll(current, shift, 1) if shift else current
            addend = lonw_ref[tap, k] * moved
            summed = addend if summed is None else summed + addend
        moved_ref[k] = summed
        return carry

    lax.fori_loop(0, levels, move_level, 0)

    def sweep_down(k, solved_prev):
        above = moved_ref[jnp.minimum(k + 1, levels - 1)]
        remapped = keep_ref[k] * moved_ref[k] + take_ref[k] * above
        solved = (remapped + below_ref[k] * solved_prev) / pivot_ref[k]
        moved_ref[k] = solved
        return solved

    last = lax.fori_loop(0, levels, sweep_down, jnp.zeros((rows, width), jnp.float32))
    out_ref[levels - 1] = last

    def sweep_up(i, result):
        k = levels - 2 - i
        result = moved_ref[k] - ratio_ref[k] * result
        out_ref[k] = result
        return result

    lax.fori_loop(0, levels - 1, sweep_up, last)


def lat_coefficients(offset, fraction):
    weights = cubic_weights(fraction)
    coeffs = []
    for place_index in range(6):
        row_delta = place_index - 2
        coeff = jnp.zeros_like(fraction)
        for tap_index in range(4):
            coeff = coeff + jnp.where(offset == tap_index - 1 - row_delta, weights[tap_index], 0.0)
        coeffs.append(coeff)
    return jnp.stack(coeffs)[..., None]


def diffusion_coefficients(kappa):
    levels = kappa.shape[0]
    face_kappa = 0.5 * (kappa[:-1] + kappa[1:])
    zero_face = jnp.zeros_like(kappa[:1])
    face_below = jnp.concatenate([zero_face, face_kappa], axis=0)
    face_above = jnp.concatenate([face_kappa, zero_face], axis=0)
    ratio_prev = jnp.zeros_like(kappa[0])
    pivots = []
    ratios = []
    for level_index in range(levels):
        below = face_below[level_index]
        above = face_above[level_index]
        pivot_value = 1.0 + below + above + below * ratio_prev
        ratio_now = -above / pivot_value
        pivots.append(pivot_value)
        ratios.append(ratio_now)
        ratio_prev = ratio_now
    return face_below[..., None], jnp.stack(pivots)[..., None], jnp.stack(ratios)[..., None]


def transport_step(padded, latc, lonw, bits, keep, take, below, pivot, ratio):
    levels = padded.shape[0]
    rows = padded.shape[1] - 6
    width = padded.shape[2]
    shape = (levels, rows, width)
    vmem = pl.BlockSpec(memory_space=pltpu.VMEM)
    size = levels * rows * width
    return pl.pallas_call(
        step_kernel,
        out_shape=jax.ShapeDtypeStruct(shape, jnp.float32),
        in_specs=[vmem] * 9,
        out_specs=vmem,
        scratch_shapes=[pltpu.VMEM(shape, jnp.float32)],
        cost_estimate=pl.CostEstimate(flops=60 * size, bytes_accessed=12 * size, transcendentals=0),
    )(padded, latc, lonw, bits, keep, take, below, pivot, ratio)


def own_rows(values, count):
    parts = lax.axis_size("lon") // (NTR // PAIR)
    start = (lax.axis_index("lon") % parts) * count
    return lax.dynamic_slice_in_dim(values, start, count, axis=values.ndim - 1)


def per_device(tracers, lon_shift, lon_frac, lat_shift, lat_frac, remap_frac, diffusivity):
    rows = tracers.shape[1]
    field = to_columns(tracers)
    count = field.shape[1]
    cells = field.shape[2] // PAIR
    lon_shift, lon_frac, lat_shift, lat_frac, remap_frac, diffusivity = (
        own_rows(v, count) for v in (lon_shift, lon_frac, lat_shift, lat_frac, remap_frac, diffusivity)
    )
    below, pivot, ratio = diffusion_coefficients(diffusivity)
    stages = cells.bit_length() - 1
    for time_step in range(STEPS):
        padded = lat_halo(field, 3)
        latc = lat_coefficients(lat_shift[time_step], lat_frac[time_step])
        lonw = jnp.stack(cubic_weights(lon_frac[time_step]))[..., None]
        amount = jnp.remainder(lon_shift[time_step], cells)
        bits = jnp.stack([(amount // 2**position % 2).astype(jnp.int32) for position in range(stages)])[..., None]
        take = remap_frac[time_step][..., None]
        keep = (1.0 - remap_frac[time_step])[..., None]
        field = transport_step(padded, latc, lonw, bits, keep, take, below, pivot, ratio)
    return from_columns(field, rows)


def solution(mesh):
    in_specs = (
        P(None, "lat", "lon"),
        P(None, None, "lat"),
        P(None, None, "lat"),
        P(None, None, "lat"),
        P(None, None, "lat"),
        P(None, None, "lat"),
        P(None, "lat"),
    )
    out_specs = P(None, "lat", "lon")
    return jax.shard_map(
        per_device, mesh=mesh, in_specs=in_specs, out_specs=out_specs, check_vma=False
    )
```

```python
import functools

import jax
import jax.numpy as jnp
from jax import lax
from jax.experimental import pallas as pl
from jax.experimental.pallas import tpu as pltpu
from jax.sharding import PartitionSpec as P

NTR = 8
STEPS = 2


def from_behind(x, axis, by):
    peers = lax.axis_size(axis)
    return lax.ppermute(x, axis, [(i, (i + by) % peers) for i in range(peers)])


def with_halo(block, sides, width, periodic):
    for axis, dim in sides:
        count = lax.axis_size(axis)
        forward = [(i, i + 1) for i in range(count - 1)]
        if periodic:
            forward.append((count - 1, 0))
        backward = [(target, source) for source, target in forward]
        low = lax.ppermute(
            lax.slice_in_dim(block, block.shape[dim] - width, None, axis=dim), axis, forward
        )
        high = lax.ppermute(lax.slice_in_dim(block, 0, width, axis=dim), axis, backward)
        block = jnp.concatenate([low, block, high], axis=dim)
    return block


def cubic_weights(fraction):
    w_zero = -fraction * (fraction - 1.0) * (fraction - 2.0) / 6.0
    w_one = (fraction + 1.0) * (fraction - 1.0) * (fraction - 2.0) / 2.0
    w_two = -(fraction + 1.0) * fraction * (fraction - 2.0) / 2.0
    w_three = (fraction + 1.0) * fraction * (fraction - 1.0) / 6.0
    return (w_zero, w_one, w_two, w_three)


def lat_step(padded, offset, fraction, row_count):
    weights = cubic_weights(fraction)
    summed = None
    for place_index in range(6):
        row_delta = place_index - 2
        coeff = jnp.zeros_like(fraction)
        for tap_index in range(4):
            coeff = coeff + jnp.where(offset == tap_index - 1 - row_delta, weights[tap_index], 0.0)
        addend = coeff[:, :, None] * padded[:, 1 + place_index : 1 + place_index + row_count, :]
        summed = addend if summed is None else summed + addend
    return summed


def lon_step(wrapped, fraction, tracer_count):
    weights = cubic_weights(fraction)
    width_cols = wrapped.shape[2] - 4 * tracer_count
    summed = None
    for tap_index in range(4):
        offset_cols = (1 + tap_index) * tracer_count
        addend = (
            weights[tap_index][:, :, None] * wrapped[:, :, offset_cols : offset_cols + width_cols]
        )
        summed = addend if summed is None else summed + addend
    return summed


def remap(tracer_field, fraction):
    level_above = jnp.concatenate([tracer_field[1:], tracer_field[-1:]], axis=0)
    return (1.0 - fraction)[:, :, None] * tracer_field + fraction[:, :, None] * level_above


def diffuse(tracer_field, kappa):
    levels = tracer_field.shape[0]
    face_kappa = 0.5 * (kappa[:-1] + kappa[1:])
    zero_face = jnp.zeros_like(kappa[:1])
    face_below = jnp.concatenate([zero_face, face_kappa], axis=0)
    face_above = jnp.concatenate([face_kappa, zero_face], axis=0)
    ratio_prev = jnp.zeros_like(kappa[0])
    solved_prev = jnp.zeros_like(tracer_field[0])
    ratios = []
    solveds = []
    for level_index in range(levels):
        below = face_below[level_index]
        above = face_above[level_index]
        pivot_value = 1.0 + below + above + below * ratio_prev
        ratio_now = -above / pivot_value
        solved_now = (tracer_field[level_index] + below[:, None] * solved_prev) / pivot_value[
            :, None
        ]
        ratios.append(ratio_now)
        solveds.append(solved_now)
        ratio_prev = ratio_now
        solved_prev = solved_now
    results = [None] * levels
    results[levels - 1] = solveds[levels - 1]
    for level_index in range(levels - 2, -1, -1):
        results[level_index] = (
            solveds[level_index] - ratios[level_index][:, None] * results[level_index + 1]
        )
    return jnp.stack(results, axis=0)


def bit_mask(amount, position):
    return (amount // 2**position % 2 == 1)[:, :, None]


PAIR = 2


def pair_order(cells):
    cols = jnp.arange(cells * NTR)
    cell, tracer = cols // NTR, cols % NTR
    target = (tracer // PAIR) * cells * PAIR + cell * PAIR + tracer % PAIR
    return target


def exact_permute(block, target, inverse):
    width = block.shape[-1]
    flat = block.reshape(-1, width)
    cols = jnp.arange(width)
    if inverse:
        matrix = cols[:, None] == target[None, :]
    else:
        matrix = cols[None, :] == target[:, None]
    matrix = matrix.astype(jnp.bfloat16)
    rest = flat
    total = None
    for _ in range(3):
        part = lax.reduce_precision(rest, exponent_bits=8, mantissa_bits=7)
        rest = rest - part
        piece = jnp.dot(part.astype(jnp.bfloat16), matrix, preferred_element_type=jnp.float32)
        total = piece if total is None else total + piece
    return total.reshape(block.shape)


GROUP = 4


def exchange_kernel(src_ref, dst_ref, relay_buf, send_sem, recv_sem, local_sem, relay_send, relay_recv, fwd_send, fwd_recv, *, src_at, dst_at):
    count = lax.axis_size("lon")
    ring = count // GROUP
    far = ring // 2
    me = lax.axis_index("lon")
    lat = lax.axis_index("lat")
    x_me, lo_me = me // GROUP, me % GROUP
    levels = relay_buf.shape[1] * 2
    half = levels // 2
    everything = pl.ds(0, levels)
    low_half, high_half = pl.ds(0, half), pl.ds(half, half)

    def device(peer):
        return (peer, lat)

    barrier = pltpu.get_barrier_semaphore()
    for offset in range(1, count):
        peer = lax.rem(me + offset, count)
        pl.semaphore_signal(barrier, 1, device_id=device(peer), device_id_type=pl.DeviceIdType.MESH)
    pl.semaphore_wait(barrier, count - 1)

    peers = [(x_me * GROUP + lax.rem(lo_me + j, GROUP), False, j - 1, j - 1) for j in range(1, GROUP)]
    for dx in range(1, ring):
        for lo in range(GROUP):
            base = GROUP - 1 + (dx - 1) * GROUP
            peers.append((lax.rem(x_me + dx, ring) * GROUP + lo, dx == far, base + lo, base + lo_me))
    copies = []
    arrivals = []
    relays = []
    for peer, split, mine, theirs in peers:
        part = low_half if split else everything
        copy = pltpu.make_async_remote_copy(
            src_ref=src_at(src_ref, peer, part),
            dst_ref=dst_at(dst_ref, me, part),
            send_sem=send_sem.at[mine],
            recv_sem=recv_sem.at[theirs],
            device_id=device(peer),
            device_id_type=pl.DeviceIdType.MESH,
        )
        copy.start()
        copies.append(copy)
        arrivals.append(
            pltpu.make_async_remote_copy(
                src_ref=src_at(src_ref, peer, part),
                dst_ref=dst_at(dst_ref, me, part),
                send_sem=send_sem.at[mine],
                recv_sem=recv_sem.at[mine],
                device_id=device(peer),
                device_id_type=pl.DeviceIdType.MESH,
            )
        )
        if split:
            lo = len(relays)
            helper = lax.rem(x_me + ring - 1, ring) * GROUP + lo
            relay = pltpu.make_async_remote_copy(
                src_ref=src_at(src_ref, peer, high_half),
                dst_ref=relay_buf.at[lo_me],
                send_sem=relay_send.at[lo],
                recv_sem=relay_recv.at[lo_me],
                device_id=device(helper),
                device_id_type=pl.DeviceIdType.MESH,
            )
            relay.start()
            relays.append(relay)
    local = pltpu.make_async_copy(src_at(src_ref, me, everything), dst_at(dst_ref, me, everything), local_sem)
    local.start()

    target = lax.rem(x_me + ring - 1, ring) * GROUP + lo_me
    forwards = []
    for lo in range(GROUP):
        origin = lax.rem(x_me + 1, ring) * GROUP + lo
        arrived = pltpu.make_async_remote_copy(
            src_ref=relay_buf.at[lo],
            dst_ref=relay_buf.at[lo],
            send_sem=relay_send.at[lo],
            recv_sem=relay_recv.at[lo],
            device_id=device(target),
            device_id_type=pl.DeviceIdType.MESH,
        )
        arrived.wait_recv()
        forward = pltpu.make_async_remote_copy(
            src_ref=relay_buf.at[lo],
            dst_ref=dst_at(dst_ref, origin, high_half),
            send_sem=fwd_send.at[lo],
            recv_sem=fwd_recv.at[lo],
            device_id=device(target),
            device_id_type=pl.DeviceIdType.MESH,
        )
        forward.start()
        forwards.append(forward)
    for copy in copies + relays + forwards:
        copy.wait_send()
    for arrival in arrivals:
        arrival.wait_recv()
    for forward in forwards:
        forward.wait_recv()
    local.wait()


def exchange(block, out_shape, piece, src_at, dst_at, ident):
    count = lax.axis_size("lon")
    levels = block.shape[0]
    return pl.pallas_call(
        functools.partial(exchange_kernel, src_at=src_at, dst_at=dst_at),
        out_shape=jax.ShapeDtypeStruct(out_shape, block.dtype),
        in_specs=[pl.BlockSpec(memory_space=pl.ANY)],
        out_specs=pl.BlockSpec(memory_space=pl.ANY),
        scratch_shapes=[
            pltpu.VMEM((GROUP, levels // 2) + piece, block.dtype),
            pltpu.SemaphoreType.DMA((count,)),
            pltpu.SemaphoreType.DMA((count,)),
            pltpu.SemaphoreType.DMA,
            pltpu.SemaphoreType.DMA((GROUP,)),
            pltpu.SemaphoreType.DMA((GROUP,)),
            pltpu.SemaphoreType.DMA((GROUP,)),
            pltpu.SemaphoreType.DMA((GROUP,)),
        ],
        compiler_params=pltpu.CompilerParams(collective_id=ident, has_side_effects=True),
    )(block)


def to_columns(block):
    levels, rows, width = block.shape
    cells = width // NTR
    devices = lax.axis_size("lon")
    parts = devices // (NTR // PAIR)
    count = rows // parts
    lane = cells * PAIR
    moved = exact_permute(block, pair_order(cells), False)

    def src_at(ref, peer, part):
        return ref.at[part, pl.ds((peer % parts) * count, count), pl.ds((peer // parts) * lane, lane)]

    def dst_at(ref, sender, part):
        return ref.at[part, :, pl.ds(sender * lane, lane)]

    return exchange(moved, (levels, count, devices * lane), (count, lane), src_at, dst_at, 0)


def from_columns(field, rows):
    levels, count, width = field.shape
    devices = lax.axis_size("lon")
    parts = devices // (NTR // PAIR)
    lane = width // devices
    cells = lane // PAIR

    def src_at(ref, peer, part):
        return ref.at[part, :, pl.ds(peer * lane, lane)]

    def dst_at(ref, sender, part):
        return ref.at[part, pl.ds((sender % parts) * count, count), pl.ds((sender // parts) * lane, lane)]

    moved = exchange(field, (levels, rows, cells * NTR), (count, lane), src_at, dst_at, 1)
    return exact_permute(moved, pair_order(cells), True)


def lat_halo(field, width):
    lon_n = lax.axis_size("lon")
    lat_n = lax.axis_size("lat")
    parts = lon_n // (NTR // PAIR)
    up = []
    for b in range(lat_n):
        for l in range(lon_n):
            t, h = l // parts, l % parts
            g = b * parts + h
            if g + 1 < lat_n * parts:
                nb, nh = (g + 1) // parts, (g + 1) % parts
                up.append((l * lat_n + b, (t * parts + nh) * lat_n + nb))
    down = [(d, s) for s, d in up]
    rows = field.shape[1]
    below = lax.ppermute(field[:, rows - width :], ("lon", "lat"), up)
    above = lax.ppermute(field[:, :width], ("lon", "lat"), down)
    return jnp.concatenate([below, field, above], axis=1)


def roll_rows(field, amount):
    cells = field.shape[2] // PAIR
    current = field
    for position in range(cells.bit_length() - 1):
        moved = jnp.roll(current, PAIR * 2**position, axis=2)
        current = jnp.where(bit_mask(amount, position), moved, current)
    return current


def lon_cubic(shifted, fraction):
    weights = cubic_weights(fraction)
    taps = [jnp.roll(shifted, PAIR * (1 - p), axis=2) for p in range(4)]
    summed = None
    for p in range(4):
        addend = weights[p][:, :, None] * taps[p]
        summed = addend if summed is None else summed + addend
    return summed


def own_rows(values, count):
    parts = lax.axis_size("lon") // (NTR // PAIR)
    start = (lax.axis_index("lon") % parts) * count
    return lax.dynamic_slice_in_dim(values, start, count, axis=values.ndim - 1)


def per_device(tracers, lon_shift, lon_frac, lat_shift, lat_frac, remap_frac, diffusivity):
    rows = tracers.shape[1]
    field = to_columns(tracers)
    count = field.shape[1]
    width = field.shape[2]
    lon_shift, lon_frac, lat_shift, lat_frac, remap_frac, diffusivity = (
        own_rows(v, count) for v in (lon_shift, lon_frac, lat_shift, lat_frac, remap_frac, diffusivity)
    )
    for time_step in range(STEPS):
        padded = lat_halo(field, 3)
        field = lat_step(padded, lat_shift[time_step], lat_frac[time_step], count)
        amount = jnp.remainder(lon_shift[time_step], width // PAIR)
        field = lon_cubic(roll_rows(field, amount), lon_frac[time_step])
        field = remap(field, remap_frac[time_step])
        field = diffuse(field, diffusivity)
    return from_columns(field, rows)


def solution(mesh):
    in_specs = (
        P(None, "lat", "lon"),
        P(None, None, "lat"),
        P(None, None, "lat"),
        P(None, None, "lat"),
        P(None, None, "lat"),
        P(None, None, "lat"),
        P(None, "lat"),
    )
    out_specs = P(None, "lat", "lon")
    return jax.shard_map(
        per_device, mesh=mesh, in_specs=in_specs, out_specs=out_specs, check_vma=False
    )
```

```python
import functools

import jax
import jax.numpy as jnp
from jax import lax
from jax.experimental import pallas as pl
from jax.experimental.pallas import tpu as pltpu
from jax.sharding import PartitionSpec as P

NTR = 8
STEPS = 2


def from_behind(x, axis, by):
    peers = lax.axis_size(axis)
    return lax.ppermute(x, axis, [(i, (i + by) % peers) for i in range(peers)])


def with_halo(block, sides, width, periodic):
    for axis, dim in sides:
        count = lax.axis_size(axis)
        forward = [(i, i + 1) for i in range(count - 1)]
        if periodic:
            forward.append((count - 1, 0))
        backward = [(target, source) for source, target in forward]
        low = lax.ppermute(
            lax.slice_in_dim(block, block.shape[dim] - width, None, axis=dim), axis, forward
        )
        high = lax.ppermute(lax.slice_in_dim(block, 0, width, axis=dim), axis, backward)
        block = jnp.concatenate([low, block, high], axis=dim)
    return block


def cubic_weights(fraction):
    w_zero = -fraction * (fraction - 1.0) * (fraction - 2.0) / 6.0
    w_one = (fraction + 1.0) * (fraction - 1.0) * (fraction - 2.0) / 2.0
    w_two = -(fraction + 1.0) * fraction * (fraction - 2.0) / 2.0
    w_three = (fraction + 1.0) * fraction * (fraction - 1.0) / 6.0
    return (w_zero, w_one, w_two, w_three)


def lat_step(padded, offset, fraction, row_count):
    weights = cubic_weights(fraction)
    summed = None
    for place_index in range(6):
        row_delta = place_index - 2
        coeff = jnp.zeros_like(fraction)
        for tap_index in range(4):
            coeff = coeff + jnp.where(offset == tap_index - 1 - row_delta, weights[tap_index], 0.0)
        addend = coeff[:, :, None] * padded[:, 1 + place_index : 1 + place_index + row_count, :]
        summed = addend if summed is None else summed + addend
    return summed


def lon_step(wrapped, fraction, tracer_count):
    weights = cubic_weights(fraction)
    width_cols = wrapped.shape[2] - 4 * tracer_count
    summed = None
    for tap_index in range(4):
        offset_cols = (1 + tap_index) * tracer_count
        addend = (
            weights[tap_index][:, :, None] * wrapped[:, :, offset_cols : offset_cols + width_cols]
        )
        summed = addend if summed is None else summed + addend
    return summed


def remap(tracer_field, fraction):
    level_above = jnp.concatenate([tracer_field[1:], tracer_field[-1:]], axis=0)
    return (1.0 - fraction)[:, :, None] * tracer_field + fraction[:, :, None] * level_above


def diffuse(tracer_field, kappa):
    levels = tracer_field.shape[0]
    face_kappa = 0.5 * (kappa[:-1] + kappa[1:])
    zero_face = jnp.zeros_like(kappa[:1])
    face_below = jnp.concatenate([zero_face, face_kappa], axis=0)
    face_above = jnp.concatenate([face_kappa, zero_face], axis=0)
    ratio_prev = jnp.zeros_like(kappa[0])
    solved_prev = jnp.zeros_like(tracer_field[0])
    ratios = []
    solveds = []
    for level_index in range(levels):
        below = face_below[level_index]
        above = face_above[level_index]
        pivot_value = 1.0 + below + above + below * ratio_prev
        ratio_now = -above / pivot_value
        solved_now = (tracer_field[level_index] + below[:, None] * solved_prev) / pivot_value[
            :, None
        ]
        ratios.append(ratio_now)
        solveds.append(solved_now)
        ratio_prev = ratio_now
        solved_prev = solved_now
    results = [None] * levels
    results[levels - 1] = solveds[levels - 1]
    for level_index in range(levels - 2, -1, -1):
        results[level_index] = (
            solveds[level_index] - ratios[level_index][:, None] * results[level_index + 1]
        )
    return jnp.stack(results, axis=0)


def bit_mask(amount, position):
    return (amount // 2**position % 2 == 1)[:, :, None]


PAIR = 2


def pair_order(cells):
    cols = jnp.arange(cells * NTR)
    cell, tracer = cols // NTR, cols % NTR
    target = (tracer // PAIR) * cells * PAIR + cell * PAIR + tracer % PAIR
    return target


def permutation(target, inverse):
    cols = jnp.arange(target.shape[0])
    if inverse:
        matrix = cols[:, None] == target[None, :]
    else:
        matrix = cols[None, :] == target[:, None]
    return matrix.astype(jnp.bfloat16)


def permute_block(block, matrix):
    high = block.astype(jnp.bfloat16)
    rest = block - high.astype(jnp.float32)
    middle = rest.astype(jnp.bfloat16)
    low = (rest - middle.astype(jnp.float32)).astype(jnp.bfloat16)
    total = jnp.dot(high, matrix, preferred_element_type=jnp.float32)
    total = total + jnp.dot(middle, matrix, preferred_element_type=jnp.float32)
    return total + jnp.dot(low, matrix, preferred_element_type=jnp.float32)


CHUNKS = 2
MESH_ID = pl.DeviceIdType.MESH


def greet(count, me, lat):
    barrier = pltpu.get_barrier_semaphore()
    for offset in range(1, count):
        peer = lax.rem(me + offset, count)
        pl.semaphore_signal(barrier, 1, device_id=(peer, lat), device_id_type=MESH_ID)
    return barrier


def entry_kernel(x_ref, matrix_ref, dst_ref, moved, send_sem, recv_sem, local_sem, *, src_at, dst_at):
    count = lax.axis_size("lon")
    me = lax.axis_index("lon")
    lat = lax.axis_index("lat")
    levels = x_ref.shape[0]
    per = levels // CHUNKS
    barrier = greet(count, me, lat)
    copies = []
    locals_ = []
    for chunk in range(CHUNKS):
        def body(k, carry):
            moved[k] = permute_block(x_ref[k], matrix_ref[...])
            return carry

        lax.fori_loop(chunk * per, (chunk + 1) * per, body, 0)
        if chunk == 0:
            pl.semaphore_wait(barrier, count - 1)
        part = pl.ds(chunk * per, per)
        for offset in range(1, count):
            peer = lax.rem(me + offset, count)
            copy = pltpu.make_async_remote_copy(
                src_ref=src_at(moved, peer, part),
                dst_ref=dst_at(dst_ref, me, part),
                send_sem=send_sem.at[chunk, offset],
                recv_sem=recv_sem.at[chunk, offset],
                device_id=(peer, lat),
                device_id_type=MESH_ID,
            )
            copy.start()
            copies.append(copy)
        local = pltpu.make_async_copy(src_at(moved, me, part), dst_at(dst_ref, me, part), local_sem.at[chunk])
        local.start()
        locals_.append(local)
    for copy in copies:
        copy.wait_send()
    for copy in copies:
        copy.wait_recv()
    for local in locals_:
        local.wait()


def exit_kernel(src_ref, matrix_ref, out_ref, landed, send_sem, recv_sem, local_sem, *, src_at, dst_at):
    count = lax.axis_size("lon")
    me = lax.axis_index("lon")
    lat = lax.axis_index("lat")
    levels = out_ref.shape[0]
    per = levels // CHUNKS
    barrier = greet(count, me, lat)
    pl.semaphore_wait(barrier, count - 1)
    copies = []
    locals_ = []
    for chunk in range(CHUNKS):
        part = pl.ds(chunk * per, per)
        row = []
        for offset in range(1, count):
            peer = lax.rem(me + offset, count)
            copy = pltpu.make_async_remote_copy(
                src_ref=src_at(src_ref, peer, part),
                dst_ref=dst_at(landed, me, part),
                send_sem=send_sem.at[chunk, offset],
                recv_sem=recv_sem.at[chunk, offset],
                device_id=(peer, lat),
                device_id_type=MESH_ID,
            )
            copy.start()
            row.append(copy)
        copies.append(row)
        local = pltpu.make_async_copy(src_at(src_ref, me, part), dst_at(landed, me, part), local_sem.at[chunk])
        local.start()
        locals_.append(local)
    for chunk in range(CHUNKS):
        for copy in copies[chunk]:
            copy.wait_recv()
        locals_[chunk].wait()

        def body(k, carry):
            out_ref[k] = permute_block(landed[k], matrix_ref[...])
            return carry

        lax.fori_loop(chunk * per, (chunk + 1) * per, body, 0)
    for row in copies:
        for copy in row:
            copy.wait_send()


def run_exchange(kernel, operand, matrix, out_shape, src_spec, out_spec, scratch, src_at, dst_at, ident):
    count = lax.axis_size("lon")
    return pl.pallas_call(
        functools.partial(kernel, src_at=src_at, dst_at=dst_at),
        out_shape=jax.ShapeDtypeStruct(out_shape, operand.dtype),
        in_specs=[src_spec, pl.BlockSpec(memory_space=pltpu.VMEM)],
        out_specs=out_spec,
        scratch_shapes=[
            pltpu.VMEM(scratch, operand.dtype),
            pltpu.SemaphoreType.DMA((CHUNKS, count)),
            pltpu.SemaphoreType.DMA((CHUNKS, count)),
            pltpu.SemaphoreType.DMA((CHUNKS,)),
        ],
        compiler_params=pltpu.CompilerParams(collective_id=ident, has_side_effects=True),
    )(operand, matrix)


def to_columns(block):
    levels, rows, width = block.shape
    cells = width // NTR
    devices = lax.axis_size("lon")
    parts = devices // (NTR // PAIR)
    count = rows // parts
    lane = cells * PAIR

    def src_at(ref, peer, part):
        return ref.at[part, pl.ds((peer % parts) * count, count), pl.ds((peer // parts) * lane, lane)]

    def dst_at(ref, sender, part):
        return ref.at[part, :, pl.ds(sender * lane, lane)]

    return run_exchange(
        entry_kernel, block, permutation(pair_order(cells), False), (levels, count, devices * lane),
        pl.BlockSpec(memory_space=pltpu.VMEM), pl.BlockSpec(memory_space=pl.ANY), block.shape,
        src_at, dst_at, 0,
    )


def from_columns(field, rows):
    levels, count, width = field.shape
    devices = lax.axis_size("lon")
    parts = devices // (NTR // PAIR)
    lane = width // devices
    cells = lane // PAIR

    def src_at(ref, peer, part):
        return ref.at[part, :, pl.ds(peer * lane, lane)]

    def dst_at(ref, sender, part):
        return ref.at[part, pl.ds((sender % parts) * count, count), pl.ds((sender // parts) * lane, lane)]

    shape = (levels, rows, cells * NTR)
    return run_exchange(
        exit_kernel, field, permutation(pair_order(cells), True), shape,
        pl.BlockSpec(memory_space=pl.ANY), pl.BlockSpec(memory_space=pltpu.VMEM), shape,
        src_at, dst_at, 1,
    )


def lat_halo(field, width):
    lon_n = lax.axis_size("lon")
    lat_n = lax.axis_size("lat")
    parts = lon_n // (NTR // PAIR)
    up = []
    for b in range(lat_n):
        for l in range(lon_n):
            t, h = l // parts, l % parts
            g = b * parts + h
            if g + 1 < lat_n * parts:
                nb, nh = (g + 1) // parts, (g + 1) % parts
                up.append((l * lat_n + b, (t * parts + nh) * lat_n + nb))
    down = [(d, s) for s, d in up]
    rows = field.shape[1]
    below = lax.ppermute(field[:, rows - width :], ("lon", "lat"), up)
    above = lax.ppermute(field[:, :width], ("lon", "lat"), down)
    return jnp.concatenate([below, field, above], axis=1)


def roll_rows(field, amount):
    cells = field.shape[2] // PAIR
    current = field
    for position in range(cells.bit_length() - 1):
        moved = jnp.roll(current, PAIR * 2**position, axis=2)
        current = jnp.where(bit_mask(amount, position), moved, current)
    return current


def lon_cubic(shifted, fraction):
    weights = cubic_weights(fraction)
    taps = [jnp.roll(shifted, PAIR * (1 - p), axis=2) for p in range(4)]
    summed = None
    for p in range(4):
        addend = weights[p][:, :, None] * taps[p]
        summed = addend if summed is None else summed + addend
    return summed


def own_rows(values, count):
    parts = lax.axis_size("lon") // (NTR // PAIR)
    start = (lax.axis_index("lon") % parts) * count
    return lax.dynamic_slice_in_dim(values, start, count, axis=values.ndim - 1)


def per_device(tracers, lon_shift, lon_frac, lat_shift, lat_frac, remap_frac, diffusivity):
    rows = tracers.shape[1]
    field = to_columns(tracers)
    count = field.shape[1]
    width = field.shape[2]
    lon_shift, lon_frac, lat_shift, lat_frac, remap_frac, diffusivity = (
        own_rows(v, count) for v in (lon_shift, lon_frac, lat_shift, lat_frac, remap_frac, diffusivity)
    )
    for time_step in range(STEPS):
        padded = lat_halo(field, 3)
        field = lat_step(padded, lat_shift[time_step], lat_frac[time_step], count)
        amount = jnp.remainder(lon_shift[time_step], width // PAIR)
        field = lon_cubic(roll_rows(field, amount), lon_frac[time_step])
        field = remap(field, remap_frac[time_step])
        field = diffuse(field, diffusivity)
    return from_columns(field, rows)


def solution(mesh):
    in_specs = (
        P(None, "lat", "lon"),
        P(None, None, "lat"),
        P(None, None, "lat"),
        P(None, None, "lat"),
        P(None, None, "lat"),
        P(None, None, "lat"),
        P(None, "lat"),
    )
    out_specs = P(None, "lat", "lon")
    return jax.shard_map(
        per_device, mesh=mesh, in_specs=in_specs, out_specs=out_specs, check_vma=False
    )
```

```python
import functools

import jax
import jax.numpy as jnp
from jax import lax
from jax.experimental import pallas as pl
from jax.experimental.pallas import tpu as pltpu
from jax.sharding import PartitionSpec as P

NTR = 8
STEPS = 2


def from_behind(x, axis, by):
    peers = lax.axis_size(axis)
    return lax.ppermute(x, axis, [(i, (i + by) % peers) for i in range(peers)])


def with_halo(block, sides, width, periodic):
    for axis, dim in sides:
        count = lax.axis_size(axis)
        forward = [(i, i + 1) for i in range(count - 1)]
        if periodic:
            forward.append((count - 1, 0))
        backward = [(target, source) for source, target in forward]
        low = lax.ppermute(
            lax.slice_in_dim(block, block.shape[dim] - width, None, axis=dim), axis, forward
        )
        high = lax.ppermute(lax.slice_in_dim(block, 0, width, axis=dim), axis, backward)
        block = jnp.concatenate([low, block, high], axis=dim)
    return block


def cubic_weights(fraction):
    w_zero = -fraction * (fraction - 1.0) * (fraction - 2.0) / 6.0
    w_one = (fraction + 1.0) * (fraction - 1.0) * (fraction - 2.0) / 2.0
    w_two = -(fraction + 1.0) * fraction * (fraction - 2.0) / 2.0
    w_three = (fraction + 1.0) * fraction * (fraction - 1.0) / 6.0
    return (w_zero, w_one, w_two, w_three)


def lat_step(padded, offset, fraction, row_count):
    weights = cubic_weights(fraction)
    summed = None
    for place_index in range(6):
        row_delta = place_index - 2
        coeff = jnp.zeros_like(fraction)
        for tap_index in range(4):
            coeff = coeff + jnp.where(offset == tap_index - 1 - row_delta, weights[tap_index], 0.0)
        addend = coeff[:, :, None] * padded[:, 1 + place_index : 1 + place_index + row_count, :]
        summed = addend if summed is None else summed + addend
    return summed


def lon_step(wrapped, fraction, tracer_count):
    weights = cubic_weights(fraction)
    width_cols = wrapped.shape[2] - 4 * tracer_count
    summed = None
    for tap_index in range(4):
        offset_cols = (1 + tap_index) * tracer_count
        addend = (
            weights[tap_index][:, :, None] * wrapped[:, :, offset_cols : offset_cols + width_cols]
        )
        summed = addend if summed is None else summed + addend
    return summed


def remap(tracer_field, fraction):
    level_above = jnp.concatenate([tracer_field[1:], tracer_field[-1:]], axis=0)
    return (1.0 - fraction)[:, :, None] * tracer_field + fraction[:, :, None] * level_above


def diffuse(tracer_field, kappa):
    levels = tracer_field.shape[0]
    face_kappa = 0.5 * (kappa[:-1] + kappa[1:])
    zero_face = jnp.zeros_like(kappa[:1])
    face_below = jnp.concatenate([zero_face, face_kappa], axis=0)
    face_above = jnp.concatenate([face_kappa, zero_face], axis=0)
    ratio_prev = jnp.zeros_like(kappa[0])
    solved_prev = jnp.zeros_like(tracer_field[0])
    ratios = []
    solveds = []
    for level_index in range(levels):
        below = face_below[level_index]
        above = face_above[level_index]
        pivot_value = 1.0 + below + above + below * ratio_prev
        ratio_now = -above / pivot_value
        solved_now = (tracer_field[level_index] + below[:, None] * solved_prev) / pivot_value[
            :, None
        ]
        ratios.append(ratio_now)
        solveds.append(solved_now)
        ratio_prev = ratio_now
        solved_prev = solved_now
    results = [None] * levels
    results[levels - 1] = solveds[levels - 1]
    for level_index in range(levels - 2, -1, -1):
        results[level_index] = (
            solveds[level_index] - ratios[level_index][:, None] * results[level_index + 1]
        )
    return jnp.stack(results, axis=0)


def bit_mask(amount, position):
    return (amount // 2**position % 2 == 1)[:, :, None]


PAIR = 2


def pair_order(cells):
    cols = jnp.arange(cells * NTR)
    cell, tracer = cols // NTR, cols % NTR
    target = (tracer // PAIR) * cells * PAIR + cell * PAIR + tracer % PAIR
    return target


def permutation(target, inverse):
    cols = jnp.arange(target.shape[0])
    if inverse:
        matrix = cols[:, None] == target[None, :]
    else:
        matrix = cols[None, :] == target[:, None]
    return matrix.astype(jnp.bfloat16)


def permute_block(block, matrix):
    high = block.astype(jnp.bfloat16)
    rest = block - high.astype(jnp.float32)
    middle = rest.astype(jnp.bfloat16)
    low = (rest - middle.astype(jnp.float32)).astype(jnp.bfloat16)
    total = jnp.dot(high, matrix, preferred_element_type=jnp.float32)
    total = total + jnp.dot(middle, matrix, preferred_element_type=jnp.float32)
    return total + jnp.dot(low, matrix, preferred_element_type=jnp.float32)


CHUNKS = 2
MESH_ID = pl.DeviceIdType.MESH


def greet(count, me, lat):
    barrier = pltpu.get_barrier_semaphore()
    for offset in range(1, count):
        peer = lax.rem(me + offset, count)
        pl.semaphore_signal(barrier, 1, device_id=(peer, lat), device_id_type=MESH_ID)
    return barrier


def entry_kernel(x_ref, matrix_ref, dst_ref, moved, send_sem, recv_sem, local_sem, *, src_at, dst_at):
    count = lax.axis_size("lon")
    me = lax.axis_index("lon")
    lat = lax.axis_index("lat")
    levels = x_ref.shape[0]
    per = levels // CHUNKS
    barrier = greet(count, me, lat)
    copies = []
    locals_ = []
    for chunk in range(CHUNKS):
        def body(k, carry):
            moved[k] = permute_block(x_ref[k], matrix_ref[...])
            return carry

        lax.fori_loop(chunk * per, (chunk + 1) * per, body, 0)
        if chunk == 0:
            pl.semaphore_wait(barrier, count - 1)
        part = pl.ds(chunk * per, per)
        for offset in range(1, count):
            peer = lax.rem(me + offset, count)
            copy = pltpu.make_async_remote_copy(
                src_ref=src_at(moved, peer, part),
                dst_ref=dst_at(dst_ref, me, part),
                send_sem=send_sem.at[chunk, offset],
                recv_sem=recv_sem.at[chunk, offset],
                device_id=(peer, lat),
                device_id_type=MESH_ID,
            )
            copy.start()
            copies.append(copy)
        local = pltpu.make_async_copy(src_at(moved, me, part), dst_at(dst_ref, me, part), local_sem.at[chunk])
        local.start()
        locals_.append(local)
    for copy in copies:
        copy.wait_send()
    for copy in copies:
        copy.wait_recv()
    for local in locals_:
        local.wait()


def exit_kernel(src_ref, matrix_ref, out_ref, landed, send_sem, recv_sem, local_sem, *, src_at, dst_at):
    count = lax.axis_size("lon")
    me = lax.axis_index("lon")
    lat = lax.axis_index("lat")
    levels = out_ref.shape[0]
    per = levels // CHUNKS
    barrier = greet(count, me, lat)
    pl.semaphore_wait(barrier, count - 1)
    copies = []
    locals_ = []
    for chunk in range(CHUNKS):
        part = pl.ds(chunk * per, per)
        row = []
        for offset in range(1, count):
            peer = lax.rem(me + offset, count)
            copy = pltpu.make_async_remote_copy(
                src_ref=src_at(src_ref, peer, part),
                dst_ref=dst_at(landed, me, part),
                send_sem=send_sem.at[chunk, offset],
                recv_sem=recv_sem.at[chunk, offset],
                device_id=(peer, lat),
                device_id_type=MESH_ID,
            )
            copy.start()
            row.append(copy)
        copies.append(row)
        local = pltpu.make_async_copy(src_at(src_ref, me, part), dst_at(landed, me, part), local_sem.at[chunk])
        local.start()
        locals_.append(local)
    for chunk in range(CHUNKS):
        for copy in copies[chunk]:
            copy.wait_recv()
        locals_[chunk].wait()

        def body(k, carry):
            out_ref[k] = permute_block(landed[k], matrix_ref[...])
            return carry

        lax.fori_loop(chunk * per, (chunk + 1) * per, body, 0)
    for row in copies:
        for copy in row:
            copy.wait_send()


def run_exchange(kernel, operand, matrix, out_shape, src_spec, out_spec, scratch, src_at, dst_at, ident):
    count = lax.axis_size("lon")
    return pl.pallas_call(
        functools.partial(kernel, src_at=src_at, dst_at=dst_at),
        out_shape=jax.ShapeDtypeStruct(out_shape, operand.dtype),
        in_specs=[src_spec, pl.BlockSpec(memory_space=pltpu.VMEM)],
        out_specs=out_spec,
        scratch_shapes=[
            pltpu.VMEM(scratch, operand.dtype),
            pltpu.SemaphoreType.DMA((CHUNKS, count)),
            pltpu.SemaphoreType.DMA((CHUNKS, count)),
            pltpu.SemaphoreType.DMA((CHUNKS,)),
        ],
        compiler_params=pltpu.CompilerParams(collective_id=ident, has_side_effects=True),
    )(operand, matrix)


def to_columns(block):
    levels, rows, width = block.shape
    cells = width // NTR
    devices = lax.axis_size("lon")
    parts = devices // (NTR // PAIR)
    count = rows // parts
    lane = cells * PAIR

    def src_at(ref, peer, part):
        return ref.at[part, pl.ds((peer % parts) * count, count), pl.ds((peer // parts) * lane, lane)]

    def dst_at(ref, sender, part):
        return ref.at[part, :, pl.ds(sender * lane, lane)]

    return run_exchange(
        entry_kernel, block, permutation(pair_order(cells), False), (levels, count, devices * lane),
        pl.BlockSpec(memory_space=pltpu.VMEM), pl.BlockSpec(memory_space=pl.ANY), block.shape,
        src_at, dst_at, 0,
    )


def from_columns(field, rows):
    levels, count, width = field.shape
    devices = lax.axis_size("lon")
    parts = devices // (NTR // PAIR)
    lane = width // devices
    cells = lane // PAIR

    def src_at(ref, peer, part):
        return ref.at[part, :, pl.ds(peer * lane, lane)]

    def dst_at(ref, sender, part):
        return ref.at[part, pl.ds((sender % parts) * count, count), pl.ds((sender // parts) * lane, lane)]

    shape = (levels, rows, cells * NTR)
    return run_exchange(
        exit_kernel, field, permutation(pair_order(cells), True), shape,
        pl.BlockSpec(memory_space=pl.ANY), pl.BlockSpec(memory_space=pltpu.VMEM), shape,
        src_at, dst_at, 1,
    )


def halo_kernel(top_ref, bottom_ref, below_ref, above_ref, send_sem, recv_sem, *, parts):
    lon = lax.axis_index("lon")
    lat = lax.axis_index("lat")
    bands = lax.axis_size("lat")
    quarter = lon % parts
    has_up = jnp.logical_or(quarter < parts - 1, lat < bands - 1)
    has_down = jnp.logical_or(quarter > 0, lat > 0)
    up = (jnp.where(quarter < parts - 1, lon + 1, lon + 1 - parts), jnp.where(quarter < parts - 1, lat, lat + 1))
    down = (jnp.where(quarter > 0, lon - 1, lon + parts - 1), jnp.where(quarter > 0, lat, lat - 1))
    barrier = pltpu.get_barrier_semaphore()

    @pl.when(has_up)
    def _():
        pl.semaphore_signal(barrier, 1, device_id=up, device_id_type=MESH_ID)

    @pl.when(has_down)
    def _():
        pl.semaphore_signal(barrier, 1, device_id=down, device_id_type=MESH_ID)

    pl.semaphore_wait(barrier, has_up.astype(jnp.int32) + has_down.astype(jnp.int32))
    to_up = pltpu.make_async_remote_copy(
        src_ref=top_ref, dst_ref=below_ref, send_sem=send_sem.at[0], recv_sem=recv_sem.at[0],
        device_id=up, device_id_type=MESH_ID,
    )
    to_down = pltpu.make_async_remote_copy(
        src_ref=bottom_ref, dst_ref=above_ref, send_sem=send_sem.at[1], recv_sem=recv_sem.at[1],
        device_id=down, device_id_type=MESH_ID,
    )

    @pl.when(has_up)
    def _():
        to_up.start()

    @pl.when(has_down)
    def _():
        to_down.start()

    @pl.when(jnp.logical_not(has_down))
    def _():
        below_ref[...] = jnp.zeros(below_ref.shape, below_ref.dtype)

    @pl.when(jnp.logical_not(has_up))
    def _():
        above_ref[...] = jnp.zeros(above_ref.shape, above_ref.dtype)

    @pl.when(has_up)
    def _():
        to_up.wait_send()
        to_down.wait_recv()

    @pl.when(has_down)
    def _():
        to_down.wait_send()
        to_up.wait_recv()


def lat_halo(field, ident):
    parts = lax.axis_size("lon") // (NTR // PAIR)
    rows = field.shape[1]
    top = field[:, rows - 2 :]
    bottom = field[:, :3]
    vmem = pl.BlockSpec(memory_space=pltpu.VMEM)
    below, above = pl.pallas_call(
        functools.partial(halo_kernel, parts=parts),
        out_shape=(jax.ShapeDtypeStruct(top.shape, field.dtype), jax.ShapeDtypeStruct(bottom.shape, field.dtype)),
        in_specs=[vmem, vmem],
        out_specs=(vmem, vmem),
        scratch_shapes=[pltpu.SemaphoreType.DMA((2,)), pltpu.SemaphoreType.DMA((2,))],
        compiler_params=pltpu.CompilerParams(collective_id=ident, has_side_effects=True),
    )(top, bottom)
    return jnp.concatenate([below[:, :1], below, field, above], axis=1)


def roll_rows(field, amount):
    cells = field.shape[2] // PAIR
    current = field
    for position in range(cells.bit_length() - 1):
        moved = jnp.roll(current, PAIR * 2**position, axis=2)
        current = jnp.where(bit_mask(amount, position), moved, current)
    return current


def lon_cubic(shifted, fraction):
    weights = cubic_weights(fraction)
    taps = [jnp.roll(shifted, PAIR * (1 - p), axis=2) for p in range(4)]
    summed = None
    for p in range(4):
        addend = weights[p][:, :, None] * taps[p]
        summed = addend if summed is None else summed + addend
    return summed


def own_rows(values, count):
    parts = lax.axis_size("lon") // (NTR // PAIR)
    start = (lax.axis_index("lon") % parts) * count
    return lax.dynamic_slice_in_dim(values, start, count, axis=values.ndim - 1)


def per_device(tracers, lon_shift, lon_frac, lat_shift, lat_frac, remap_frac, diffusivity):
    rows = tracers.shape[1]
    field = to_columns(tracers)
    count = field.shape[1]
    width = field.shape[2]
    lon_shift, lon_frac, lat_shift, lat_frac, remap_frac, diffusivity = (
        own_rows(v, count) for v in (lon_shift, lon_frac, lat_shift, lat_frac, remap_frac, diffusivity)
    )
    for time_step in range(STEPS):
        padded = lat_halo(field, 2 + time_step)
        field = lat_step(padded, lat_shift[time_step], lat_frac[time_step], count)
        amount = jnp.remainder(lon_shift[time_step], width // PAIR)
        field = lon_cubic(roll_rows(field, amount), lon_frac[time_step])
        field = remap(field, remap_frac[time_step])
        field = diffuse(field, diffusivity)
    return from_columns(field, rows)


def solution(mesh):
    in_specs = (
        P(None, "lat", "lon"),
        P(None, None, "lat"),
        P(None, None, "lat"),
        P(None, None, "lat"),
        P(None, None, "lat"),
        P(None, None, "lat"),
        P(None, "lat"),
    )
    out_specs = P(None, "lat", "lon")
    return jax.shard_map(
        per_device, mesh=mesh, in_specs=in_specs, out_specs=out_specs, check_vma=False
    )
```

```python
import functools

import jax
import jax.numpy as jnp
from jax import lax
from jax.experimental import pallas as pl
from jax.experimental.pallas import tpu as pltpu
from jax.sharding import PartitionSpec as P

NTR = 8
STEPS = 2


def from_behind(x, axis, by):
    peers = lax.axis_size(axis)
    return lax.ppermute(x, axis, [(i, (i + by) % peers) for i in range(peers)])


def with_halo(block, sides, width, periodic):
    for axis, dim in sides:
        count = lax.axis_size(axis)
        forward = [(i, i + 1) for i in range(count - 1)]
        if periodic:
            forward.append((count - 1, 0))
        backward = [(target, source) for source, target in forward]
        low = lax.ppermute(
            lax.slice_in_dim(block, block.shape[dim] - width, None, axis=dim), axis, forward
        )
        high = lax.ppermute(lax.slice_in_dim(block, 0, width, axis=dim), axis, backward)
        block = jnp.concatenate([low, block, high], axis=dim)
    return block


def cubic_weights(fraction):
    w_zero = -fraction * (fraction - 1.0) * (fraction - 2.0) / 6.0
    w_one = (fraction + 1.0) * (fraction - 1.0) * (fraction - 2.0) / 2.0
    w_two = -(fraction + 1.0) * fraction * (fraction - 2.0) / 2.0
    w_three = (fraction + 1.0) * fraction * (fraction - 1.0) / 6.0
    return (w_zero, w_one, w_two, w_three)


def lat_step(padded, offset, fraction, row_count):
    weights = cubic_weights(fraction)
    summed = None
    for place_index in range(6):
        row_delta = place_index - 2
        coeff = jnp.zeros_like(fraction)
        for tap_index in range(4):
            coeff = coeff + jnp.where(offset == tap_index - 1 - row_delta, weights[tap_index], 0.0)
        addend = coeff[:, :, None] * padded[:, 1 + place_index : 1 + place_index + row_count, :]
        summed = addend if summed is None else summed + addend
    return summed


def lon_step(wrapped, fraction, tracer_count):
    weights = cubic_weights(fraction)
    width_cols = wrapped.shape[2] - 4 * tracer_count
    summed = None
    for tap_index in range(4):
        offset_cols = (1 + tap_index) * tracer_count
        addend = (
            weights[tap_index][:, :, None] * wrapped[:, :, offset_cols : offset_cols + width_cols]
        )
        summed = addend if summed is None else summed + addend
    return summed


def remap(tracer_field, fraction):
    level_above = jnp.concatenate([tracer_field[1:], tracer_field[-1:]], axis=0)
    return (1.0 - fraction)[:, :, None] * tracer_field + fraction[:, :, None] * level_above


def diffuse(tracer_field, kappa):
    levels = tracer_field.shape[0]
    face_kappa = 0.5 * (kappa[:-1] + kappa[1:])
    zero_face = jnp.zeros_like(kappa[:1])
    face_below = jnp.concatenate([zero_face, face_kappa], axis=0)
    face_above = jnp.concatenate([face_kappa, zero_face], axis=0)
    ratio_prev = jnp.zeros_like(kappa[0])
    solved_prev = jnp.zeros_like(tracer_field[0])
    ratios = []
    solveds = []
    for level_index in range(levels):
        below = face_below[level_index]
        above = face_above[level_index]
        pivot_value = 1.0 + below + above + below * ratio_prev
        ratio_now = -above / pivot_value
        solved_now = (tracer_field[level_index] + below[:, None] * solved_prev) / pivot_value[
            :, None
        ]
        ratios.append(ratio_now)
        solveds.append(solved_now)
        ratio_prev = ratio_now
        solved_prev = solved_now
    results = [None] * levels
    results[levels - 1] = solveds[levels - 1]
    for level_index in range(levels - 2, -1, -1):
        results[level_index] = (
            solveds[level_index] - ratios[level_index][:, None] * results[level_index + 1]
        )
    return jnp.stack(results, axis=0)


def bit_mask(amount, position):
    return (amount // 2**position % 2 == 1)[:, :, None]


PAIR = 2


def pair_order(cells):
    cols = jnp.arange(cells * NTR)
    cell, tracer = cols // NTR, cols % NTR
    target = (tracer // PAIR) * cells * PAIR + cell * PAIR + tracer % PAIR
    return target


def permutation(target, inverse):
    cols = jnp.arange(target.shape[0])
    if inverse:
        matrix = cols[:, None] == target[None, :]
    else:
        matrix = cols[None, :] == target[:, None]
    return matrix.astype(jnp.bfloat16)


def permute_block(block, matrix):
    high = block.astype(jnp.bfloat16)
    rest = block - high.astype(jnp.float32)
    middle = rest.astype(jnp.bfloat16)
    low = (rest - middle.astype(jnp.float32)).astype(jnp.bfloat16)
    total = jnp.dot(high, matrix, preferred_element_type=jnp.float32)
    total = total + jnp.dot(middle, matrix, preferred_element_type=jnp.float32)
    return total + jnp.dot(low, matrix, preferred_element_type=jnp.float32)


CHUNKS = 2
MESH_ID = pl.DeviceIdType.MESH


def greet(count, me, lat):
    barrier = pltpu.get_barrier_semaphore()
    for offset in range(1, count):
        peer = lax.rem(me + offset, count)
        pl.semaphore_signal(barrier, 1, device_id=(peer, lat), device_id_type=MESH_ID)
    return barrier


def entry_kernel(x_ref, matrix_ref, dst_ref, moved, send_sem, recv_sem, local_sem, *, src_at, dst_at):
    count = lax.axis_size("lon")
    me = lax.axis_index("lon")
    lat = lax.axis_index("lat")
    levels = x_ref.shape[0]
    per = levels // CHUNKS
    barrier = greet(count, me, lat)
    copies = []
    locals_ = []
    for chunk in range(CHUNKS):
        def body(k, carry):
            moved[k] = permute_block(x_ref[k], matrix_ref[...])
            return carry

        lax.fori_loop(chunk * per, (chunk + 1) * per, body, 0)
        if chunk == 0:
            pl.semaphore_wait(barrier, count - 1)
        part = pl.ds(chunk * per, per)
        for offset in range(1, count):
            peer = lax.rem(me + offset, count)
            copy = pltpu.make_async_remote_copy(
                src_ref=src_at(moved, peer, part),
                dst_ref=dst_at(dst_ref, me, part),
                send_sem=send_sem.at[chunk, offset],
                recv_sem=recv_sem.at[chunk, offset],
                device_id=(peer, lat),
                device_id_type=MESH_ID,
            )
            copy.start()
            copies.append(copy)
        local = pltpu.make_async_copy(src_at(moved, me, part), dst_at(dst_ref, me, part), local_sem.at[chunk])
        local.start()
        locals_.append(local)
    for copy in copies:
        copy.wait_send()
    for copy in copies:
        copy.wait_recv()
    for local in locals_:
        local.wait()


def exit_kernel(src_ref, matrix_ref, out_ref, landed, send_sem, recv_sem, local_sem, *, src_at, dst_at):
    count = lax.axis_size("lon")
    me = lax.axis_index("lon")
    lat = lax.axis_index("lat")
    levels = out_ref.shape[0]
    per = levels // CHUNKS
    barrier = greet(count, me, lat)
    pl.semaphore_wait(barrier, count - 1)
    copies = []
    locals_ = []
    for chunk in range(CHUNKS):
        part = pl.ds(chunk * per, per)
        row = []
        for offset in range(1, count):
            peer = lax.rem(me + offset, count)
            copy = pltpu.make_async_remote_copy(
                src_ref=src_at(src_ref, peer, part),
                dst_ref=dst_at(landed, me, part),
                send_sem=send_sem.at[chunk, offset],
                recv_sem=recv_sem.at[chunk, offset],
                device_id=(peer, lat),
                device_id_type=MESH_ID,
            )
            copy.start()
            row.append(copy)
        copies.append(row)
        local = pltpu.make_async_copy(src_at(src_ref, me, part), dst_at(landed, me, part), local_sem.at[chunk])
        local.start()
        locals_.append(local)
    for chunk in range(CHUNKS):
        for copy in copies[chunk]:
            copy.wait_recv()
        locals_[chunk].wait()

        def body(k, carry):
            out_ref[k] = permute_block(landed[k], matrix_ref[...])
            return carry

        lax.fori_loop(chunk * per, (chunk + 1) * per, body, 0)
    for row in copies:
        for copy in row:
            copy.wait_send()


def run_exchange(kernel, operand, matrix, out_shape, src_spec, out_spec, scratch, src_at, dst_at, ident):
    count = lax.axis_size("lon")
    return pl.pallas_call(
        functools.partial(kernel, src_at=src_at, dst_at=dst_at),
        out_shape=jax.ShapeDtypeStruct(out_shape, operand.dtype),
        in_specs=[src_spec, pl.BlockSpec(memory_space=pltpu.VMEM)],
        out_specs=out_spec,
        scratch_shapes=[
            pltpu.VMEM(scratch, operand.dtype),
            pltpu.SemaphoreType.DMA((CHUNKS, count)),
            pltpu.SemaphoreType.DMA((CHUNKS, count)),
            pltpu.SemaphoreType.DMA((CHUNKS,)),
        ],
        compiler_params=pltpu.CompilerParams(collective_id=ident, has_side_effects=True),
    )(operand, matrix)


def to_columns(block):
    levels, rows, width = block.shape
    cells = width // NTR
    devices = lax.axis_size("lon")
    parts = devices // (NTR // PAIR)
    count = rows // parts
    lane = cells * PAIR

    def src_at(ref, peer, part):
        return ref.at[part, pl.ds((peer % parts) * count, count), pl.ds((peer // parts) * lane, lane)]

    def dst_at(ref, sender, part):
        return ref.at[part, :, pl.ds(sender * lane, lane)]

    return run_exchange(
        entry_kernel, block, permutation(pair_order(cells), False), (levels, count, devices * lane),
        pl.BlockSpec(memory_space=pltpu.VMEM), pl.BlockSpec(memory_space=pl.ANY), block.shape,
        src_at, dst_at, 0,
    )


def from_columns(field, rows):
    levels, count, width = field.shape
    devices = lax.axis_size("lon")
    parts = devices // (NTR // PAIR)
    lane = width // devices
    cells = lane // PAIR

    def src_at(ref, peer, part):
        return ref.at[part, :, pl.ds(peer * lane, lane)]

    def dst_at(ref, sender, part):
        return ref.at[part, pl.ds((sender % parts) * count, count), pl.ds((sender // parts) * lane, lane)]

    shape = (levels, rows, cells * NTR)
    return run_exchange(
        exit_kernel, field, permutation(pair_order(cells), True), shape,
        pl.BlockSpec(memory_space=pl.ANY), pl.BlockSpec(memory_space=pltpu.VMEM), shape,
        src_at, dst_at, 1,
    )


def lat_halo(field, width):
    lon_n = lax.axis_size("lon")
    lat_n = lax.axis_size("lat")
    parts = lon_n // (NTR // PAIR)
    up = []
    for b in range(lat_n):
        for l in range(lon_n):
            t, h = l // parts, l % parts
            g = b * parts + h
            if g + 1 < lat_n * parts:
                nb, nh = (g + 1) // parts, (g + 1) % parts
                up.append((l * lat_n + b, (t * parts + nh) * lat_n + nb))
    down = [(d, s) for s, d in up]
    rows = field.shape[1]
    below = lax.ppermute(field[:, rows - width + 1 :], ("lon", "lat"), up)
    above = lax.ppermute(field[:, :width], ("lon", "lat"), down)
    return below, above


def roll_rows(field, amount):
    cells = field.shape[2] // PAIR
    current = field
    for position in range(cells.bit_length() - 1):
        moved = jnp.roll(current, PAIR * 2**position, axis=2)
        current = jnp.where(bit_mask(amount, position), moved, current)
    return current


def lon_cubic(shifted, fraction):
    weights = cubic_weights(fraction)
    taps = [jnp.roll(shifted, PAIR * (1 - p), axis=2) for p in range(4)]
    summed = None
    for p in range(4):
        addend = weights[p][:, :, None] * taps[p]
        summed = addend if summed is None else summed + addend
    return summed


def own_rows(values, count):
    parts = lax.axis_size("lon") // (NTR // PAIR)
    start = (lax.axis_index("lon") % parts) * count
    return lax.dynamic_slice_in_dim(values, start, count, axis=values.ndim - 1)


def lat_part(source, offset, fraction):
    count = fraction.shape[1]
    weights = cubic_weights(fraction)
    summed = None
    for place_index in range(6):
        row_delta = place_index - 2
        coeff = jnp.zeros_like(fraction)
        for tap_index in range(4):
            coeff = coeff + jnp.where(offset == tap_index - 1 - row_delta, weights[tap_index], 0.0)
        addend = coeff[:, :, None] * source[:, place_index : place_index + count, :]
        summed = addend if summed is None else summed + addend
    return summed


def transport(field, params):
    lon_shift, lon_frac, remap_frac, diffusivity = params
    cells = field.shape[2] // PAIR
    amount = jnp.remainder(lon_shift, cells)
    field = lon_cubic(roll_rows(field, amount), lon_frac)
    field = remap(field, remap_frac)
    return diffuse(field, diffusivity)


def per_device(tracers, lon_shift, lon_frac, lat_shift, lat_frac, remap_frac, diffusivity):
    rows = tracers.shape[1]
    field = to_columns(tracers)
    count = field.shape[1]
    lon_shift, lon_frac, lat_shift, lat_frac, remap_frac, diffusivity = (
        own_rows(v, count) for v in (lon_shift, lon_frac, lat_shift, lat_frac, remap_frac, diffusivity)
    )
    low, high = 2, count - 3

    def rows_of(values, pick):
        return jnp.concatenate([values[..., a:b] for a, b in pick], axis=-1)

    inner = ((low, high),)
    edges = ((0, low), (high, count))
    for time_step in range(STEPS):
        below, above = lat_halo(field, 3)
        step_params = (lon_shift[time_step], lon_frac[time_step], remap_frac[time_step], diffusivity)
        middle = lat_part(field, lat_shift[time_step][:, low:high], lat_frac[time_step][:, low:high])
        middle = transport(middle, [rows_of(v, inner) for v in step_params])
        lower = lat_part(
            jnp.concatenate([below, field[:, : low + 3]], axis=1),
            lat_shift[time_step][:, :low], lat_frac[time_step][:, :low],
        )
        upper = lat_part(
            jnp.concatenate([field[:, high - 2 :], above], axis=1),
            lat_shift[time_step][:, high:], lat_frac[time_step][:, high:],
        )
        rim = transport(jnp.concatenate([lower, upper], axis=1), [rows_of(v, edges) for v in step_params])
        field = jnp.concatenate([rim[:, :low], middle, rim[:, low:]], axis=1)
    return from_columns(field, rows)


def solution(mesh):
    in_specs = (
        P(None, "lat", "lon"),
        P(None, None, "lat"),
        P(None, None, "lat"),
        P(None, None, "lat"),
        P(None, None, "lat"),
        P(None, None, "lat"),
        P(None, "lat"),
    )
    out_specs = P(None, "lat", "lon")
    return jax.shard_map(
        per_device, mesh=mesh, in_specs=in_specs, out_specs=out_specs, check_vma=False
    )
```

```python
import functools

import jax
import jax.numpy as jnp
from jax import lax
from jax.experimental import pallas as pl
from jax.experimental.pallas import tpu as pltpu
from jax.sharding import PartitionSpec as P

NTR = 8
STEPS = 2


def from_behind(x, axis, by):
    peers = lax.axis_size(axis)
    return lax.ppermute(x, axis, [(i, (i + by) % peers) for i in range(peers)])


def with_halo(block, sides, width, periodic):
    for axis, dim in sides:
        count = lax.axis_size(axis)
        forward = [(i, i + 1) for i in range(count - 1)]
        if periodic:
            forward.append((count - 1, 0))
        backward = [(target, source) for source, target in forward]
        low = lax.ppermute(
            lax.slice_in_dim(block, block.shape[dim] - width, None, axis=dim), axis, forward
        )
        high = lax.ppermute(lax.slice_in_dim(block, 0, width, axis=dim), axis, backward)
        block = jnp.concatenate([low, block, high], axis=dim)
    return block


def cubic_weights(fraction):
    w_zero = -fraction * (fraction - 1.0) * (fraction - 2.0) / 6.0
    w_one = (fraction + 1.0) * (fraction - 1.0) * (fraction - 2.0) / 2.0
    w_two = -(fraction + 1.0) * fraction * (fraction - 2.0) / 2.0
    w_three = (fraction + 1.0) * fraction * (fraction - 1.0) / 6.0
    return (w_zero, w_one, w_two, w_three)


def lat_step(padded, offset, fraction, row_count):
    weights = cubic_weights(fraction)
    summed = None
    for place_index in range(6):
        row_delta = place_index - 2
        coeff = jnp.zeros_like(fraction)
        for tap_index in range(4):
            coeff = coeff + jnp.where(offset == tap_index - 1 - row_delta, weights[tap_index], 0.0)
        addend = coeff[:, :, None] * padded[:, 1 + place_index : 1 + place_index + row_count, :]
        summed = addend if summed is None else summed + addend
    return summed


def lon_step(wrapped, fraction, tracer_count):
    weights = cubic_weights(fraction)
    width_cols = wrapped.shape[2] - 4 * tracer_count
    summed = None
    for tap_index in range(4):
        offset_cols = (1 + tap_index) * tracer_count
        addend = (
            weights[tap_index][:, :, None] * wrapped[:, :, offset_cols : offset_cols + width_cols]
        )
        summed = addend if summed is None else summed + addend
    return summed


def remap(tracer_field, fraction):
    level_above = jnp.concatenate([tracer_field[1:], tracer_field[-1:]], axis=0)
    return (1.0 - fraction)[:, :, None] * tracer_field + fraction[:, :, None] * level_above


def diffuse(tracer_field, kappa):
    levels = tracer_field.shape[0]
    face_kappa = 0.5 * (kappa[:-1] + kappa[1:])
    zero_face = jnp.zeros_like(kappa[:1])
    face_below = jnp.concatenate([zero_face, face_kappa], axis=0)
    face_above = jnp.concatenate([face_kappa, zero_face], axis=0)
    ratio_prev = jnp.zeros_like(kappa[0])
    solved_prev = jnp.zeros_like(tracer_field[0])
    ratios = []
    solveds = []
    for level_index in range(levels):
        below = face_below[level_index]
        above = face_above[level_index]
        pivot_value = 1.0 + below + above + below * ratio_prev
        ratio_now = -above / pivot_value
        solved_now = (tracer_field[level_index] + below[:, None] * solved_prev) / pivot_value[
            :, None
        ]
        ratios.append(ratio_now)
        solveds.append(solved_now)
        ratio_prev = ratio_now
        solved_prev = solved_now
    results = [None] * levels
    results[levels - 1] = solveds[levels - 1]
    for level_index in range(levels - 2, -1, -1):
        results[level_index] = (
            solveds[level_index] - ratios[level_index][:, None] * results[level_index + 1]
        )
    return jnp.stack(results, axis=0)


def bit_mask(amount, position):
    return (amount // 2**position % 2 == 1)[:, :, None]


PAIR = 2


def pair_order(cells):
    cols = jnp.arange(cells * NTR)
    cell, tracer = cols // NTR, cols % NTR
    target = (tracer // PAIR) * cells * PAIR + cell * PAIR + tracer % PAIR
    return target


def permutation(target, inverse):
    cols = jnp.arange(target.shape[0])
    if inverse:
        matrix = cols[:, None] == target[None, :]
    else:
        matrix = cols[None, :] == target[:, None]
    return matrix.astype(jnp.bfloat16)


def permute_block(block, matrix):
    high = block.astype(jnp.bfloat16)
    rest = block - high.astype(jnp.float32)
    middle = rest.astype(jnp.bfloat16)
    low = (rest - middle.astype(jnp.float32)).astype(jnp.bfloat16)
    total = jnp.dot(high, matrix, preferred_element_type=jnp.float32)
    total = total + jnp.dot(middle, matrix, preferred_element_type=jnp.float32)
    return total + jnp.dot(low, matrix, preferred_element_type=jnp.float32)


CHUNKS = 4
MESH_ID = pl.DeviceIdType.MESH


def greet(count, me, lat):
    barrier = pltpu.get_barrier_semaphore()
    for offset in range(1, count):
        peer = lax.rem(me + offset, count)
        pl.semaphore_signal(barrier, 1, device_id=(peer, lat), device_id_type=MESH_ID)
    return barrier


def entry_kernel(x_ref, matrix_ref, dst_ref, moved, send_sem, recv_sem, local_sem, *, src_at, dst_at):
    count = lax.axis_size("lon")
    me = lax.axis_index("lon")
    lat = lax.axis_index("lat")
    levels = x_ref.shape[0]
    per = levels // CHUNKS
    barrier = greet(count, me, lat)
    copies = []
    locals_ = []
    for chunk in range(CHUNKS):
        def body(k, carry):
            moved[k] = permute_block(x_ref[k], matrix_ref[...])
            return carry

        lax.fori_loop(chunk * per, (chunk + 1) * per, body, 0)
        if chunk == 0:
            pl.semaphore_wait(barrier, count - 1)
        part = pl.ds(chunk * per, per)
        for offset in range(1, count):
            peer = lax.rem(me + offset, count)
            copy = pltpu.make_async_remote_copy(
                src_ref=src_at(moved, peer, part),
                dst_ref=dst_at(dst_ref, me, part),
                send_sem=send_sem.at[chunk, offset],
                recv_sem=recv_sem.at[chunk, offset],
                device_id=(peer, lat),
                device_id_type=MESH_ID,
            )
            copy.start()
            copies.append(copy)
        local = pltpu.make_async_copy(src_at(moved, me, part), dst_at(dst_ref, me, part), local_sem.at[chunk])
        local.start()
        locals_.append(local)
    for copy in copies:
        copy.wait_send()
    for copy in copies:
        copy.wait_recv()
    for local in locals_:
        local.wait()


def exit_kernel(src_ref, matrix_ref, out_ref, landed, send_sem, recv_sem, local_sem, *, src_at, dst_at):
    count = lax.axis_size("lon")
    me = lax.axis_index("lon")
    lat = lax.axis_index("lat")
    levels = out_ref.shape[0]
    per = levels // CHUNKS
    barrier = greet(count, me, lat)
    pl.semaphore_wait(barrier, count - 1)
    copies = []
    locals_ = []
    for chunk in range(CHUNKS):
        part = pl.ds(chunk * per, per)
        row = []
        for offset in range(1, count):
            peer = lax.rem(me + offset, count)
            copy = pltpu.make_async_remote_copy(
                src_ref=src_at(src_ref, peer, part),
                dst_ref=dst_at(landed, me, part),
                send_sem=send_sem.at[chunk, offset],
                recv_sem=recv_sem.at[chunk, offset],
                device_id=(peer, lat),
                device_id_type=MESH_ID,
            )
            copy.start()
            row.append(copy)
        copies.append(row)
        local = pltpu.make_async_copy(src_at(src_ref, me, part), dst_at(landed, me, part), local_sem.at[chunk])
        local.start()
        locals_.append(local)
    for chunk in range(CHUNKS):
        for copy in copies[chunk]:
            copy.wait_recv()
        locals_[chunk].wait()

        def body(k, carry):
            out_ref[k] = permute_block(landed[k], matrix_ref[...])
            return carry

        lax.fori_loop(chunk * per, (chunk + 1) * per, body, 0)
    for row in copies:
        for copy in row:
            copy.wait_send()


def run_exchange(kernel, operand, matrix, out_shape, src_spec, out_spec, scratch, src_at, dst_at, ident):
    count = lax.axis_size("lon")
    return pl.pallas_call(
        functools.partial(kernel, src_at=src_at, dst_at=dst_at),
        out_shape=jax.ShapeDtypeStruct(out_shape, operand.dtype),
        in_specs=[src_spec, pl.BlockSpec(memory_space=pltpu.VMEM)],
        out_specs=out_spec,
        scratch_shapes=[
            pltpu.VMEM(scratch, operand.dtype),
            pltpu.SemaphoreType.DMA((CHUNKS, count)),
            pltpu.SemaphoreType.DMA((CHUNKS, count)),
            pltpu.SemaphoreType.DMA((CHUNKS,)),
        ],
        compiler_params=pltpu.CompilerParams(collective_id=ident, has_side_effects=True),
    )(operand, matrix)


def to_columns(block):
    levels, rows, width = block.shape
    cells = width // NTR
    devices = lax.axis_size("lon")
    parts = devices // (NTR // PAIR)
    count = rows // parts
    lane = cells * PAIR

    def src_at(ref, peer, part):
        return ref.at[part, pl.ds((peer % parts) * count, count), pl.ds((peer // parts) * lane, lane)]

    def dst_at(ref, sender, part):
        return ref.at[part, :, pl.ds(sender * lane, lane)]

    return run_exchange(
        entry_kernel, block, permutation(pair_order(cells), False), (levels, count, devices * lane),
        pl.BlockSpec(memory_space=pltpu.VMEM), pl.BlockSpec(memory_space=pl.ANY), block.shape,
        src_at, dst_at, 0,
    )


def from_columns(field, rows):
    levels, count, width = field.shape
    devices = lax.axis_size("lon")
    parts = devices // (NTR // PAIR)
    lane = width // devices
    cells = lane // PAIR

    def src_at(ref, peer, part):
        return ref.at[part, :, pl.ds(peer * lane, lane)]

    def dst_at(ref, sender, part):
        return ref.at[part, pl.ds((sender % parts) * count, count), pl.ds((sender // parts) * lane, lane)]

    shape = (levels, rows, cells * NTR)
    return run_exchange(
        exit_kernel, field, permutation(pair_order(cells), True), shape,
        pl.BlockSpec(memory_space=pl.ANY), pl.BlockSpec(memory_space=pltpu.VMEM), shape,
        src_at, dst_at, 1,
    )


def lat_halo(field, width):
    lon_n = lax.axis_size("lon")
    lat_n = lax.axis_size("lat")
    parts = lon_n // (NTR // PAIR)
    up = []
    for b in range(lat_n):
        for l in range(lon_n):
            t, h = l // parts, l % parts
            g = b * parts + h
            if g + 1 < lat_n * parts:
                nb, nh = (g + 1) // parts, (g + 1) % parts
                up.append((l * lat_n + b, (t * parts + nh) * lat_n + nb))
    down = [(d, s) for s, d in up]
    rows = field.shape[1]
    below = lax.ppermute(field[:, rows - width + 1 :], ("lon", "lat"), up)
    above = lax.ppermute(field[:, :width], ("lon", "lat"), down)
    return jnp.concatenate([below[:, :1], below, field, above], axis=1)


def roll_rows(field, amount):
    cells = field.shape[2] // PAIR
    current = field
    for position in range(cells.bit_length() - 1):
        moved = jnp.roll(current, PAIR * 2**position, axis=2)
        current = jnp.where(bit_mask(amount, position), moved, current)
    return current


def lon_cubic(shifted, fraction):
    weights = cubic_weights(fraction)
    taps = [jnp.roll(shifted, PAIR * (1 - p), axis=2) for p in range(4)]
    summed = None
    for p in range(4):
        addend = weights[p][:, :, None] * taps[p]
        summed = addend if summed is None else summed + addend
    return summed


def own_rows(values, count):
    parts = lax.axis_size("lon") // (NTR // PAIR)
    start = (lax.axis_index("lon") % parts) * count
    return lax.dynamic_slice_in_dim(values, start, count, axis=values.ndim - 1)


def per_device(tracers, lon_shift, lon_frac, lat_shift, lat_frac, remap_frac, diffusivity):
    rows = tracers.shape[1]
    field = to_columns(tracers)
    count = field.shape[1]
    width = field.shape[2]
    lon_shift, lon_frac, lat_shift, lat_frac, remap_frac, diffusivity = (
        own_rows(v, count) for v in (lon_shift, lon_frac, lat_shift, lat_frac, remap_frac, diffusivity)
    )
    for time_step in range(STEPS):
        padded = lat_halo(field, 3)
        field = lat_step(padded, lat_shift[time_step], lat_frac[time_step], count)
        amount = jnp.remainder(lon_shift[time_step], width // PAIR)
        field = lon_cubic(roll_rows(field, amount), lon_frac[time_step])
        field = remap(field, remap_frac[time_step])
        field = diffuse(field, diffusivity)
    return from_columns(field, rows)


def solution(mesh):
    in_specs = (
        P(None, "lat", "lon"),
        P(None, None, "lat"),
        P(None, None, "lat"),
        P(None, None, "lat"),
        P(None, None, "lat"),
        P(None, None, "lat"),
        P(None, "lat"),
    )
    out_specs = P(None, "lat", "lon")
    return jax.shard_map(
        per_device, mesh=mesh, in_specs=in_specs, out_specs=out_specs, check_vma=False
    )
```

```python
import functools

import jax
import jax.numpy as jnp
from jax import lax
from jax.experimental import pallas as pl
from jax.experimental.pallas import tpu as pltpu
from jax.sharding import PartitionSpec as P

NTR = 8
STEPS = 2


def from_behind(x, axis, by):
    peers = lax.axis_size(axis)
    return lax.ppermute(x, axis, [(i, (i + by) % peers) for i in range(peers)])


def with_halo(block, sides, width, periodic):
    for axis, dim in sides:
        count = lax.axis_size(axis)
        forward = [(i, i + 1) for i in range(count - 1)]
        if periodic:
            forward.append((count - 1, 0))
        backward = [(target, source) for source, target in forward]
        low = lax.ppermute(
            lax.slice_in_dim(block, block.shape[dim] - width, None, axis=dim), axis, forward
        )
        high = lax.ppermute(lax.slice_in_dim(block, 0, width, axis=dim), axis, backward)
        block = jnp.concatenate([low, block, high], axis=dim)
    return block


def cubic_weights(fraction):
    w_zero = -fraction * (fraction - 1.0) * (fraction - 2.0) / 6.0
    w_one = (fraction + 1.0) * (fraction - 1.0) * (fraction - 2.0) / 2.0
    w_two = -(fraction + 1.0) * fraction * (fraction - 2.0) / 2.0
    w_three = (fraction + 1.0) * fraction * (fraction - 1.0) / 6.0
    return (w_zero, w_one, w_two, w_three)


def lat_step(padded, offset, fraction, row_count):
    weights = cubic_weights(fraction)
    summed = None
    for place_index in range(6):
        row_delta = place_index - 2
        coeff = jnp.zeros_like(fraction)
        for tap_index in range(4):
            coeff = coeff + jnp.where(offset == tap_index - 1 - row_delta, weights[tap_index], 0.0)
        addend = coeff[:, :, None] * padded[:, 1 + place_index : 1 + place_index + row_count, :]
        summed = addend if summed is None else summed + addend
    return summed


def lon_step(wrapped, fraction, tracer_count):
    weights = cubic_weights(fraction)
    width_cols = wrapped.shape[2] - 4 * tracer_count
    summed = None
    for tap_index in range(4):
        offset_cols = (1 + tap_index) * tracer_count
        addend = (
            weights[tap_index][:, :, None] * wrapped[:, :, offset_cols : offset_cols + width_cols]
        )
        summed = addend if summed is None else summed + addend
    return summed


def remap(tracer_field, fraction):
    level_above = jnp.concatenate([tracer_field[1:], tracer_field[-1:]], axis=0)
    return (1.0 - fraction)[:, :, None] * tracer_field + fraction[:, :, None] * level_above


def diffuse(tracer_field, kappa):
    levels = tracer_field.shape[0]
    face_kappa = 0.5 * (kappa[:-1] + kappa[1:])
    zero_face = jnp.zeros_like(kappa[:1])
    face_below = jnp.concatenate([zero_face, face_kappa], axis=0)
    face_above = jnp.concatenate([face_kappa, zero_face], axis=0)
    ratio_prev = jnp.zeros_like(kappa[0])
    solved_prev = jnp.zeros_like(tracer_field[0])
    ratios = []
    solveds = []
    for level_index in range(levels):
        below = face_below[level_index]
        above = face_above[level_index]
        pivot_value = 1.0 + below + above + below * ratio_prev
        ratio_now = -above / pivot_value
        solved_now = (tracer_field[level_index] + below[:, None] * solved_prev) / pivot_value[
            :, None
        ]
        ratios.append(ratio_now)
        solveds.append(solved_now)
        ratio_prev = ratio_now
        solved_prev = solved_now
    results = [None] * levels
    results[levels - 1] = solveds[levels - 1]
    for level_index in range(levels - 2, -1, -1):
        results[level_index] = (
            solveds[level_index] - ratios[level_index][:, None] * results[level_index + 1]
        )
    return jnp.stack(results, axis=0)


def bit_mask(amount, position):
    return (amount // 2**position % 2 == 1)[:, :, None]


PAIR = 2


def pair_order(cells):
    cols = jnp.arange(cells * NTR)
    cell, tracer = cols // NTR, cols % NTR
    target = (tracer // PAIR) * cells * PAIR + cell * PAIR + tracer % PAIR
    return target


def permutation(target, inverse):
    cols = jnp.arange(target.shape[0])
    if inverse:
        matrix = cols[:, None] == target[None, :]
    else:
        matrix = cols[None, :] == target[:, None]
    return matrix.astype(jnp.bfloat16)


def permute_block(block, matrix):
    high = block.astype(jnp.bfloat16)
    rest = block - high.astype(jnp.float32)
    middle = rest.astype(jnp.bfloat16)
    low = (rest - middle.astype(jnp.float32)).astype(jnp.bfloat16)
    total = jnp.dot(high, matrix, preferred_element_type=jnp.float32)
    total = total + jnp.dot(middle, matrix, preferred_element_type=jnp.float32)
    return total + jnp.dot(low, matrix, preferred_element_type=jnp.float32)


CHUNKS = 4
MESH_ID = pl.DeviceIdType.MESH


def greet(count, me, lat):
    barrier = pltpu.get_barrier_semaphore()
    for offset in range(1, count):
        peer = lax.rem(me + offset, count)
        pl.semaphore_signal(barrier, 1, device_id=(peer, lat), device_id_type=MESH_ID)
    return barrier


def neighbours(parts):
    lon = lax.axis_index("lon")
    lat = lax.axis_index("lat")
    bands = lax.axis_size("lat")
    quarter = lon % parts
    inside_up = quarter < parts - 1
    inside_down = quarter > 0
    has_up = jnp.logical_or(inside_up, lat < bands - 1)
    has_down = jnp.logical_or(inside_down, lat > 0)
    up = (jnp.where(inside_up, lon + 1, lon + 1 - parts), jnp.where(inside_up, lat, lat + 1))
    down = (jnp.where(inside_down, lon - 1, lon + parts - 1), jnp.where(inside_down, lat, lat - 1))
    return has_up, up, has_down, down


def entry_kernel(x_ref, matrix_ref, field_ref, below_ref, above_ref, moved, landed, top_stage, bottom_stage,
                 send_sem, recv_sem, local_sem, halo_send, halo_recv, *, src_at, dst_at, parts):
    count = lax.axis_size("lon")
    me = lax.axis_index("lon")
    lat = lax.axis_index("lat")
    levels = x_ref.shape[0]
    rows = landed.shape[1]
    per = levels // CHUNKS
    has_up, up, has_down, down = neighbours(parts)
    barrier = greet(count, me, lat)

    @pl.when(has_up)
    def _():
        pl.semaphore_signal(barrier, 1, device_id=up, device_id_type=MESH_ID)

    @pl.when(has_down)
    def _():
        pl.semaphore_signal(barrier, 1, device_id=down, device_id_type=MESH_ID)

    copies = []
    locals_ = []
    for chunk in range(CHUNKS):
        def body(k, carry):
            moved[k] = permute_block(x_ref[k], matrix_ref[...])
            return carry

        lax.fori_loop(chunk * per, (chunk + 1) * per, body, 0)
        if chunk == 0:
            pl.semaphore_wait(barrier, count - 1 + has_up.astype(jnp.int32) + has_down.astype(jnp.int32))
        part = pl.ds(chunk * per, per)
        for offset in range(1, count):
            peer = lax.rem(me + offset, count)
            copy = pltpu.make_async_remote_copy(
                src_ref=src_at(moved, peer, part),
                dst_ref=dst_at(landed, me, part),
                send_sem=send_sem.at[chunk, offset],
                recv_sem=recv_sem.at[chunk, offset],
                device_id=(peer, lat),
                device_id_type=MESH_ID,
            )
            copy.start()
            copies.append(copy)
        local = pltpu.make_async_copy(src_at(moved, me, part), dst_at(landed, me, part), local_sem.at[chunk])
        local.start()
        locals_.append(local)
    for copy in copies:
        copy.wait_recv()
    for local in locals_:
        local.wait()
    top_stage[...] = landed[:, rows - top_stage.shape[1] :, :]
    bottom_stage[...] = landed[:, : bottom_stage.shape[1], :]
    to_up = pltpu.make_async_remote_copy(
        src_ref=top_stage, dst_ref=below_ref, send_sem=halo_send.at[0], recv_sem=halo_recv.at[0],
        device_id=up, device_id_type=MESH_ID,
    )
    to_down = pltpu.make_async_remote_copy(
        src_ref=bottom_stage, dst_ref=above_ref, send_sem=halo_send.at[1], recv_sem=halo_recv.at[1],
        device_id=down, device_id_type=MESH_ID,
    )

    @pl.when(has_up)
    def _():
        to_up.start()

    @pl.when(has_down)
    def _():
        to_down.start()

    field_ref[...] = landed[...]

    @pl.when(jnp.logical_not(has_down))
    def _():
        below_ref[...] = jnp.zeros(below_ref.shape, below_ref.dtype)

    @pl.when(jnp.logical_not(has_up))
    def _():
        above_ref[...] = jnp.zeros(above_ref.shape, above_ref.dtype)

    for copy in copies:
        copy.wait_send()

    @pl.when(has_up)
    def _():
        to_up.wait_send()
        to_down.wait_recv()

    @pl.when(has_down)
    def _():
        to_down.wait_send()
        to_up.wait_recv()


def exit_kernel(src_ref, matrix_ref, out_ref, landed, send_sem, recv_sem, local_sem, *, src_at, dst_at):
    count = lax.axis_size("lon")
    me = lax.axis_index("lon")
    lat = lax.axis_index("lat")
    levels = out_ref.shape[0]
    per = levels // CHUNKS
    barrier = greet(count, me, lat)
    pl.semaphore_wait(barrier, count - 1)
    copies = []
    locals_ = []
    for chunk in range(CHUNKS):
        part = pl.ds(chunk * per, per)
        row = []
        for offset in range(1, count):
            peer = lax.rem(me + offset, count)
            copy = pltpu.make_async_remote_copy(
                src_ref=src_at(src_ref, peer, part),
                dst_ref=dst_at(landed, me, part),
                send_sem=send_sem.at[chunk, offset],
                recv_sem=recv_sem.at[chunk, offset],
                device_id=(peer, lat),
                device_id_type=MESH_ID,
            )
            copy.start()
            row.append(copy)
        copies.append(row)
        local = pltpu.make_async_copy(src_at(src_ref, me, part), dst_at(landed, me, part), local_sem.at[chunk])
        local.start()
        locals_.append(local)
    for chunk in range(CHUNKS):
        for copy in copies[chunk]:
            copy.wait_recv()
        locals_[chunk].wait()

        def body(k, carry):
            out_ref[k] = permute_block(landed[k], matrix_ref[...])
            return carry

        lax.fori_loop(chunk * per, (chunk + 1) * per, body, 0)
    for row in copies:
        for copy in row:
            copy.wait_send()


def run_exchange(kernel, operand, matrix, out_shape, src_spec, out_spec, scratch, src_at, dst_at, ident):
    count = lax.axis_size("lon")
    return pl.pallas_call(
        functools.partial(kernel, src_at=src_at, dst_at=dst_at),
        out_shape=jax.ShapeDtypeStruct(out_shape, operand.dtype),
        in_specs=[src_spec, pl.BlockSpec(memory_space=pltpu.VMEM)],
        out_specs=out_spec,
        scratch_shapes=[
            pltpu.VMEM(scratch, operand.dtype),
            pltpu.SemaphoreType.DMA((CHUNKS, count)),
            pltpu.SemaphoreType.DMA((CHUNKS, count)),
            pltpu.SemaphoreType.DMA((CHUNKS,)),
        ],
        compiler_params=pltpu.CompilerParams(collective_id=ident, has_side_effects=True),
    )(operand, matrix)


def to_columns(block):
    levels, rows, width = block.shape
    cells = width // NTR
    devices = lax.axis_size("lon")
    parts = devices // (NTR // PAIR)
    count = rows // parts
    lane = cells * PAIR

    def src_at(ref, peer, part):
        return ref.at[part, pl.ds((peer % parts) * count, count), pl.ds((peer // parts) * lane, lane)]

    def dst_at(ref, sender, part):
        return ref.at[part, :, pl.ds(sender * lane, lane)]

    vmem = pl.BlockSpec(memory_space=pltpu.VMEM)
    field_shape = (levels, count, devices * lane)
    below_shape = (levels, 2, devices * lane)
    above_shape = (levels, 3, devices * lane)
    return pl.pallas_call(
        functools.partial(entry_kernel, src_at=src_at, dst_at=dst_at, parts=parts),
        out_shape=tuple(jax.ShapeDtypeStruct(shape, block.dtype) for shape in (field_shape, below_shape, above_shape)),
        in_specs=[vmem, vmem],
        out_specs=(vmem, vmem, vmem),
        scratch_shapes=[
            pltpu.VMEM(block.shape, block.dtype),
            pltpu.VMEM(field_shape, block.dtype),
            pltpu.VMEM(below_shape, block.dtype),
            pltpu.VMEM(above_shape, block.dtype),
            pltpu.SemaphoreType.DMA((CHUNKS, devices)),
            pltpu.SemaphoreType.DMA((CHUNKS, devices)),
            pltpu.SemaphoreType.DMA((CHUNKS,)),
            pltpu.SemaphoreType.DMA((2,)),
            pltpu.SemaphoreType.DMA((2,)),
        ],
        compiler_params=pltpu.CompilerParams(collective_id=0, has_side_effects=True),
    )(block, permutation(pair_order(cells), False))


def from_columns(field, rows):
    levels, count, width = field.shape
    devices = lax.axis_size("lon")
    parts = devices // (NTR // PAIR)
    lane = width // devices
    cells = lane // PAIR

    def src_at(ref, peer, part):
        return ref.at[part, :, pl.ds(peer * lane, lane)]

    def dst_at(ref, sender, part):
        return ref.at[part, pl.ds((sender % parts) * count, count), pl.ds((sender // parts) * lane, lane)]

    shape = (levels, rows, cells * NTR)
    return run_exchange(
        exit_kernel, field, permutation(pair_order(cells), True), shape,
        pl.BlockSpec(memory_space=pl.ANY), pl.BlockSpec(memory_space=pltpu.VMEM), shape,
        src_at, dst_at, 1,
    )


def lat_halo(field, width):
    lon_n = lax.axis_size("lon")
    lat_n = lax.axis_size("lat")
    parts = lon_n // (NTR // PAIR)
    up = []
    for b in range(lat_n):
        for l in range(lon_n):
            t, h = l // parts, l % parts
            g = b * parts + h
            if g + 1 < lat_n * parts:
                nb, nh = (g + 1) // parts, (g + 1) % parts
                up.append((l * lat_n + b, (t * parts + nh) * lat_n + nb))
    down = [(d, s) for s, d in up]
    rows = field.shape[1]
    below = lax.ppermute(field[:, rows - width + 1 :], ("lon", "lat"), up)
    above = lax.ppermute(field[:, :width], ("lon", "lat"), down)
    return jnp.concatenate([below[:, :1], below, field, above], axis=1)


def roll_rows(field, amount):
    cells = field.shape[2] // PAIR
    current = field
    for position in range(cells.bit_length() - 1):
        moved = jnp.roll(current, PAIR * 2**position, axis=2)
        current = jnp.where(bit_mask(amount, position), moved, current)
    return current


def lon_cubic(shifted, fraction):
    weights = cubic_weights(fraction)
    taps = [jnp.roll(shifted, PAIR * (1 - p), axis=2) for p in range(4)]
    summed = None
    for p in range(4):
        addend = weights[p][:, :, None] * taps[p]
        summed = addend if summed is None else summed + addend
    return summed


def own_rows(values, count):
    parts = lax.axis_size("lon") // (NTR // PAIR)
    start = (lax.axis_index("lon") % parts) * count
    return lax.dynamic_slice_in_dim(values, start, count, axis=values.ndim - 1)


def per_device(tracers, lon_shift, lon_frac, lat_shift, lat_frac, remap_frac, diffusivity):
    rows = tracers.shape[1]
    field, below, above = to_columns(tracers)
    count = field.shape[1]
    width = field.shape[2]
    lon_shift, lon_frac, lat_shift, lat_frac, remap_frac, diffusivity = (
        own_rows(v, count) for v in (lon_shift, lon_frac, lat_shift, lat_frac, remap_frac, diffusivity)
    )
    for time_step in range(STEPS):
        if time_step == 0:
            padded = jnp.concatenate([below[:, :1], below, field, above], axis=1)
        else:
            padded = lat_halo(field, 3)
        field = lat_step(padded, lat_shift[time_step], lat_frac[time_step], count)
        amount = jnp.remainder(lon_shift[time_step], width // PAIR)
        field = lon_cubic(roll_rows(field, amount), lon_frac[time_step])
        field = remap(field, remap_frac[time_step])
        field = diffuse(field, diffusivity)
    return from_columns(field, rows)


def solution(mesh):
    in_specs = (
        P(None, "lat", "lon"),
        P(None, None, "lat"),
        P(None, None, "lat"),
        P(None, None, "lat"),
        P(None, None, "lat"),
        P(None, None, "lat"),
        P(None, "lat"),
    )
    out_specs = P(None, "lat", "lon")
    return jax.shard_map(
        per_device, mesh=mesh, in_specs=in_specs, out_specs=out_specs, check_vma=False
    )
```

```python
import functools

import jax
import jax.numpy as jnp
from jax import lax
from jax.experimental import pallas as pl
from jax.experimental.pallas import tpu as pltpu
from jax.sharding import PartitionSpec as P

NTR = 8
STEPS = 2


def from_behind(x, axis, by):
    peers = lax.axis_size(axis)
    return lax.ppermute(x, axis, [(i, (i + by) % peers) for i in range(peers)])


def with_halo(block, sides, width, periodic):
    for axis, dim in sides:
        count = lax.axis_size(axis)
        forward = [(i, i + 1) for i in range(count - 1)]
        if periodic:
            forward.append((count - 1, 0))
        backward = [(target, source) for source, target in forward]
        low = lax.ppermute(
            lax.slice_in_dim(block, block.shape[dim] - width, None, axis=dim), axis, forward
        )
        high = lax.ppermute(lax.slice_in_dim(block, 0, width, axis=dim), axis, backward)
        block = jnp.concatenate([low, block, high], axis=dim)
    return block


def cubic_weights(fraction):
    w_zero = -fraction * (fraction - 1.0) * (fraction - 2.0) / 6.0
    w_one = (fraction + 1.0) * (fraction - 1.0) * (fraction - 2.0) / 2.0
    w_two = -(fraction + 1.0) * fraction * (fraction - 2.0) / 2.0
    w_three = (fraction + 1.0) * fraction * (fraction - 1.0) / 6.0
    return (w_zero, w_one, w_two, w_three)


def lat_step(padded, offset, fraction, row_count):
    weights = cubic_weights(fraction)
    summed = None
    for place_index in range(6):
        row_delta = place_index - 2
        coeff = jnp.zeros_like(fraction)
        for tap_index in range(4):
            coeff = coeff + jnp.where(offset == tap_index - 1 - row_delta, weights[tap_index], 0.0)
        addend = coeff[:, :, None] * padded[:, 1 + place_index : 1 + place_index + row_count, :]
        summed = addend if summed is None else summed + addend
    return summed


def lon_step(wrapped, fraction, tracer_count):
    weights = cubic_weights(fraction)
    width_cols = wrapped.shape[2] - 4 * tracer_count
    summed = None
    for tap_index in range(4):
        offset_cols = (1 + tap_index) * tracer_count
        addend = (
            weights[tap_index][:, :, None] * wrapped[:, :, offset_cols : offset_cols + width_cols]
        )
        summed = addend if summed is None else summed + addend
    return summed


def remap(tracer_field, fraction):
    level_above = jnp.concatenate([tracer_field[1:], tracer_field[-1:]], axis=0)
    return (1.0 - fraction)[:, :, None] * tracer_field + fraction[:, :, None] * level_above


def diffuse(tracer_field, kappa):
    levels = tracer_field.shape[0]
    face_kappa = 0.5 * (kappa[:-1] + kappa[1:])
    zero_face = jnp.zeros_like(kappa[:1])
    face_below = jnp.concatenate([zero_face, face_kappa], axis=0)
    face_above = jnp.concatenate([face_kappa, zero_face], axis=0)
    ratio_prev = jnp.zeros_like(kappa[0])
    solved_prev = jnp.zeros_like(tracer_field[0])
    ratios = []
    solveds = []
    for level_index in range(levels):
        below = face_below[level_index]
        above = face_above[level_index]
        pivot_value = 1.0 + below + above + below * ratio_prev
        ratio_now = -above / pivot_value
        solved_now = (tracer_field[level_index] + below[:, None] * solved_prev) / pivot_value[
            :, None
        ]
        ratios.append(ratio_now)
        solveds.append(solved_now)
        ratio_prev = ratio_now
        solved_prev = solved_now
    results = [None] * levels
    results[levels - 1] = solveds[levels - 1]
    for level_index in range(levels - 2, -1, -1):
        results[level_index] = (
            solveds[level_index] - ratios[level_index][:, None] * results[level_index + 1]
        )
    return jnp.stack(results, axis=0)


def bit_mask(amount, position):
    return (amount // 2**position % 2 == 1)[:, :, None]


PAIR = 2


def pair_order(cells):
    cols = jnp.arange(cells * NTR)
    cell, tracer = cols // NTR, cols % NTR
    target = (tracer // PAIR) * cells * PAIR + cell * PAIR + tracer % PAIR
    return target


def permutation(target, inverse):
    cols = jnp.arange(target.shape[0])
    if inverse:
        matrix = cols[:, None] == target[None, :]
    else:
        matrix = cols[None, :] == target[:, None]
    return matrix.astype(jnp.bfloat16)


def permute_block(block, matrix):
    high = block.astype(jnp.bfloat16)
    rest = block - high.astype(jnp.float32)
    middle = rest.astype(jnp.bfloat16)
    low = (rest - middle.astype(jnp.float32)).astype(jnp.bfloat16)
    total = jnp.dot(high, matrix, preferred_element_type=jnp.float32)
    total = total + jnp.dot(middle, matrix, preferred_element_type=jnp.float32)
    return total + jnp.dot(low, matrix, preferred_element_type=jnp.float32)


CHUNKS = 4
MESH_ID = pl.DeviceIdType.MESH


def greet(count, me, lat):
    barrier = pltpu.get_barrier_semaphore()
    for offset in range(1, count):
        peer = lax.rem(me + offset, count)
        pl.semaphore_signal(barrier, 1, device_id=(peer, lat), device_id_type=MESH_ID)
    return barrier


def neighbours(parts):
    lon = lax.axis_index("lon")
    lat = lax.axis_index("lat")
    bands = lax.axis_size("lat")
    quarter = lon % parts
    inside_up = quarter < parts - 1
    inside_down = quarter > 0
    has_up = jnp.logical_or(inside_up, lat < bands - 1)
    has_down = jnp.logical_or(inside_down, lat > 0)
    up = (jnp.where(inside_up, lon + 1, lon + 1 - parts), jnp.where(inside_up, lat, lat + 1))
    down = (jnp.where(inside_down, lon - 1, lon + parts - 1), jnp.where(inside_down, lat, lat - 1))
    return has_up, up, has_down, down


def entry_kernel(x_ref, matrix_ref, padded_ref, moved, landed, top_stage, bottom_stage, below_ref, above_ref,
                 send_sem, recv_sem, local_sem, halo_send, halo_recv, *, src_at, dst_at, parts):
    count = lax.axis_size("lon")
    me = lax.axis_index("lon")
    lat = lax.axis_index("lat")
    levels = x_ref.shape[0]
    rows = landed.shape[1]
    per = levels // CHUNKS
    has_up, up, has_down, down = neighbours(parts)
    barrier = greet(count, me, lat)

    @pl.when(has_up)
    def _():
        pl.semaphore_signal(barrier, 1, device_id=up, device_id_type=MESH_ID)

    @pl.when(has_down)
    def _():
        pl.semaphore_signal(barrier, 1, device_id=down, device_id_type=MESH_ID)

    copies = []
    locals_ = []
    for chunk in range(CHUNKS):
        def body(k, carry):
            moved[k] = permute_block(x_ref[k], matrix_ref[...])
            return carry

        lax.fori_loop(chunk * per, (chunk + 1) * per, body, 0)
        if chunk == 0:
            pl.semaphore_wait(barrier, count - 1 + has_up.astype(jnp.int32) + has_down.astype(jnp.int32))
        part = pl.ds(chunk * per, per)
        for offset in range(1, count):
            peer = lax.rem(me + offset, count)
            copy = pltpu.make_async_remote_copy(
                src_ref=src_at(moved, peer, part),
                dst_ref=dst_at(landed, me, part),
                send_sem=send_sem.at[chunk, offset],
                recv_sem=recv_sem.at[chunk, offset],
                device_id=(peer, lat),
                device_id_type=MESH_ID,
            )
            copy.start()
            copies.append(copy)
        local = pltpu.make_async_copy(src_at(moved, me, part), dst_at(landed, me, part), local_sem.at[chunk])
        local.start()
        locals_.append(local)
    for copy in copies:
        copy.wait_recv()
    for local in locals_:
        local.wait()
    top_stage[...] = landed[:, rows - top_stage.shape[1] :, :]
    bottom_stage[...] = landed[:, : bottom_stage.shape[1], :]
    to_up = pltpu.make_async_remote_copy(
        src_ref=top_stage, dst_ref=below_ref, send_sem=halo_send.at[0], recv_sem=halo_recv.at[0],
        device_id=up, device_id_type=MESH_ID,
    )
    to_down = pltpu.make_async_remote_copy(
        src_ref=bottom_stage, dst_ref=above_ref, send_sem=halo_send.at[1], recv_sem=halo_recv.at[1],
        device_id=down, device_id_type=MESH_ID,
    )

    @pl.when(has_up)
    def _():
        to_up.start()

    @pl.when(has_down)
    def _():
        to_down.start()

    low = below_ref.shape[1] + 1
    padded_ref[:, low : low + rows, :] = landed[...]
    padded_ref[:, :1, :] = jnp.zeros((levels, 1, landed.shape[2]), landed.dtype)

    for copy in copies:
        copy.wait_send()

    @pl.when(has_up)
    def _():
        to_up.wait_send()
        to_down.wait_recv()
        padded_ref[:, low + rows :, :] = above_ref[...]

    @pl.when(jnp.logical_not(has_up))
    def _():
        padded_ref[:, low + rows :, :] = jnp.zeros(above_ref.shape, above_ref.dtype)

    @pl.when(has_down)
    def _():
        to_down.wait_send()
        to_up.wait_recv()
        padded_ref[:, 1:low, :] = below_ref[...]

    @pl.when(jnp.logical_not(has_down))
    def _():
        padded_ref[:, 1:low, :] = jnp.zeros(below_ref.shape, below_ref.dtype)


def exit_kernel(src_ref, matrix_ref, out_ref, landed, send_sem, recv_sem, local_sem, *, src_at, dst_at):
    count = lax.axis_size("lon")
    me = lax.axis_index("lon")
    lat = lax.axis_index("lat")
    levels = out_ref.shape[0]
    per = levels // CHUNKS
    barrier = greet(count, me, lat)
    pl.semaphore_wait(barrier, count - 1)
    copies = []
    locals_ = []
    for chunk in range(CHUNKS):
        part = pl.ds(chunk * per, per)
        row = []
        for offset in range(1, count):
            peer = lax.rem(me + offset, count)
            copy = pltpu.make_async_remote_copy(
                src_ref=src_at(src_ref, peer, part),
                dst_ref=dst_at(landed, me, part),
                send_sem=send_sem.at[chunk, offset],
                recv_sem=recv_sem.at[chunk, offset],
                device_id=(peer, lat),
                device_id_type=MESH_ID,
            )
            copy.start()
            row.append(copy)
        copies.append(row)
        local = pltpu.make_async_copy(src_at(src_ref, me, part), dst_at(landed, me, part), local_sem.at[chunk])
        local.start()
        locals_.append(local)
    for chunk in range(CHUNKS):
        for copy in copies[chunk]:
            copy.wait_recv()
        locals_[chunk].wait()

        def body(k, carry):
            out_ref[k] = permute_block(landed[k], matrix_ref[...])
            return carry

        lax.fori_loop(chunk * per, (chunk + 1) * per, body, 0)
    for row in copies:
        for copy in row:
            copy.wait_send()


def run_exchange(kernel, operand, matrix, out_shape, src_spec, out_spec, scratch, src_at, dst_at, ident):
    count = lax.axis_size("lon")
    return pl.pallas_call(
        functools.partial(kernel, src_at=src_at, dst_at=dst_at),
        out_shape=jax.ShapeDtypeStruct(out_shape, operand.dtype),
        in_specs=[src_spec, pl.BlockSpec(memory_space=pltpu.VMEM)],
        out_specs=out_spec,
        scratch_shapes=[
            pltpu.VMEM(scratch, operand.dtype),
            pltpu.SemaphoreType.DMA((CHUNKS, count)),
            pltpu.SemaphoreType.DMA((CHUNKS, count)),
            pltpu.SemaphoreType.DMA((CHUNKS,)),
        ],
        compiler_params=pltpu.CompilerParams(collective_id=ident, has_side_effects=True),
    )(operand, matrix)


def to_columns(block):
    levels, rows, width = block.shape
    cells = width // NTR
    devices = lax.axis_size("lon")
    parts = devices // (NTR // PAIR)
    count = rows // parts
    lane = cells * PAIR

    def src_at(ref, peer, part):
        return ref.at[part, pl.ds((peer % parts) * count, count), pl.ds((peer // parts) * lane, lane)]

    def dst_at(ref, sender, part):
        return ref.at[part, :, pl.ds(sender * lane, lane)]

    vmem = pl.BlockSpec(memory_space=pltpu.VMEM)
    field_shape = (levels, count, devices * lane)
    below_shape = (levels, 2, devices * lane)
    above_shape = (levels, 3, devices * lane)
    padded_shape = (levels, count + 6, devices * lane)
    return pl.pallas_call(
        functools.partial(entry_kernel, src_at=src_at, dst_at=dst_at, parts=parts),
        out_shape=jax.ShapeDtypeStruct(padded_shape, block.dtype),
        in_specs=[vmem, vmem],
        out_specs=vmem,
        scratch_shapes=[
            pltpu.VMEM(block.shape, block.dtype),
            pltpu.VMEM(field_shape, block.dtype),
            pltpu.VMEM(below_shape, block.dtype),
            pltpu.VMEM(above_shape, block.dtype),
            pltpu.VMEM(below_shape, block.dtype),
            pltpu.VMEM(above_shape, block.dtype),
            pltpu.SemaphoreType.DMA((CHUNKS, devices)),
            pltpu.SemaphoreType.DMA((CHUNKS, devices)),
            pltpu.SemaphoreType.DMA((CHUNKS,)),
            pltpu.SemaphoreType.DMA((2,)),
            pltpu.SemaphoreType.DMA((2,)),
        ],
        compiler_params=pltpu.CompilerParams(collective_id=0, has_side_effects=True),
    )(block, permutation(pair_order(cells), False))


def from_columns(field, rows):
    levels, count, width = field.shape
    devices = lax.axis_size("lon")
    parts = devices // (NTR // PAIR)
    lane = width // devices
    cells = lane // PAIR

    def src_at(ref, peer, part):
        return ref.at[part, :, pl.ds(peer * lane, lane)]

    def dst_at(ref, sender, part):
        return ref.at[part, pl.ds((sender % parts) * count, count), pl.ds((sender // parts) * lane, lane)]

    shape = (levels, rows, cells * NTR)
    return run_exchange(
        exit_kernel, field, permutation(pair_order(cells), True), shape,
        pl.BlockSpec(memory_space=pl.ANY), pl.BlockSpec(memory_space=pltpu.VMEM), shape,
        src_at, dst_at, 1,
    )


def lat_halo(field, width):
    lon_n = lax.axis_size("lon")
    lat_n = lax.axis_size("lat")
    parts = lon_n // (NTR // PAIR)
    up = []
    for b in range(lat_n):
        for l in range(lon_n):
            t, h = l // parts, l % parts
            g = b * parts + h
            if g + 1 < lat_n * parts:
                nb, nh = (g + 1) // parts, (g + 1) % parts
                up.append((l * lat_n + b, (t * parts + nh) * lat_n + nb))
    down = [(d, s) for s, d in up]
    rows = field.shape[1]
    below = lax.ppermute(field[:, rows - width + 1 :], ("lon", "lat"), up)
    above = lax.ppermute(field[:, :width], ("lon", "lat"), down)
    return jnp.concatenate([below[:, :1], below, field, above], axis=1)


def roll_rows(field, amount):
    cells = field.shape[2] // PAIR
    current = field
    for position in range(cells.bit_length() - 1):
        moved = jnp.roll(current, PAIR * 2**position, axis=2)
        current = jnp.where(bit_mask(amount, position), moved, current)
    return current


def lon_cubic(shifted, fraction):
    weights = cubic_weights(fraction)
    taps = [jnp.roll(shifted, PAIR * (1 - p), axis=2) for p in range(4)]
    summed = None
    for p in range(4):
        addend = weights[p][:, :, None] * taps[p]
        summed = addend if summed is None else summed + addend
    return summed


def own_rows(values, count):
    parts = lax.axis_size("lon") // (NTR // PAIR)
    start = (lax.axis_index("lon") % parts) * count
    return lax.dynamic_slice_in_dim(values, start, count, axis=values.ndim - 1)


def per_device(tracers, lon_shift, lon_frac, lat_shift, lat_frac, remap_frac, diffusivity):
    rows = tracers.shape[1]
    first = to_columns(tracers)
    count = first.shape[1] - 6
    width = first.shape[2]
    lon_shift, lon_frac, lat_shift, lat_frac, remap_frac, diffusivity = (
        own_rows(v, count) for v in (lon_shift, lon_frac, lat_shift, lat_frac, remap_frac, diffusivity)
    )
    for time_step in range(STEPS):
        if time_step == 0:
            padded = first
        else:
            padded = lat_halo(field, 3)
        field = lat_step(padded, lat_shift[time_step], lat_frac[time_step], count)
        amount = jnp.remainder(lon_shift[time_step], width // PAIR)
        field = lon_cubic(roll_rows(field, amount), lon_frac[time_step])
        field = remap(field, remap_frac[time_step])
        field = diffuse(field, diffusivity)
    return from_columns(field, rows)


def solution(mesh):
    in_specs = (
        P(None, "lat", "lon"),
        P(None, None, "lat"),
        P(None, None, "lat"),
        P(None, None, "lat"),
        P(None, None, "lat"),
        P(None, None, "lat"),
        P(None, "lat"),
    )
    out_specs = P(None, "lat", "lon")
    return jax.shard_map(
        per_device, mesh=mesh, in_specs=in_specs, out_specs=out_specs, check_vma=False
    )
```

```python
import functools

import jax
import jax.numpy as jnp
from jax import lax
from jax.experimental import pallas as pl
from jax.experimental.pallas import tpu as pltpu
from jax.sharding import PartitionSpec as P

NTR = 8
STEPS = 2


def from_behind(x, axis, by):
    peers = lax.axis_size(axis)
    return lax.ppermute(x, axis, [(i, (i + by) % peers) for i in range(peers)])


def with_halo(block, sides, width, periodic):
    for axis, dim in sides:
        count = lax.axis_size(axis)
        forward = [(i, i + 1) for i in range(count - 1)]
        if periodic:
            forward.append((count - 1, 0))
        backward = [(target, source) for source, target in forward]
        low = lax.ppermute(
            lax.slice_in_dim(block, block.shape[dim] - width, None, axis=dim), axis, forward
        )
        high = lax.ppermute(lax.slice_in_dim(block, 0, width, axis=dim), axis, backward)
        block = jnp.concatenate([low, block, high], axis=dim)
    return block


def cubic_weights(fraction):
    w_zero = -fraction * (fraction - 1.0) * (fraction - 2.0) / 6.0
    w_one = (fraction + 1.0) * (fraction - 1.0) * (fraction - 2.0) / 2.0
    w_two = -(fraction + 1.0) * fraction * (fraction - 2.0) / 2.0
    w_three = (fraction + 1.0) * fraction * (fraction - 1.0) / 6.0
    return (w_zero, w_one, w_two, w_three)


def lat_step(padded, offset, fraction, row_count):
    weights = cubic_weights(fraction)
    summed = None
    for place_index in range(6):
        row_delta = place_index - 2
        coeff = jnp.zeros_like(fraction)
        for tap_index in range(4):
            coeff = coeff + jnp.where(offset == tap_index - 1 - row_delta, weights[tap_index], 0.0)
        addend = coeff[:, :, None] * padded[:, 1 + place_index : 1 + place_index + row_count, :]
        summed = addend if summed is None else summed + addend
    return summed


def lon_step(wrapped, fraction, tracer_count):
    weights = cubic_weights(fraction)
    width_cols = wrapped.shape[2] - 4 * tracer_count
    summed = None
    for tap_index in range(4):
        offset_cols = (1 + tap_index) * tracer_count
        addend = (
            weights[tap_index][:, :, None] * wrapped[:, :, offset_cols : offset_cols + width_cols]
        )
        summed = addend if summed is None else summed + addend
    return summed


def remap(tracer_field, fraction):
    level_above = jnp.concatenate([tracer_field[1:], tracer_field[-1:]], axis=0)
    return (1.0 - fraction)[:, :, None] * tracer_field + fraction[:, :, None] * level_above


def diffuse(tracer_field, kappa):
    levels = tracer_field.shape[0]
    face_kappa = 0.5 * (kappa[:-1] + kappa[1:])
    zero_face = jnp.zeros_like(kappa[:1])
    face_below = jnp.concatenate([zero_face, face_kappa], axis=0)
    face_above = jnp.concatenate([face_kappa, zero_face], axis=0)
    ratio_prev = jnp.zeros_like(kappa[0])
    solved_prev = jnp.zeros_like(tracer_field[0])
    ratios = []
    solveds = []
    for level_index in range(levels):
        below = face_below[level_index]
        above = face_above[level_index]
        pivot_value = 1.0 + below + above + below * ratio_prev
        ratio_now = -above / pivot_value
        solved_now = (tracer_field[level_index] + below[:, None] * solved_prev) / pivot_value[
            :, None
        ]
        ratios.append(ratio_now)
        solveds.append(solved_now)
        ratio_prev = ratio_now
        solved_prev = solved_now
    results = [None] * levels
    results[levels - 1] = solveds[levels - 1]
    for level_index in range(levels - 2, -1, -1):
        results[level_index] = (
            solveds[level_index] - ratios[level_index][:, None] * results[level_index + 1]
        )
    return jnp.stack(results, axis=0)


def bit_mask(amount, position):
    return (amount // 2**position % 2 == 1)[:, :, None]


PAIR = 2


def pair_order(cells):
    cols = jnp.arange(cells * NTR)
    cell, tracer = cols // NTR, cols % NTR
    target = (tracer // PAIR) * cells * PAIR + cell * PAIR + tracer % PAIR
    return target


def permutation(target, inverse):
    cols = jnp.arange(target.shape[0])
    if inverse:
        matrix = cols[:, None] == target[None, :]
    else:
        matrix = cols[None, :] == target[:, None]
    return matrix.astype(jnp.bfloat16)


def permute_block(block, matrix):
    high = block.astype(jnp.bfloat16)
    rest = block - high.astype(jnp.float32)
    middle = rest.astype(jnp.bfloat16)
    low = (rest - middle.astype(jnp.float32)).astype(jnp.bfloat16)
    total = jnp.dot(high, matrix, preferred_element_type=jnp.float32)
    total = total + jnp.dot(middle, matrix, preferred_element_type=jnp.float32)
    return total + jnp.dot(low, matrix, preferred_element_type=jnp.float32)


CHUNKS = 4
MESH_ID = pl.DeviceIdType.MESH


def greet(count, me, lat):
    barrier = pltpu.get_barrier_semaphore()
    for offset in range(1, count):
        peer = lax.rem(me + offset, count)
        pl.semaphore_signal(barrier, 1, device_id=(peer, lat), device_id_type=MESH_ID)
    return barrier


def neighbours(parts):
    lon = lax.axis_index("lon")
    lat = lax.axis_index("lat")
    bands = lax.axis_size("lat")
    quarter = lon % parts
    inside_up = quarter < parts - 1
    inside_down = quarter > 0
    has_up = jnp.logical_or(inside_up, lat < bands - 1)
    has_down = jnp.logical_or(inside_down, lat > 0)
    up = (jnp.where(inside_up, lon + 1, lon + 1 - parts), jnp.where(inside_up, lat, lat + 1))
    down = (jnp.where(inside_down, lon - 1, lon + parts - 1), jnp.where(inside_down, lat, lat - 1))
    return has_up, up, has_down, down


def entry_kernel(x_ref, matrix_ref, field_ref, below_ref, above_ref, moved, landed, top_stage, bottom_stage,
                 zero_low, zero_high, send_sem, recv_sem, local_sem, halo_send, halo_recv, store_sem,
                 *, src_at, dst_at, parts):
    count = lax.axis_size("lon")
    me = lax.axis_index("lon")
    lat = lax.axis_index("lat")
    levels = x_ref.shape[0]
    rows = landed.shape[1]
    per = levels // CHUNKS
    has_up, up, has_down, down = neighbours(parts)
    barrier = greet(count, me, lat)

    @pl.when(has_up)
    def _():
        pl.semaphore_signal(barrier, 1, device_id=up, device_id_type=MESH_ID)

    @pl.when(has_down)
    def _():
        pl.semaphore_signal(barrier, 1, device_id=down, device_id_type=MESH_ID)

    copies = []
    locals_ = []
    for chunk in range(CHUNKS):
        def body(k, carry):
            moved[k] = permute_block(x_ref[k], matrix_ref[...])
            return carry

        lax.fori_loop(chunk * per, (chunk + 1) * per, body, 0)
        if chunk == 0:
            pl.semaphore_wait(barrier, count - 1 + has_up.astype(jnp.int32) + has_down.astype(jnp.int32))
        part = pl.ds(chunk * per, per)
        for offset in range(1, count):
            peer = lax.rem(me + offset, count)
            copy = pltpu.make_async_remote_copy(
                src_ref=src_at(moved, peer, part),
                dst_ref=dst_at(landed, me, part),
                send_sem=send_sem.at[chunk, offset],
                recv_sem=recv_sem.at[chunk, offset],
                device_id=(peer, lat),
                device_id_type=MESH_ID,
            )
            copy.start()
            copies.append(copy)
        local = pltpu.make_async_copy(src_at(moved, me, part), dst_at(landed, me, part), local_sem.at[chunk])
        local.start()
        locals_.append(local)
    for copy in copies:
        copy.wait_recv()
    for local in locals_:
        local.wait()
    top_stage[...] = landed[:, rows - top_stage.shape[1] :, :]
    bottom_stage[...] = landed[:, : bottom_stage.shape[1], :]
    to_up = pltpu.make_async_remote_copy(
        src_ref=top_stage, dst_ref=below_ref, send_sem=halo_send.at[0], recv_sem=halo_recv.at[0],
        device_id=up, device_id_type=MESH_ID,
    )
    to_down = pltpu.make_async_remote_copy(
        src_ref=bottom_stage, dst_ref=above_ref, send_sem=halo_send.at[1], recv_sem=halo_recv.at[1],
        device_id=down, device_id_type=MESH_ID,
    )

    @pl.when(has_up)
    def _():
        to_up.start()

    @pl.when(has_down)
    def _():
        to_down.start()

    store = pltpu.make_async_copy(landed, field_ref, store_sem.at[0])
    store.start()
    fill_low = pltpu.make_async_copy(zero_low, below_ref, store_sem.at[1])
    fill_high = pltpu.make_async_copy(zero_high, above_ref, store_sem.at[2])

    @pl.when(jnp.logical_not(has_down))
    def _():
        zero_low[...] = jnp.zeros(zero_low.shape, zero_low.dtype)
        fill_low.start()
        fill_low.wait()

    @pl.when(jnp.logical_not(has_up))
    def _():
        zero_high[...] = jnp.zeros(zero_high.shape, zero_high.dtype)
        fill_high.start()
        fill_high.wait()

    store.wait()

    for copy in copies:
        copy.wait_send()

    @pl.when(has_up)
    def _():
        to_up.wait_send()
        to_down.wait_recv()

    @pl.when(has_down)
    def _():
        to_down.wait_send()
        to_up.wait_recv()


def exit_kernel(src_ref, matrix_ref, out_ref, landed, send_sem, recv_sem, local_sem, *, src_at, dst_at):
    count = lax.axis_size("lon")
    me = lax.axis_index("lon")
    lat = lax.axis_index("lat")
    levels = out_ref.shape[0]
    per = levels // CHUNKS
    barrier = greet(count, me, lat)
    pl.semaphore_wait(barrier, count - 1)
    copies = []
    locals_ = []
    for chunk in range(CHUNKS):
        part = pl.ds(chunk * per, per)
        row = []
        for offset in range(1, count):
            peer = lax.rem(me + offset, count)
            copy = pltpu.make_async_remote_copy(
                src_ref=src_at(src_ref, peer, part),
                dst_ref=dst_at(landed, me, part),
                send_sem=send_sem.at[chunk, offset],
                recv_sem=recv_sem.at[chunk, offset],
                device_id=(peer, lat),
                device_id_type=MESH_ID,
            )
            copy.start()
            row.append(copy)
        copies.append(row)
        local = pltpu.make_async_copy(src_at(src_ref, me, part), dst_at(landed, me, part), local_sem.at[chunk])
        local.start()
        locals_.append(local)
    for chunk in range(CHUNKS):
        for copy in copies[chunk]:
            copy.wait_recv()
        locals_[chunk].wait()

        def body(k, carry):
            out_ref[k] = permute_block(landed[k], matrix_ref[...])
            return carry

        lax.fori_loop(chunk * per, (chunk + 1) * per, body, 0)
    for row in copies:
        for copy in row:
            copy.wait_send()


def run_exchange(kernel, operand, matrix, out_shape, src_spec, out_spec, scratch, src_at, dst_at, ident):
    count = lax.axis_size("lon")
    return pl.pallas_call(
        functools.partial(kernel, src_at=src_at, dst_at=dst_at),
        out_shape=jax.ShapeDtypeStruct(out_shape, operand.dtype),
        in_specs=[src_spec, pl.BlockSpec(memory_space=pltpu.VMEM)],
        out_specs=out_spec,
        scratch_shapes=[
            pltpu.VMEM(scratch, operand.dtype),
            pltpu.SemaphoreType.DMA((CHUNKS, count)),
            pltpu.SemaphoreType.DMA((CHUNKS, count)),
            pltpu.SemaphoreType.DMA((CHUNKS,)),
        ],
        compiler_params=pltpu.CompilerParams(collective_id=ident, has_side_effects=True),
    )(operand, matrix)


def to_columns(block):
    levels, rows, width = block.shape
    cells = width // NTR
    devices = lax.axis_size("lon")
    parts = devices // (NTR // PAIR)
    count = rows // parts
    lane = cells * PAIR

    def src_at(ref, peer, part):
        return ref.at[part, pl.ds((peer % parts) * count, count), pl.ds((peer // parts) * lane, lane)]

    def dst_at(ref, sender, part):
        return ref.at[part, :, pl.ds(sender * lane, lane)]

    vmem = pl.BlockSpec(memory_space=pltpu.VMEM)
    hbm = pl.BlockSpec(memory_space=pl.ANY)
    field_shape = (levels, count, devices * lane)
    below_shape = (levels, 2, devices * lane)
    above_shape = (levels, 3, devices * lane)
    return pl.pallas_call(
        functools.partial(entry_kernel, src_at=src_at, dst_at=dst_at, parts=parts),
        out_shape=tuple(jax.ShapeDtypeStruct(shape, block.dtype) for shape in (field_shape, below_shape, above_shape)),
        in_specs=[vmem, vmem],
        out_specs=(hbm, hbm, hbm),
        scratch_shapes=[
            pltpu.VMEM(block.shape, block.dtype),
            pltpu.VMEM(field_shape, block.dtype),
            pltpu.VMEM(below_shape, block.dtype),
            pltpu.VMEM(above_shape, block.dtype),
            pltpu.VMEM(below_shape, block.dtype),
            pltpu.VMEM(above_shape, block.dtype),
            pltpu.SemaphoreType.DMA((CHUNKS, devices)),
            pltpu.SemaphoreType.DMA((CHUNKS, devices)),
            pltpu.SemaphoreType.DMA((CHUNKS,)),
            pltpu.SemaphoreType.DMA((2,)),
            pltpu.SemaphoreType.DMA((2,)),
            pltpu.SemaphoreType.DMA((3,)),
        ],
        compiler_params=pltpu.CompilerParams(collective_id=0, has_side_effects=True),
    )(block, permutation(pair_order(cells), False))


def from_columns(field, rows):
    levels, count, width = field.shape
    devices = lax.axis_size("lon")
    parts = devices // (NTR // PAIR)
    lane = width // devices
    cells = lane // PAIR

    def src_at(ref, peer, part):
        return ref.at[part, :, pl.ds(peer * lane, lane)]

    def dst_at(ref, sender, part):
        return ref.at[part, pl.ds((sender % parts) * count, count), pl.ds((sender // parts) * lane, lane)]

    shape = (levels, rows, cells * NTR)
    return run_exchange(
        exit_kernel, field, permutation(pair_order(cells), True), shape,
        pl.BlockSpec(memory_space=pl.ANY), pl.BlockSpec(memory_space=pltpu.VMEM), shape,
        src_at, dst_at, 1,
    )


def lat_halo(field, width):
    lon_n = lax.axis_size("lon")
    lat_n = lax.axis_size("lat")
    parts = lon_n // (NTR // PAIR)
    up = []
    for b in range(lat_n):
        for l in range(lon_n):
            t, h = l // parts, l % parts
            g = b * parts + h
            if g + 1 < lat_n * parts:
                nb, nh = (g + 1) // parts, (g + 1) % parts
                up.append((l * lat_n + b, (t * parts + nh) * lat_n + nb))
    down = [(d, s) for s, d in up]
    rows = field.shape[1]
    below = lax.ppermute(field[:, rows - width + 1 :], ("lon", "lat"), up)
    above = lax.ppermute(field[:, :width], ("lon", "lat"), down)
    return jnp.concatenate([below[:, :1], below, field, above], axis=1)


def roll_rows(field, amount):
    cells = field.shape[2] // PAIR
    current = field
    for position in range(cells.bit_length() - 1):
        moved = jnp.roll(current, PAIR * 2**position, axis=2)
        current = jnp.where(bit_mask(amount, position), moved, current)
    return current


def lon_cubic(shifted, fraction):
    weights = cubic_weights(fraction)
    taps = [jnp.roll(shifted, PAIR * (1 - p), axis=2) for p in range(4)]
    summed = None
    for p in range(4):
        addend = weights[p][:, :, None] * taps[p]
        summed = addend if summed is None else summed + addend
    return summed


def own_rows(values, count):
    parts = lax.axis_size("lon") // (NTR // PAIR)
    start = (lax.axis_index("lon") % parts) * count
    return lax.dynamic_slice_in_dim(values, start, count, axis=values.ndim - 1)


def per_device(tracers, lon_shift, lon_frac, lat_shift, lat_frac, remap_frac, diffusivity):
    rows = tracers.shape[1]
    field, below, above = to_columns(tracers)
    count = field.shape[1]
    width = field.shape[2]
    lon_shift, lon_frac, lat_shift, lat_frac, remap_frac, diffusivity = (
        own_rows(v, count) for v in (lon_shift, lon_frac, lat_shift, lat_frac, remap_frac, diffusivity)
    )
    for time_step in range(STEPS):
        if time_step == 0:
            padded = jnp.concatenate([below[:, :1], below, field, above], axis=1)
        else:
            padded = lat_halo(field, 3)
        field = lat_step(padded, lat_shift[time_step], lat_frac[time_step], count)
        amount = jnp.remainder(lon_shift[time_step], width // PAIR)
        field = lon_cubic(roll_rows(field, amount), lon_frac[time_step])
        field = remap(field, remap_frac[time_step])
        field = diffuse(field, diffusivity)
    return from_columns(field, rows)


def solution(mesh):
    in_specs = (
        P(None, "lat", "lon"),
        P(None, None, "lat"),
        P(None, None, "lat"),
        P(None, None, "lat"),
        P(None, None, "lat"),
        P(None, None, "lat"),
        P(None, "lat"),
    )
    out_specs = P(None, "lat", "lon")
    return jax.shard_map(
        per_device, mesh=mesh, in_specs=in_specs, out_specs=out_specs, check_vma=False
    )
```

```python
import functools

import jax
import jax.numpy as jnp
from jax import lax
from jax.experimental import pallas as pl
from jax.experimental.pallas import tpu as pltpu
from jax.sharding import PartitionSpec as P

NTR = 8
STEPS = 2


def from_behind(x, axis, by):
    peers = lax.axis_size(axis)
    return lax.ppermute(x, axis, [(i, (i + by) % peers) for i in range(peers)])


def with_halo(block, sides, width, periodic):
    for axis, dim in sides:
        count = lax.axis_size(axis)
        forward = [(i, i + 1) for i in range(count - 1)]
        if periodic:
            forward.append((count - 1, 0))
        backward = [(target, source) for source, target in forward]
        low = lax.ppermute(
            lax.slice_in_dim(block, block.shape[dim] - width, None, axis=dim), axis, forward
        )
        high = lax.ppermute(lax.slice_in_dim(block, 0, width, axis=dim), axis, backward)
        block = jnp.concatenate([low, block, high], axis=dim)
    return block


def cubic_weights(fraction):
    w_zero = -fraction * (fraction - 1.0) * (fraction - 2.0) / 6.0
    w_one = (fraction + 1.0) * (fraction - 1.0) * (fraction - 2.0) / 2.0
    w_two = -(fraction + 1.0) * fraction * (fraction - 2.0) / 2.0
    w_three = (fraction + 1.0) * fraction * (fraction - 1.0) / 6.0
    return (w_zero, w_one, w_two, w_three)


def lat_step(padded, offset, fraction, row_count):
    weights = cubic_weights(fraction)
    summed = None
    for place_index in range(6):
        row_delta = place_index - 2
        coeff = jnp.zeros_like(fraction)
        for tap_index in range(4):
            coeff = coeff + jnp.where(offset == tap_index - 1 - row_delta, weights[tap_index], 0.0)
        addend = coeff[:, :, None] * padded[:, 1 + place_index : 1 + place_index + row_count, :]
        summed = addend if summed is None else summed + addend
    return summed


def lon_step(wrapped, fraction, tracer_count):
    weights = cubic_weights(fraction)
    width_cols = wrapped.shape[2] - 4 * tracer_count
    summed = None
    for tap_index in range(4):
        offset_cols = (1 + tap_index) * tracer_count
        addend = (
            weights[tap_index][:, :, None] * wrapped[:, :, offset_cols : offset_cols + width_cols]
        )
        summed = addend if summed is None else summed + addend
    return summed


def remap(tracer_field, fraction):
    level_above = jnp.concatenate([tracer_field[1:], tracer_field[-1:]], axis=0)
    return (1.0 - fraction)[:, :, None] * tracer_field + fraction[:, :, None] * level_above


def diffuse(tracer_field, kappa):
    levels = tracer_field.shape[0]
    face_kappa = 0.5 * (kappa[:-1] + kappa[1:])
    zero_face = jnp.zeros_like(kappa[:1])
    face_below = jnp.concatenate([zero_face, face_kappa], axis=0)
    face_above = jnp.concatenate([face_kappa, zero_face], axis=0)
    ratio_prev = jnp.zeros_like(kappa[0])
    solved_prev = jnp.zeros_like(tracer_field[0])
    ratios = []
    solveds = []
    for level_index in range(levels):
        below = face_below[level_index]
        above = face_above[level_index]
        pivot_value = 1.0 + below + above + below * ratio_prev
        ratio_now = -above / pivot_value
        solved_now = (tracer_field[level_index] + below[:, None] * solved_prev) / pivot_value[
            :, None
        ]
        ratios.append(ratio_now)
        solveds.append(solved_now)
        ratio_prev = ratio_now
        solved_prev = solved_now
    results = [None] * levels
    results[levels - 1] = solveds[levels - 1]
    for level_index in range(levels - 2, -1, -1):
        results[level_index] = (
            solveds[level_index] - ratios[level_index][:, None] * results[level_index + 1]
        )
    return jnp.stack(results, axis=0)


def bit_mask(amount, position):
    return (amount // 2**position % 2 == 1)[:, :, None]


PAIR = 2


def pair_order(cells):
    cols = jnp.arange(cells * NTR)
    cell, tracer = cols // NTR, cols % NTR
    target = (tracer // PAIR) * cells * PAIR + cell * PAIR + tracer % PAIR
    return target


def permutation(target, inverse):
    cols = jnp.arange(target.shape[0])
    if inverse:
        matrix = cols[:, None] == target[None, :]
    else:
        matrix = cols[None, :] == target[:, None]
    return matrix.astype(jnp.bfloat16)


def permute_block(block, matrix):
    high = block.astype(jnp.bfloat16)
    rest = block - high.astype(jnp.float32)
    middle = rest.astype(jnp.bfloat16)
    low = (rest - middle.astype(jnp.float32)).astype(jnp.bfloat16)
    total = jnp.dot(high, matrix, preferred_element_type=jnp.float32)
    total = total + jnp.dot(middle, matrix, preferred_element_type=jnp.float32)
    return total + jnp.dot(low, matrix, preferred_element_type=jnp.float32)


CHUNKS = 4
MESH_ID = pl.DeviceIdType.MESH


def greet(count, me, lat):
    barrier = pltpu.get_barrier_semaphore()
    for offset in range(1, count):
        peer = lax.rem(me + offset, count)
        pl.semaphore_signal(barrier, 1, device_id=(peer, lat), device_id_type=MESH_ID)
    return barrier


def neighbours(parts):
    lon = lax.axis_index("lon")
    lat = lax.axis_index("lat")
    bands = lax.axis_size("lat")
    quarter = lon % parts
    inside_up = quarter < parts - 1
    inside_down = quarter > 0
    has_up = jnp.logical_or(inside_up, lat < bands - 1)
    has_down = jnp.logical_or(inside_down, lat > 0)
    up = (jnp.where(inside_up, lon + 1, lon + 1 - parts), jnp.where(inside_up, lat, lat + 1))
    down = (jnp.where(inside_down, lon - 1, lon + parts - 1), jnp.where(inside_down, lat, lat - 1))
    return has_up, up, has_down, down


def entry_kernel(x_ref, matrix_ref, field_ref, below_ref, above_ref, moved, landed, top_stage, bottom_stage,
                 zero_low, zero_high, send_sem, recv_sem, local_sem, halo_send, halo_recv, store_sem,
                 *, src_at, dst_at, parts):
    count = lax.axis_size("lon")
    me = lax.axis_index("lon")
    lat = lax.axis_index("lat")
    levels = x_ref.shape[0]
    rows = landed.shape[1]
    per = levels // CHUNKS
    has_up, up, has_down, down = neighbours(parts)
    barrier = greet(count, me, lat)

    @pl.when(has_up)
    def _():
        pl.semaphore_signal(barrier, 1, device_id=up, device_id_type=MESH_ID)

    @pl.when(has_down)
    def _():
        pl.semaphore_signal(barrier, 1, device_id=down, device_id_type=MESH_ID)

    copies = []
    locals_ = []
    for chunk in range(CHUNKS):
        def body(k, carry):
            moved[k] = permute_block(x_ref[k], matrix_ref[...])
            return carry

        lax.fori_loop(chunk * per, (chunk + 1) * per, body, 0)
        if chunk == 0:
            pl.semaphore_wait(barrier, count - 1 + has_up.astype(jnp.int32) + has_down.astype(jnp.int32))
        part = pl.ds(chunk * per, per)
        for offset in range(1, count):
            peer = lax.rem(me + offset, count)
            copy = pltpu.make_async_remote_copy(
                src_ref=src_at(moved, peer, part),
                dst_ref=dst_at(landed, me, part),
                send_sem=send_sem.at[chunk, offset],
                recv_sem=recv_sem.at[chunk, offset],
                device_id=(peer, lat),
                device_id_type=MESH_ID,
            )
            copy.start()
            copies.append(copy)
        local = pltpu.make_async_copy(src_at(moved, me, part), dst_at(landed, me, part), local_sem.at[chunk])
        local.start()
        locals_.append(local)
    for copy in copies:
        copy.wait_recv()
    for local in locals_:
        local.wait()
    top_stage[...] = landed[:, rows - top_stage.shape[1] :, :]
    bottom_stage[...] = landed[:, : bottom_stage.shape[1], :]
    to_up = pltpu.make_async_remote_copy(
        src_ref=top_stage, dst_ref=below_ref, send_sem=halo_send.at[0], recv_sem=halo_recv.at[0],
        device_id=up, device_id_type=MESH_ID,
    )
    to_down = pltpu.make_async_remote_copy(
        src_ref=bottom_stage, dst_ref=above_ref, send_sem=halo_send.at[1], recv_sem=halo_recv.at[1],
        device_id=down, device_id_type=MESH_ID,
    )

    @pl.when(has_up)
    def _():
        to_up.start()

    @pl.when(has_down)
    def _():
        to_down.start()

    store = pltpu.make_async_copy(landed, field_ref, store_sem.at[0])
    store.start()
    fill_low = pltpu.make_async_copy(zero_low, below_ref, store_sem.at[1])
    fill_high = pltpu.make_async_copy(zero_high, above_ref, store_sem.at[2])

    @pl.when(jnp.logical_not(has_down))
    def _():
        zero_low[...] = jnp.zeros(zero_low.shape, zero_low.dtype)
        fill_low.start()
        fill_low.wait()

    @pl.when(jnp.logical_not(has_up))
    def _():
        zero_high[...] = jnp.zeros(zero_high.shape, zero_high.dtype)
        fill_high.start()
        fill_high.wait()

    store.wait()

    for copy in copies:
        copy.wait_send()

    @pl.when(has_up)
    def _():
        to_up.wait_send()
        to_down.wait_recv()

    @pl.when(has_down)
    def _():
        to_down.wait_send()
        to_up.wait_recv()


def exit_kernel(src_ref, out_ref, landed, send_sem, recv_sem, local_sem, *, src_at, dst_at):
    count = lax.axis_size("lon")
    me = lax.axis_index("lon")
    lat = lax.axis_index("lat")
    levels = out_ref.shape[0]
    per = levels // CHUNKS
    barrier = greet(count, me, lat)
    pl.semaphore_wait(barrier, count - 1)
    copies = []
    locals_ = []
    for chunk in range(CHUNKS):
        part = pl.ds(chunk * per, per)
        row = []
        for offset in range(1, count):
            peer = lax.rem(me + offset, count)
            copy = pltpu.make_async_remote_copy(
                src_ref=src_at(src_ref, peer, part),
                dst_ref=dst_at(landed, me, part),
                send_sem=send_sem.at[chunk, offset],
                recv_sem=recv_sem.at[chunk, offset],
                device_id=(peer, lat),
                device_id_type=MESH_ID,
            )
            copy.start()
            row.append(copy)
        copies.append(row)
        local = pltpu.make_async_copy(src_at(src_ref, me, part), dst_at(landed, me, part), local_sem.at[chunk])
        local.start()
        locals_.append(local)
    for chunk in range(CHUNKS):
        for copy in copies[chunk]:
            copy.wait_recv()
        locals_[chunk].wait()
        part = pl.ds(chunk * per, per)
        out_ref[part] = landed[part]
    for row in copies:
        for copy in row:
            copy.wait_send()


def unpermute_kernel(landed_ref, matrix_ref, out_ref, result, store_sem):
    levels = landed_ref.shape[0]
    per = levels // CHUNKS
    stores = []
    for chunk in range(CHUNKS):
        def body(k, carry):
            result[k] = permute_block(landed_ref[k], matrix_ref[...])
            return carry

        lax.fori_loop(chunk * per, (chunk + 1) * per, body, 0)
        part = pl.ds(chunk * per, per)
        store = pltpu.make_async_copy(result.at[part], out_ref.at[part], store_sem.at[chunk])
        store.start()
        stores.append(store)
    for store in stores:
        store.wait()


def run_exchange(kernel, operand, matrix, out_shape, src_spec, out_spec, scratch, src_at, dst_at, ident):
    count = lax.axis_size("lon")
    return pl.pallas_call(
        functools.partial(kernel, src_at=src_at, dst_at=dst_at),
        out_shape=jax.ShapeDtypeStruct(out_shape, operand.dtype),
        in_specs=[src_spec, pl.BlockSpec(memory_space=pltpu.VMEM)],
        out_specs=out_spec,
        scratch_shapes=[
            pltpu.VMEM(scratch, operand.dtype),
            pltpu.SemaphoreType.DMA((CHUNKS, count)),
            pltpu.SemaphoreType.DMA((CHUNKS, count)),
            pltpu.SemaphoreType.DMA((CHUNKS,)),
        ],
        compiler_params=pltpu.CompilerParams(collective_id=ident, has_side_effects=True),
    )(operand, matrix)


def to_columns(block):
    levels, rows, width = block.shape
    cells = width // NTR
    devices = lax.axis_size("lon")
    parts = devices // (NTR // PAIR)
    count = rows // parts
    lane = cells * PAIR

    def src_at(ref, peer, part):
        return ref.at[part, pl.ds((peer % parts) * count, count), pl.ds((peer // parts) * lane, lane)]

    def dst_at(ref, sender, part):
        return ref.at[part, :, pl.ds(sender * lane, lane)]

    vmem = pl.BlockSpec(memory_space=pltpu.VMEM)
    hbm = pl.BlockSpec(memory_space=pl.ANY)
    field_shape = (levels, count, devices * lane)
    below_shape = (levels, 2, devices * lane)
    above_shape = (levels, 3, devices * lane)
    return pl.pallas_call(
        functools.partial(entry_kernel, src_at=src_at, dst_at=dst_at, parts=parts),
        out_shape=tuple(jax.ShapeDtypeStruct(shape, block.dtype) for shape in (field_shape, below_shape, above_shape)),
        in_specs=[vmem, vmem],
        out_specs=(hbm, hbm, hbm),
        scratch_shapes=[
            pltpu.VMEM(block.shape, block.dtype),
            pltpu.VMEM(field_shape, block.dtype),
            pltpu.VMEM(below_shape, block.dtype),
            pltpu.VMEM(above_shape, block.dtype),
            pltpu.VMEM(below_shape, block.dtype),
            pltpu.VMEM(above_shape, block.dtype),
            pltpu.SemaphoreType.DMA((CHUNKS, devices)),
            pltpu.SemaphoreType.DMA((CHUNKS, devices)),
            pltpu.SemaphoreType.DMA((CHUNKS,)),
            pltpu.SemaphoreType.DMA((2,)),
            pltpu.SemaphoreType.DMA((2,)),
            pltpu.SemaphoreType.DMA((3,)),
        ],
        compiler_params=pltpu.CompilerParams(collective_id=0, has_side_effects=True),
    )(block, permutation(pair_order(cells), False))


def from_columns(field, rows):
    levels, count, width = field.shape
    devices = lax.axis_size("lon")
    parts = devices // (NTR // PAIR)
    lane = width // devices
    cells = lane // PAIR

    def src_at(ref, peer, part):
        return ref.at[part, :, pl.ds(peer * lane, lane)]

    def dst_at(ref, sender, part):
        return ref.at[part, pl.ds((sender % parts) * count, count), pl.ds((sender // parts) * lane, lane)]

    shape = (levels, rows, cells * NTR)
    vmem = pl.BlockSpec(memory_space=pltpu.VMEM)
    landed = pl.pallas_call(
        functools.partial(exit_kernel, src_at=src_at, dst_at=dst_at),
        out_shape=jax.ShapeDtypeStruct(shape, field.dtype),
        in_specs=[pl.BlockSpec(memory_space=pl.ANY)],
        out_specs=vmem,
        scratch_shapes=[
            pltpu.VMEM(shape, field.dtype),
            pltpu.SemaphoreType.DMA((CHUNKS, devices)),
            pltpu.SemaphoreType.DMA((CHUNKS, devices)),
            pltpu.SemaphoreType.DMA((CHUNKS,)),
        ],
        compiler_params=pltpu.CompilerParams(collective_id=1, has_side_effects=True),
    )(field)
    return pl.pallas_call(
        unpermute_kernel,
        out_shape=jax.ShapeDtypeStruct(shape, field.dtype),
        in_specs=[vmem, vmem],
        out_specs=pl.BlockSpec(memory_space=pl.ANY),
        scratch_shapes=[pltpu.VMEM(shape, field.dtype), pltpu.SemaphoreType.DMA((CHUNKS,))],
    )(landed, permutation(pair_order(cells), True))


def lat_halo(field, width):
    lon_n = lax.axis_size("lon")
    lat_n = lax.axis_size("lat")
    parts = lon_n // (NTR // PAIR)
    up = []
    for b in range(lat_n):
        for l in range(lon_n):
            t, h = l // parts, l % parts
            g = b * parts + h
            if g + 1 < lat_n * parts:
                nb, nh = (g + 1) // parts, (g + 1) % parts
                up.append((l * lat_n + b, (t * parts + nh) * lat_n + nb))
    down = [(d, s) for s, d in up]
    rows = field.shape[1]
    below = lax.ppermute(field[:, rows - width + 1 :], ("lon", "lat"), up)
    above = lax.ppermute(field[:, :width], ("lon", "lat"), down)
    return jnp.concatenate([below[:, :1], below, field, above], axis=1)


def roll_rows(field, amount):
    cells = field.shape[2] // PAIR
    current = field
    for position in range(cells.bit_length() - 1):
        moved = jnp.roll(current, PAIR * 2**position, axis=2)
        current = jnp.where(bit_mask(amount, position), moved, current)
    return current


def lon_cubic(shifted, fraction):
    weights = cubic_weights(fraction)
    taps = [jnp.roll(shifted, PAIR * (1 - p), axis=2) for p in range(4)]
    summed = None
    for p in range(4):
        addend = weights[p][:, :, None] * taps[p]
        summed = addend if summed is None else summed + addend
    return summed


def own_rows(values, count):
    parts = lax.axis_size("lon") // (NTR // PAIR)
    start = (lax.axis_index("lon") % parts) * count
    return lax.dynamic_slice_in_dim(values, start, count, axis=values.ndim - 1)


def per_device(tracers, lon_shift, lon_frac, lat_shift, lat_frac, remap_frac, diffusivity):
    rows = tracers.shape[1]
    field, below, above = to_columns(tracers)
    count = field.shape[1]
    width = field.shape[2]
    lon_shift, lon_frac, lat_shift, lat_frac, remap_frac, diffusivity = (
        own_rows(v, count) for v in (lon_shift, lon_frac, lat_shift, lat_frac, remap_frac, diffusivity)
    )
    for time_step in range(STEPS):
        if time_step == 0:
            padded = jnp.concatenate([below[:, :1], below, field, above], axis=1)
        else:
            padded = lat_halo(field, 3)
        field = lat_step(padded, lat_shift[time_step], lat_frac[time_step], count)
        amount = jnp.remainder(lon_shift[time_step], width // PAIR)
        field = lon_cubic(roll_rows(field, amount), lon_frac[time_step])
        field = remap(field, remap_frac[time_step])
        field = diffuse(field, diffusivity)
    return from_columns(field, rows)


def solution(mesh):
    in_specs = (
        P(None, "lat", "lon"),
        P(None, None, "lat"),
        P(None, None, "lat"),
        P(None, None, "lat"),
        P(None, None, "lat"),
        P(None, None, "lat"),
        P(None, "lat"),
    )
    out_specs = P(None, "lat", "lon")
    return jax.shard_map(
        per_device, mesh=mesh, in_specs=in_specs, out_specs=out_specs, check_vma=False
    )
```

```python
import functools

import jax
import jax.numpy as jnp
from jax import lax
from jax.experimental import pallas as pl
from jax.experimental.pallas import tpu as pltpu
from jax.sharding import PartitionSpec as P

NTR = 8
STEPS = 2


def from_behind(x, axis, by):
    peers = lax.axis_size(axis)
    return lax.ppermute(x, axis, [(i, (i + by) % peers) for i in range(peers)])


def with_halo(block, sides, width, periodic):
    for axis, dim in sides:
        count = lax.axis_size(axis)
        forward = [(i, i + 1) for i in range(count - 1)]
        if periodic:
            forward.append((count - 1, 0))
        backward = [(target, source) for source, target in forward]
        low = lax.ppermute(
            lax.slice_in_dim(block, block.shape[dim] - width, None, axis=dim), axis, forward
        )
        high = lax.ppermute(lax.slice_in_dim(block, 0, width, axis=dim), axis, backward)
        block = jnp.concatenate([low, block, high], axis=dim)
    return block


def cubic_weights(fraction):
    w_zero = -fraction * (fraction - 1.0) * (fraction - 2.0) / 6.0
    w_one = (fraction + 1.0) * (fraction - 1.0) * (fraction - 2.0) / 2.0
    w_two = -(fraction + 1.0) * fraction * (fraction - 2.0) / 2.0
    w_three = (fraction + 1.0) * fraction * (fraction - 1.0) / 6.0
    return (w_zero, w_one, w_two, w_three)


def lat_step(padded, offset, fraction, row_count):
    weights = cubic_weights(fraction)
    summed = None
    for place_index in range(6):
        row_delta = place_index - 2
        coeff = jnp.zeros_like(fraction)
        for tap_index in range(4):
            coeff = coeff + jnp.where(offset == tap_index - 1 - row_delta, weights[tap_index], 0.0)
        addend = coeff[:, :, None] * padded[:, 1 + place_index : 1 + place_index + row_count, :]
        summed = addend if summed is None else summed + addend
    return summed


def lat_pieces(below, field, above, offset, fraction):
    rows = field.shape[1]
    low = below.shape[1]
    weights = cubic_weights(fraction)
    summed = None
    for place_index in range(6):
        row_delta = place_index - 2
        coeff = jnp.zeros_like(fraction)
        for tap_index in range(4):
            coeff = coeff + jnp.where(offset == tap_index - 1 - row_delta, weights[tap_index], 0.0)
        start = place_index - low
        if start < 0:
            window = jnp.concatenate([below[:, low + start :], field[:, : rows + start]], axis=1)
        elif start > 0:
            window = jnp.concatenate([field[:, start:], above[:, :start]], axis=1)
        else:
            window = field
        addend = coeff[:, :, None] * window
        summed = addend if summed is None else summed + addend
    return summed


def lon_step(wrapped, fraction, tracer_count):
    weights = cubic_weights(fraction)
    width_cols = wrapped.shape[2] - 4 * tracer_count
    summed = None
    for tap_index in range(4):
        offset_cols = (1 + tap_index) * tracer_count
        addend = (
            weights[tap_index][:, :, None] * wrapped[:, :, offset_cols : offset_cols + width_cols]
        )
        summed = addend if summed is None else summed + addend
    return summed


def remap(tracer_field, fraction):
    level_above = jnp.concatenate([tracer_field[1:], tracer_field[-1:]], axis=0)
    return (1.0 - fraction)[:, :, None] * tracer_field + fraction[:, :, None] * level_above


def diffuse(tracer_field, kappa):
    levels = tracer_field.shape[0]
    face_kappa = 0.5 * (kappa[:-1] + kappa[1:])
    zero_face = jnp.zeros_like(kappa[:1])
    face_below = jnp.concatenate([zero_face, face_kappa], axis=0)
    face_above = jnp.concatenate([face_kappa, zero_face], axis=0)
    ratio_prev = jnp.zeros_like(kappa[0])
    solved_prev = jnp.zeros_like(tracer_field[0])
    ratios = []
    solveds = []
    for level_index in range(levels):
        below = face_below[level_index]
        above = face_above[level_index]
        pivot_value = 1.0 + below + above + below * ratio_prev
        ratio_now = -above / pivot_value
        solved_now = (tracer_field[level_index] + below[:, None] * solved_prev) / pivot_value[
            :, None
        ]
        ratios.append(ratio_now)
        solveds.append(solved_now)
        ratio_prev = ratio_now
        solved_prev = solved_now
    results = [None] * levels
    results[levels - 1] = solveds[levels - 1]
    for level_index in range(levels - 2, -1, -1):
        results[level_index] = (
            solveds[level_index] - ratios[level_index][:, None] * results[level_index + 1]
        )
    return jnp.stack(results, axis=0)


def bit_mask(amount, position):
    return (amount // 2**position % 2 == 1)[:, :, None]


PAIR = 2


def pair_order(cells):
    cols = jnp.arange(cells * NTR)
    cell, tracer = cols // NTR, cols % NTR
    target = (tracer // PAIR) * cells * PAIR + cell * PAIR + tracer % PAIR
    return target


def permutation(target, inverse):
    cols = jnp.arange(target.shape[0])
    if inverse:
        matrix = cols[:, None] == target[None, :]
    else:
        matrix = cols[None, :] == target[:, None]
    return matrix.astype(jnp.bfloat16)


def permute_block(block, matrix):
    high = block.astype(jnp.bfloat16)
    rest = block - high.astype(jnp.float32)
    middle = rest.astype(jnp.bfloat16)
    low = (rest - middle.astype(jnp.float32)).astype(jnp.bfloat16)
    total = jnp.dot(high, matrix, preferred_element_type=jnp.float32)
    total = total + jnp.dot(middle, matrix, preferred_element_type=jnp.float32)
    return total + jnp.dot(low, matrix, preferred_element_type=jnp.float32)


CHUNKS = 4
MESH_ID = pl.DeviceIdType.MESH


def greet(count, me, lat):
    barrier = pltpu.get_barrier_semaphore()
    for offset in range(1, count):
        peer = lax.rem(me + offset, count)
        pl.semaphore_signal(barrier, 1, device_id=(peer, lat), device_id_type=MESH_ID)
    return barrier


def neighbours(parts):
    lon = lax.axis_index("lon")
    lat = lax.axis_index("lat")
    bands = lax.axis_size("lat")
    quarter = lon % parts
    inside_up = quarter < parts - 1
    inside_down = quarter > 0
    has_up = jnp.logical_or(inside_up, lat < bands - 1)
    has_down = jnp.logical_or(inside_down, lat > 0)
    up = (jnp.where(inside_up, lon + 1, lon + 1 - parts), jnp.where(inside_up, lat, lat + 1))
    down = (jnp.where(inside_down, lon - 1, lon + parts - 1), jnp.where(inside_down, lat, lat - 1))
    return has_up, up, has_down, down


def entry_kernel(x_ref, matrix_ref, field_ref, below_ref, above_ref, moved, landed, top_stage, bottom_stage,
                 zero_low, zero_high, send_sem, recv_sem, local_sem, halo_send, halo_recv, store_sem,
                 *, src_at, dst_at, parts):
    count = lax.axis_size("lon")
    me = lax.axis_index("lon")
    lat = lax.axis_index("lat")
    levels = x_ref.shape[0]
    rows = landed.shape[1]
    per = levels // CHUNKS
    has_up, up, has_down, down = neighbours(parts)
    barrier = greet(count, me, lat)

    @pl.when(has_up)
    def _():
        pl.semaphore_signal(barrier, 1, device_id=up, device_id_type=MESH_ID)

    @pl.when(has_down)
    def _():
        pl.semaphore_signal(barrier, 1, device_id=down, device_id_type=MESH_ID)

    copies = []
    locals_ = []
    for chunk in range(CHUNKS):
        def body(k, carry):
            moved[k] = permute_block(x_ref[k], matrix_ref[...])
            return carry

        lax.fori_loop(chunk * per, (chunk + 1) * per, body, 0)
        if chunk == 0:
            pl.semaphore_wait(barrier, count - 1 + has_up.astype(jnp.int32) + has_down.astype(jnp.int32))
        part = pl.ds(chunk * per, per)
        for offset in range(1, count):
            peer = lax.rem(me + offset, count)
            copy = pltpu.make_async_remote_copy(
                src_ref=src_at(moved, peer, part),
                dst_ref=dst_at(landed, me, part),
                send_sem=send_sem.at[chunk, offset],
                recv_sem=recv_sem.at[chunk, offset],
                device_id=(peer, lat),
                device_id_type=MESH_ID,
            )
            copy.start()
            copies.append(copy)
        local = pltpu.make_async_copy(src_at(moved, me, part), dst_at(landed, me, part), local_sem.at[chunk])
        local.start()
        locals_.append(local)
    for copy in copies:
        copy.wait_recv()
    for local in locals_:
        local.wait()
    top_stage[...] = landed[:, rows - top_stage.shape[1] :, :]
    bottom_stage[...] = landed[:, : bottom_stage.shape[1], :]
    to_up = pltpu.make_async_remote_copy(
        src_ref=top_stage, dst_ref=below_ref, send_sem=halo_send.at[0], recv_sem=halo_recv.at[0],
        device_id=up, device_id_type=MESH_ID,
    )
    to_down = pltpu.make_async_remote_copy(
        src_ref=bottom_stage, dst_ref=above_ref, send_sem=halo_send.at[1], recv_sem=halo_recv.at[1],
        device_id=down, device_id_type=MESH_ID,
    )

    @pl.when(has_up)
    def _():
        to_up.start()

    @pl.when(has_down)
    def _():
        to_down.start()

    store = pltpu.make_async_copy(landed, field_ref, store_sem.at[0])
    store.start()
    fill_low = pltpu.make_async_copy(zero_low, below_ref, store_sem.at[1])
    fill_high = pltpu.make_async_copy(zero_high, above_ref, store_sem.at[2])

    @pl.when(jnp.logical_not(has_down))
    def _():
        zero_low[...] = jnp.zeros(zero_low.shape, zero_low.dtype)
        fill_low.start()
        fill_low.wait()

    @pl.when(jnp.logical_not(has_up))
    def _():
        zero_high[...] = jnp.zeros(zero_high.shape, zero_high.dtype)
        fill_high.start()
        fill_high.wait()

    store.wait()

    for copy in copies:
        copy.wait_send()

    @pl.when(has_up)
    def _():
        to_up.wait_send()
        to_down.wait_recv()

    @pl.when(has_down)
    def _():
        to_down.wait_send()
        to_up.wait_recv()


def exit_kernel(src_ref, matrix_ref, out_ref, landed, send_sem, recv_sem, local_sem, *, src_at, dst_at):
    count = lax.axis_size("lon")
    me = lax.axis_index("lon")
    lat = lax.axis_index("lat")
    levels = out_ref.shape[0]
    per = levels // CHUNKS
    barrier = greet(count, me, lat)
    pl.semaphore_wait(barrier, count - 1)
    copies = []
    locals_ = []
    for chunk in range(CHUNKS):
        part = pl.ds(chunk * per, per)
        row = []
        for offset in range(1, count):
            peer = lax.rem(me + offset, count)
            copy = pltpu.make_async_remote_copy(
                src_ref=src_at(src_ref, peer, part),
                dst_ref=dst_at(landed, me, part),
                send_sem=send_sem.at[chunk, offset],
                recv_sem=recv_sem.at[chunk, offset],
                device_id=(peer, lat),
                device_id_type=MESH_ID,
            )
            copy.start()
            row.append(copy)
        copies.append(row)
        local = pltpu.make_async_copy(src_at(src_ref, me, part), dst_at(landed, me, part), local_sem.at[chunk])
        local.start()
        locals_.append(local)
    for chunk in range(CHUNKS):
        for copy in copies[chunk]:
            copy.wait_recv()
        locals_[chunk].wait()

        def body(k, carry):
            out_ref[k] = permute_block(landed[k], matrix_ref[...])
            return carry

        lax.fori_loop(chunk * per, (chunk + 1) * per, body, 0)
    for row in copies:
        for copy in row:
            copy.wait_send()


def run_exchange(kernel, operand, matrix, out_shape, src_spec, out_spec, scratch, src_at, dst_at, ident):
    count = lax.axis_size("lon")
    return pl.pallas_call(
        functools.partial(kernel, src_at=src_at, dst_at=dst_at),
        out_shape=jax.ShapeDtypeStruct(out_shape, operand.dtype),
        in_specs=[src_spec, pl.BlockSpec(memory_space=pltpu.VMEM)],
        out_specs=out_spec,
        scratch_shapes=[
            pltpu.VMEM(scratch, operand.dtype),
            pltpu.SemaphoreType.DMA((CHUNKS, count)),
            pltpu.SemaphoreType.DMA((CHUNKS, count)),
            pltpu.SemaphoreType.DMA((CHUNKS,)),
        ],
        compiler_params=pltpu.CompilerParams(collective_id=ident, has_side_effects=True),
    )(operand, matrix)


def to_columns(block):
    levels, rows, width = block.shape
    cells = width // NTR
    devices = lax.axis_size("lon")
    parts = devices // (NTR // PAIR)
    count = rows // parts
    lane = cells * PAIR

    def src_at(ref, peer, part):
        return ref.at[part, pl.ds((peer % parts) * count, count), pl.ds((peer // parts) * lane, lane)]

    def dst_at(ref, sender, part):
        return ref.at[part, :, pl.ds(sender * lane, lane)]

    vmem = pl.BlockSpec(memory_space=pltpu.VMEM)
    hbm = pl.BlockSpec(memory_space=pl.ANY)
    field_shape = (levels, count, devices * lane)
    below_shape = (levels, 2, devices * lane)
    above_shape = (levels, 3, devices * lane)
    return pl.pallas_call(
        functools.partial(entry_kernel, src_at=src_at, dst_at=dst_at, parts=parts),
        out_shape=tuple(jax.ShapeDtypeStruct(shape, block.dtype) for shape in (field_shape, below_shape, above_shape)),
        in_specs=[vmem, vmem],
        out_specs=(hbm, hbm, hbm),
        scratch_shapes=[
            pltpu.VMEM(block.shape, block.dtype),
            pltpu.VMEM(field_shape, block.dtype),
            pltpu.VMEM(below_shape, block.dtype),
            pltpu.VMEM(above_shape, block.dtype),
            pltpu.VMEM(below_shape, block.dtype),
            pltpu.VMEM(above_shape, block.dtype),
            pltpu.SemaphoreType.DMA((CHUNKS, devices)),
            pltpu.SemaphoreType.DMA((CHUNKS, devices)),
            pltpu.SemaphoreType.DMA((CHUNKS,)),
            pltpu.SemaphoreType.DMA((2,)),
            pltpu.SemaphoreType.DMA((2,)),
            pltpu.SemaphoreType.DMA((3,)),
        ],
        compiler_params=pltpu.CompilerParams(collective_id=0, has_side_effects=True),
    )(block, permutation(pair_order(cells), False))


def from_columns(field, rows):
    levels, count, width = field.shape
    devices = lax.axis_size("lon")
    parts = devices // (NTR // PAIR)
    lane = width // devices
    cells = lane // PAIR

    def src_at(ref, peer, part):
        return ref.at[part, :, pl.ds(peer * lane, lane)]

    def dst_at(ref, sender, part):
        return ref.at[part, pl.ds((sender % parts) * count, count), pl.ds((sender // parts) * lane, lane)]

    shape = (levels, rows, cells * NTR)
    return run_exchange(
        exit_kernel, field, permutation(pair_order(cells), True), shape,
        pl.BlockSpec(memory_space=pl.ANY), pl.BlockSpec(memory_space=pltpu.VMEM), shape,
        src_at, dst_at, 1,
    )


def lat_halo(field, width):
    lon_n = lax.axis_size("lon")
    lat_n = lax.axis_size("lat")
    parts = lon_n // (NTR // PAIR)
    up = []
    for b in range(lat_n):
        for l in range(lon_n):
            t, h = l // parts, l % parts
            g = b * parts + h
            if g + 1 < lat_n * parts:
                nb, nh = (g + 1) // parts, (g + 1) % parts
                up.append((l * lat_n + b, (t * parts + nh) * lat_n + nb))
    down = [(d, s) for s, d in up]
    rows = field.shape[1]
    below = lax.ppermute(field[:, rows - width + 1 :], ("lon", "lat"), up)
    above = lax.ppermute(field[:, :width], ("lon", "lat"), down)
    return jnp.concatenate([below[:, :1], below, field, above], axis=1)


def roll_rows(field, amount):
    cells = field.shape[2] // PAIR
    current = field
    for position in range(cells.bit_length() - 1):
        moved = jnp.roll(current, PAIR * 2**position, axis=2)
        current = jnp.where(bit_mask(amount, position), moved, current)
    return current


def lon_cubic(shifted, fraction):
    weights = cubic_weights(fraction)
    taps = [jnp.roll(shifted, PAIR * (1 - p), axis=2) for p in range(4)]
    summed = None
    for p in range(4):
        addend = weights[p][:, :, None] * taps[p]
        summed = addend if summed is None else summed + addend
    return summed


def own_rows(values, count):
    parts = lax.axis_size("lon") // (NTR // PAIR)
    start = (lax.axis_index("lon") % parts) * count
    return lax.dynamic_slice_in_dim(values, start, count, axis=values.ndim - 1)


def per_device(tracers, lon_shift, lon_frac, lat_shift, lat_frac, remap_frac, diffusivity):
    rows = tracers.shape[1]
    field, below, above = to_columns(tracers)
    count = field.shape[1]
    width = field.shape[2]
    lon_shift, lon_frac, lat_shift, lat_frac, remap_frac, diffusivity = (
        own_rows(v, count) for v in (lon_shift, lon_frac, lat_shift, lat_frac, remap_frac, diffusivity)
    )
    for time_step in range(STEPS):
        if time_step == 0:
            field = lat_pieces(below, field, above, lat_shift[time_step], lat_frac[time_step])
        else:
            padded = lat_halo(field, 3)
            field = lat_step(padded, lat_shift[time_step], lat_frac[time_step], count)
        amount = jnp.remainder(lon_shift[time_step], width // PAIR)
        field = lon_cubic(roll_rows(field, amount), lon_frac[time_step])
        field = remap(field, remap_frac[time_step])
        field = diffuse(field, diffusivity)
    return from_columns(field, rows)


def solution(mesh):
    in_specs = (
        P(None, "lat", "lon"),
        P(None, None, "lat"),
        P(None, None, "lat"),
        P(None, None, "lat"),
        P(None, None, "lat"),
        P(None, None, "lat"),
        P(None, "lat"),
    )
    out_specs = P(None, "lat", "lon")
    return jax.shard_map(
        per_device, mesh=mesh, in_specs=in_specs, out_specs=out_specs, check_vma=False
    )
```

```python
import functools

import jax
import numpy as np
import jax.numpy as jnp
from jax import lax
from jax.experimental import pallas as pl
from jax.experimental.pallas import tpu as pltpu
from jax.sharding import PartitionSpec as P

NTR = 8
STEPS = 2


def from_behind(x, axis, by):
    peers = lax.axis_size(axis)
    return lax.ppermute(x, axis, [(i, (i + by) % peers) for i in range(peers)])


def with_halo(block, sides, width, periodic):
    for axis, dim in sides:
        count = lax.axis_size(axis)
        forward = [(i, i + 1) for i in range(count - 1)]
        if periodic:
            forward.append((count - 1, 0))
        backward = [(target, source) for source, target in forward]
        low = lax.ppermute(
            lax.slice_in_dim(block, block.shape[dim] - width, None, axis=dim), axis, forward
        )
        high = lax.ppermute(lax.slice_in_dim(block, 0, width, axis=dim), axis, backward)
        block = jnp.concatenate([low, block, high], axis=dim)
    return block


def cubic_weights(fraction):
    w_zero = -fraction * (fraction - 1.0) * (fraction - 2.0) / 6.0
    w_one = (fraction + 1.0) * (fraction - 1.0) * (fraction - 2.0) / 2.0
    w_two = -(fraction + 1.0) * fraction * (fraction - 2.0) / 2.0
    w_three = (fraction + 1.0) * fraction * (fraction - 1.0) / 6.0
    return (w_zero, w_one, w_two, w_three)


def lat_step(padded, offset, fraction, row_count):
    weights = cubic_weights(fraction)
    summed = None
    for place_index in range(6):
        row_delta = place_index - 2
        coeff = jnp.zeros_like(fraction)
        for tap_index in range(4):
            coeff = coeff + jnp.where(offset == tap_index - 1 - row_delta, weights[tap_index], 0.0)
        addend = coeff[:, :, None] * padded[:, 1 + place_index : 1 + place_index + row_count, :]
        summed = addend if summed is None else summed + addend
    return summed


def lon_step(wrapped, fraction, tracer_count):
    weights = cubic_weights(fraction)
    width_cols = wrapped.shape[2] - 4 * tracer_count
    summed = None
    for tap_index in range(4):
        offset_cols = (1 + tap_index) * tracer_count
        addend = (
            weights[tap_index][:, :, None] * wrapped[:, :, offset_cols : offset_cols + width_cols]
        )
        summed = addend if summed is None else summed + addend
    return summed


def remap(tracer_field, fraction):
    level_above = jnp.concatenate([tracer_field[1:], tracer_field[-1:]], axis=0)
    return (1.0 - fraction)[:, :, None] * tracer_field + fraction[:, :, None] * level_above


def diffuse(tracer_field, kappa):
    levels = tracer_field.shape[0]
    face_kappa = 0.5 * (kappa[:-1] + kappa[1:])
    zero_face = jnp.zeros_like(kappa[:1])
    face_below = jnp.concatenate([zero_face, face_kappa], axis=0)
    face_above = jnp.concatenate([face_kappa, zero_face], axis=0)
    ratio_prev = jnp.zeros_like(kappa[0])
    solved_prev = jnp.zeros_like(tracer_field[0])
    ratios = []
    solveds = []
    for level_index in range(levels):
        below = face_below[level_index]
        above = face_above[level_index]
        pivot_value = 1.0 + below + above + below * ratio_prev
        ratio_now = -above / pivot_value
        solved_now = (tracer_field[level_index] + below[:, None] * solved_prev) / pivot_value[
            :, None
        ]
        ratios.append(ratio_now)
        solveds.append(solved_now)
        ratio_prev = ratio_now
        solved_prev = solved_now
    results = [None] * levels
    results[levels - 1] = solveds[levels - 1]
    for level_index in range(levels - 2, -1, -1):
        results[level_index] = (
            solveds[level_index] - ratios[level_index][:, None] * results[level_index + 1]
        )
    return jnp.stack(results, axis=0)


def bit_mask(amount, position):
    return (amount // 2**position % 2 == 1)[:, :, None]


PAIR = 2


def pair_order(cells):
    cols = np.arange(cells * NTR)
    cell, tracer = cols // NTR, cols % NTR
    return (tracer // PAIR) * cells * PAIR + cell * PAIR + tracer % PAIR


def permutation(target, inverse):
    cols = np.arange(target.shape[0])
    if inverse:
        matrix = cols[:, None] == target[None, :]
    else:
        matrix = cols[None, :] == target[:, None]
    return jnp.asarray(matrix.astype(np.float32), dtype=jnp.bfloat16)


def permute_block(block, matrix):
    high = block.astype(jnp.bfloat16)
    rest = block - high.astype(jnp.float32)
    middle = rest.astype(jnp.bfloat16)
    low = (rest - middle.astype(jnp.float32)).astype(jnp.bfloat16)
    total = jnp.dot(high, matrix, preferred_element_type=jnp.float32)
    total = total + jnp.dot(middle, matrix, preferred_element_type=jnp.float32)
    return total + jnp.dot(low, matrix, preferred_element_type=jnp.float32)


CHUNKS = 4
MESH_ID = pl.DeviceIdType.MESH


def greet(count, me, lat):
    barrier = pltpu.get_barrier_semaphore()
    for offset in range(1, count):
        peer = lax.rem(me + offset, count)
        pl.semaphore_signal(barrier, 1, device_id=(peer, lat), device_id_type=MESH_ID)
    return barrier


def neighbours(parts):
    lon = lax.axis_index("lon")
    lat = lax.axis_index("lat")
    bands = lax.axis_size("lat")
    quarter = lon % parts
    inside_up = quarter < parts - 1
    inside_down = quarter > 0
    has_up = jnp.logical_or(inside_up, lat < bands - 1)
    has_down = jnp.logical_or(inside_down, lat > 0)
    up = (jnp.where(inside_up, lon + 1, lon + 1 - parts), jnp.where(inside_up, lat, lat + 1))
    down = (jnp.where(inside_down, lon - 1, lon + parts - 1), jnp.where(inside_down, lat, lat - 1))
    return has_up, up, has_down, down


def entry_kernel(x_ref, matrix_ref, field_ref, below_ref, above_ref, moved, landed, top_stage, bottom_stage,
                 zero_low, zero_high, send_sem, recv_sem, local_sem, halo_send, halo_recv, store_sem,
                 *, src_at, dst_at, parts):
    count = lax.axis_size("lon")
    me = lax.axis_index("lon")
    lat = lax.axis_index("lat")
    levels = x_ref.shape[0]
    rows = landed.shape[1]
    per = levels // CHUNKS
    has_up, up, has_down, down = neighbours(parts)
    barrier = greet(count, me, lat)

    @pl.when(has_up)
    def _():
        pl.semaphore_signal(barrier, 1, device_id=up, device_id_type=MESH_ID)

    @pl.when(has_down)
    def _():
        pl.semaphore_signal(barrier, 1, device_id=down, device_id_type=MESH_ID)

    copies = []
    locals_ = []
    for chunk in range(CHUNKS):
        def body(k, carry):
            moved[k] = permute_block(x_ref[k], matrix_ref[...])
            return carry

        lax.fori_loop(chunk * per, (chunk + 1) * per, body, 0)
        if chunk == 0:
            pl.semaphore_wait(barrier, count - 1 + has_up.astype(jnp.int32) + has_down.astype(jnp.int32))
        part = pl.ds(chunk * per, per)
        for offset in range(1, count):
            peer = lax.rem(me + offset, count)
            copy = pltpu.make_async_remote_copy(
                src_ref=src_at(moved, peer, part),
                dst_ref=dst_at(landed, me, part),
                send_sem=send_sem.at[chunk, offset],
                recv_sem=recv_sem.at[chunk, offset],
                device_id=(peer, lat),
                device_id_type=MESH_ID,
            )
            copy.start()
            copies.append(copy)
        local = pltpu.make_async_copy(src_at(moved, me, part), dst_at(landed, me, part), local_sem.at[chunk])
        local.start()
        locals_.append(local)
    for copy in copies:
        copy.wait_recv()
    for local in locals_:
        local.wait()
    top_stage[...] = landed[:, rows - top_stage.shape[1] :, :]
    bottom_stage[...] = landed[:, : bottom_stage.shape[1], :]
    to_up = pltpu.make_async_remote_copy(
        src_ref=top_stage, dst_ref=below_ref, send_sem=halo_send.at[0], recv_sem=halo_recv.at[0],
        device_id=up, device_id_type=MESH_ID,
    )
    to_down = pltpu.make_async_remote_copy(
        src_ref=bottom_stage, dst_ref=above_ref, send_sem=halo_send.at[1], recv_sem=halo_recv.at[1],
        device_id=down, device_id_type=MESH_ID,
    )

    @pl.when(has_up)
    def _():
        to_up.start()

    @pl.when(has_down)
    def _():
        to_down.start()

    store = pltpu.make_async_copy(landed, field_ref, store_sem.at[0])
    store.start()
    fill_low = pltpu.make_async_copy(zero_low, below_ref, store_sem.at[1])
    fill_high = pltpu.make_async_copy(zero_high, above_ref, store_sem.at[2])

    @pl.when(jnp.logical_not(has_down))
    def _():
        zero_low[...] = jnp.zeros(zero_low.shape, zero_low.dtype)
        fill_low.start()
        fill_low.wait()

    @pl.when(jnp.logical_not(has_up))
    def _():
        zero_high[...] = jnp.zeros(zero_high.shape, zero_high.dtype)
        fill_high.start()
        fill_high.wait()

    store.wait()

    for copy in copies:
        copy.wait_send()

    @pl.when(has_up)
    def _():
        to_up.wait_send()
        to_down.wait_recv()

    @pl.when(has_down)
    def _():
        to_down.wait_send()
        to_up.wait_recv()


def exit_kernel(src_ref, matrix_ref, out_ref, landed, send_sem, recv_sem, local_sem, *, src_at, dst_at):
    count = lax.axis_size("lon")
    me = lax.axis_index("lon")
    lat = lax.axis_index("lat")
    levels = out_ref.shape[0]
    per = levels // CHUNKS
    barrier = greet(count, me, lat)
    pl.semaphore_wait(barrier, count - 1)
    copies = []
    locals_ = []
    for chunk in range(CHUNKS):
        part = pl.ds(chunk * per, per)
        row = []
        for offset in range(1, count):
            peer = lax.rem(me + offset, count)
            copy = pltpu.make_async_remote_copy(
                src_ref=src_at(src_ref, peer, part),
                dst_ref=dst_at(landed, me, part),
                send_sem=send_sem.at[chunk, offset],
                recv_sem=recv_sem.at[chunk, offset],
                device_id=(peer, lat),
                device_id_type=MESH_ID,
            )
            copy.start()
            row.append(copy)
        copies.append(row)
        local = pltpu.make_async_copy(src_at(src_ref, me, part), dst_at(landed, me, part), local_sem.at[chunk])
        local.start()
        locals_.append(local)
    for chunk in range(CHUNKS):
        for copy in copies[chunk]:
            copy.wait_recv()
        locals_[chunk].wait()

        def body(k, carry):
            out_ref[k] = permute_block(landed[k], matrix_ref[...])
            return carry

        lax.fori_loop(chunk * per, (chunk + 1) * per, body, 0)
    for row in copies:
        for copy in row:
            copy.wait_send()


def run_exchange(kernel, operand, matrix, out_shape, src_spec, out_spec, scratch, src_at, dst_at, ident):
    count = lax.axis_size("lon")
    return pl.pallas_call(
        functools.partial(kernel, src_at=src_at, dst_at=dst_at),
        out_shape=jax.ShapeDtypeStruct(out_shape, operand.dtype),
        in_specs=[src_spec, pl.BlockSpec(memory_space=pltpu.VMEM)],
        out_specs=out_spec,
        scratch_shapes=[
            pltpu.VMEM(scratch, operand.dtype),
            pltpu.SemaphoreType.DMA((CHUNKS, count)),
            pltpu.SemaphoreType.DMA((CHUNKS, count)),
            pltpu.SemaphoreType.DMA((CHUNKS,)),
        ],
        compiler_params=pltpu.CompilerParams(collective_id=ident, has_side_effects=True),
    )(operand, matrix)


def to_columns(block):
    levels, rows, width = block.shape
    cells = width // NTR
    devices = lax.axis_size("lon")
    parts = devices // (NTR // PAIR)
    count = rows // parts
    lane = cells * PAIR

    def src_at(ref, peer, part):
        return ref.at[part, pl.ds((peer % parts) * count, count), pl.ds((peer // parts) * lane, lane)]

    def dst_at(ref, sender, part):
        return ref.at[part, :, pl.ds(sender * lane, lane)]

    vmem = pl.BlockSpec(memory_space=pltpu.VMEM)
    hbm = pl.BlockSpec(memory_space=pl.ANY)
    field_shape = (levels, count, devices * lane)
    below_shape = (levels, 2, devices * lane)
    above_shape = (levels, 3, devices * lane)
    return pl.pallas_call(
        functools.partial(entry_kernel, src_at=src_at, dst_at=dst_at, parts=parts),
        out_shape=tuple(jax.ShapeDtypeStruct(shape, block.dtype) for shape in (field_shape, below_shape, above_shape)),
        in_specs=[vmem, vmem],
        out_specs=(hbm, hbm, hbm),
        scratch_shapes=[
            pltpu.VMEM(block.shape, block.dtype),
            pltpu.VMEM(field_shape, block.dtype),
            pltpu.VMEM(below_shape, block.dtype),
            pltpu.VMEM(above_shape, block.dtype),
            pltpu.VMEM(below_shape, block.dtype),
            pltpu.VMEM(above_shape, block.dtype),
            pltpu.SemaphoreType.DMA((CHUNKS, devices)),
            pltpu.SemaphoreType.DMA((CHUNKS, devices)),
            pltpu.SemaphoreType.DMA((CHUNKS,)),
            pltpu.SemaphoreType.DMA((2,)),
            pltpu.SemaphoreType.DMA((2,)),
            pltpu.SemaphoreType.DMA((3,)),
        ],
        compiler_params=pltpu.CompilerParams(collective_id=0, has_side_effects=True),
    )(block, permutation(pair_order(cells), False))


def from_columns(field, rows):
    levels, count, width = field.shape
    devices = lax.axis_size("lon")
    parts = devices // (NTR // PAIR)
    lane = width // devices
    cells = lane // PAIR

    def src_at(ref, peer, part):
        return ref.at[part, :, pl.ds(peer * lane, lane)]

    def dst_at(ref, sender, part):
        return ref.at[part, pl.ds((sender % parts) * count, count), pl.ds((sender // parts) * lane, lane)]

    shape = (levels, rows, cells * NTR)
    return run_exchange(
        exit_kernel, field, permutation(pair_order(cells), True), shape,
        pl.BlockSpec(memory_space=pl.ANY), pl.BlockSpec(memory_space=pltpu.VMEM), shape,
        src_at, dst_at, 1,
    )


def lat_halo(field, width):
    lon_n = lax.axis_size("lon")
    lat_n = lax.axis_size("lat")
    parts = lon_n // (NTR // PAIR)
    up = []
    for b in range(lat_n):
        for l in range(lon_n):
            t, h = l // parts, l % parts
            g = b * parts + h
            if g + 1 < lat_n * parts:
                nb, nh = (g + 1) // parts, (g + 1) % parts
                up.append((l * lat_n + b, (t * parts + nh) * lat_n + nb))
    down = [(d, s) for s, d in up]
    rows = field.shape[1]
    below = lax.ppermute(field[:, rows - width + 1 :], ("lon", "lat"), up)
    above = lax.ppermute(field[:, :width], ("lon", "lat"), down)
    return jnp.concatenate([below[:, :1], below, field, above], axis=1)


def roll_rows(field, amount):
    cells = field.shape[2] // PAIR
    current = field
    for position in range(cells.bit_length() - 1):
        moved = jnp.roll(current, PAIR * 2**position, axis=2)
        current = jnp.where(bit_mask(amount, position), moved, current)
    return current


def lon_cubic(shifted, fraction):
    weights = cubic_weights(fraction)
    taps = [jnp.roll(shifted, PAIR * (1 - p), axis=2) for p in range(4)]
    summed = None
    for p in range(4):
        addend = weights[p][:, :, None] * taps[p]
        summed = addend if summed is None else summed + addend
    return summed


def own_rows(values, count):
    parts = lax.axis_size("lon") // (NTR // PAIR)
    start = (lax.axis_index("lon") % parts) * count
    return lax.dynamic_slice_in_dim(values, start, count, axis=values.ndim - 1)


def per_device(tracers, lon_shift, lon_frac, lat_shift, lat_frac, remap_frac, diffusivity):
    rows = tracers.shape[1]
    field, below, above = to_columns(tracers)
    count = field.shape[1]
    width = field.shape[2]
    lon_shift, lon_frac, lat_shift, lat_frac, remap_frac, diffusivity = (
        own_rows(v, count) for v in (lon_shift, lon_frac, lat_shift, lat_frac, remap_frac, diffusivity)
    )
    for time_step in range(STEPS):
        if time_step == 0:
            padded = jnp.concatenate([below[:, :1], below, field, above], axis=1)
        else:
            padded = lat_halo(field, 3)
        field = lat_step(padded, lat_shift[time_step], lat_frac[time_step], count)
        amount = jnp.remainder(lon_shift[time_step], width // PAIR)
        field = lon_cubic(roll_rows(field, amount), lon_frac[time_step])
        field = remap(field, remap_frac[time_step])
        field = diffuse(field, diffusivity)
    return from_columns(field, rows)


def solution(mesh):
    in_specs = (
        P(None, "lat", "lon"),
        P(None, None, "lat"),
        P(None, None, "lat"),
        P(None, None, "lat"),
        P(None, None, "lat"),
        P(None, None, "lat"),
        P(None, "lat"),
    )
    out_specs = P(None, "lat", "lon")
    return jax.shard_map(
        per_device, mesh=mesh, in_specs=in_specs, out_specs=out_specs, check_vma=False
    )
```

```python
import functools

import jax
import numpy as np
import jax.numpy as jnp
from jax import lax
from jax.experimental import pallas as pl
from jax.experimental.pallas import tpu as pltpu
from jax.sharding import PartitionSpec as P

NTR = 8
STEPS = 2


def from_behind(x, axis, by):
    peers = lax.axis_size(axis)
    return lax.ppermute(x, axis, [(i, (i + by) % peers) for i in range(peers)])


def with_halo(block, sides, width, periodic):
    for axis, dim in sides:
        count = lax.axis_size(axis)
        forward = [(i, i + 1) for i in range(count - 1)]
        if periodic:
            forward.append((count - 1, 0))
        backward = [(target, source) for source, target in forward]
        low = lax.ppermute(
            lax.slice_in_dim(block, block.shape[dim] - width, None, axis=dim), axis, forward
        )
        high = lax.ppermute(lax.slice_in_dim(block, 0, width, axis=dim), axis, backward)
        block = jnp.concatenate([low, block, high], axis=dim)
    return block


def cubic_weights(fraction):
    w_zero = -fraction * (fraction - 1.0) * (fraction - 2.0) / 6.0
    w_one = (fraction + 1.0) * (fraction - 1.0) * (fraction - 2.0) / 2.0
    w_two = -(fraction + 1.0) * fraction * (fraction - 2.0) / 2.0
    w_three = (fraction + 1.0) * fraction * (fraction - 1.0) / 6.0
    return (w_zero, w_one, w_two, w_three)


def lat_step(padded, offset, fraction, row_count):
    weights = cubic_weights(fraction)
    summed = None
    for place_index in range(6):
        row_delta = place_index - 2
        coeff = jnp.zeros_like(fraction)
        for tap_index in range(4):
            coeff = coeff + jnp.where(offset == tap_index - 1 - row_delta, weights[tap_index], 0.0)
        addend = coeff[:, :, None] * padded[:, 1 + place_index : 1 + place_index + row_count, :]
        summed = addend if summed is None else summed + addend
    return summed


def lon_step(wrapped, fraction, tracer_count):
    weights = cubic_weights(fraction)
    width_cols = wrapped.shape[2] - 4 * tracer_count
    summed = None
    for tap_index in range(4):
        offset_cols = (1 + tap_index) * tracer_count
        addend = (
            weights[tap_index][:, :, None] * wrapped[:, :, offset_cols : offset_cols + width_cols]
        )
        summed = addend if summed is None else summed + addend
    return summed


def remap(tracer_field, fraction):
    level_above = jnp.concatenate([tracer_field[1:], tracer_field[-1:]], axis=0)
    return (1.0 - fraction)[:, :, None] * tracer_field + fraction[:, :, None] * level_above


def diffuse(tracer_field, kappa):
    levels = tracer_field.shape[0]
    face_kappa = 0.5 * (kappa[:-1] + kappa[1:])
    zero_face = jnp.zeros_like(kappa[:1])
    face_below = jnp.concatenate([zero_face, face_kappa], axis=0)
    face_above = jnp.concatenate([face_kappa, zero_face], axis=0)
    ratio_prev = jnp.zeros_like(kappa[0])
    solved_prev = jnp.zeros_like(tracer_field[0])
    ratios = []
    solveds = []
    for level_index in range(levels):
        below = face_below[level_index]
        above = face_above[level_index]
        pivot_value = 1.0 + below + above + below * ratio_prev
        ratio_now = -above / pivot_value
        solved_now = (tracer_field[level_index] + below[:, None] * solved_prev) / pivot_value[
            :, None
        ]
        ratios.append(ratio_now)
        solveds.append(solved_now)
        ratio_prev = ratio_now
        solved_prev = solved_now
    results = [None] * levels
    results[levels - 1] = solveds[levels - 1]
    for level_index in range(levels - 2, -1, -1):
        results[level_index] = (
            solveds[level_index] - ratios[level_index][:, None] * results[level_index + 1]
        )
    return jnp.stack(results, axis=0)


def bit_mask(amount, position):
    return (amount // 2**position % 2 == 1)[:, :, None]


PAIR = 2


def pair_order(cells):
    cols = np.arange(cells * NTR)
    cell, tracer = cols // NTR, cols % NTR
    return (tracer // PAIR) * cells * PAIR + cell * PAIR + tracer % PAIR


def permutation(target, inverse):
    cols = np.arange(target.shape[0])
    if inverse:
        matrix = cols[:, None] == target[None, :]
    else:
        matrix = cols[None, :] == target[:, None]
    return jnp.asarray(matrix.astype(np.float32), dtype=jnp.bfloat16)


def permute_block(block, matrix):
    high = block.astype(jnp.bfloat16)
    rest = block - high.astype(jnp.float32)
    middle = rest.astype(jnp.bfloat16)
    low = (rest - middle.astype(jnp.float32)).astype(jnp.bfloat16)
    total = jnp.dot(high, matrix, preferred_element_type=jnp.float32)
    total = total + jnp.dot(middle, matrix, preferred_element_type=jnp.float32)
    return total + jnp.dot(low, matrix, preferred_element_type=jnp.float32)


CHUNKS = 6
MESH_ID = pl.DeviceIdType.MESH


def greet(count, me, lat):
    barrier = pltpu.get_barrier_semaphore()
    for offset in range(1, count):
        peer = lax.rem(me + offset, count)
        pl.semaphore_signal(barrier, 1, device_id=(peer, lat), device_id_type=MESH_ID)
    return barrier


def neighbours(parts):
    lon = lax.axis_index("lon")
    lat = lax.axis_index("lat")
    bands = lax.axis_size("lat")
    quarter = lon % parts
    inside_up = quarter < parts - 1
    inside_down = quarter > 0
    has_up = jnp.logical_or(inside_up, lat < bands - 1)
    has_down = jnp.logical_or(inside_down, lat > 0)
    up = (jnp.where(inside_up, lon + 1, lon + 1 - parts), jnp.where(inside_up, lat, lat + 1))
    down = (jnp.where(inside_down, lon - 1, lon + parts - 1), jnp.where(inside_down, lat, lat - 1))
    return has_up, up, has_down, down


def entry_kernel(x_ref, matrix_ref, field_ref, below_ref, above_ref, moved, landed, top_stage, bottom_stage,
                 zero_low, zero_high, send_sem, recv_sem, local_sem, halo_send, halo_recv, store_sem,
                 *, src_at, dst_at, parts):
    count = lax.axis_size("lon")
    me = lax.axis_index("lon")
    lat = lax.axis_index("lat")
    levels = x_ref.shape[0]
    rows = landed.shape[1]
    per = levels // CHUNKS
    has_up, up, has_down, down = neighbours(parts)
    barrier = greet(count, me, lat)

    @pl.when(has_up)
    def _():
        pl.semaphore_signal(barrier, 1, device_id=up, device_id_type=MESH_ID)

    @pl.when(has_down)
    def _():
        pl.semaphore_signal(barrier, 1, device_id=down, device_id_type=MESH_ID)

    copies = []
    locals_ = []
    for chunk in range(CHUNKS):
        def body(k, carry):
            moved[k] = permute_block(x_ref[k], matrix_ref[...])
            return carry

        lax.fori_loop(chunk * per, (chunk + 1) * per, body, 0)
        if chunk == 0:
            pl.semaphore_wait(barrier, count - 1 + has_up.astype(jnp.int32) + has_down.astype(jnp.int32))
        part = pl.ds(chunk * per, per)
        for offset in range(1, count):
            peer = lax.rem(me + offset, count)
            copy = pltpu.make_async_remote_copy(
                src_ref=src_at(moved, peer, part),
                dst_ref=dst_at(landed, me, part),
                send_sem=send_sem.at[chunk, offset],
                recv_sem=recv_sem.at[chunk, offset],
                device_id=(peer, lat),
                device_id_type=MESH_ID,
            )
            copy.start()
            copies.append(copy)
        local = pltpu.make_async_copy(src_at(moved, me, part), dst_at(landed, me, part), local_sem.at[chunk])
        local.start()
        locals_.append(local)
    for copy in copies:
        copy.wait_recv()
    for local in locals_:
        local.wait()
    top_stage[...] = landed[:, rows - top_stage.shape[1] :, :]
    bottom_stage[...] = landed[:, : bottom_stage.shape[1], :]
    to_up = pltpu.make_async_remote_copy(
        src_ref=top_stage, dst_ref=below_ref, send_sem=halo_send.at[0], recv_sem=halo_recv.at[0],
        device_id=up, device_id_type=MESH_ID,
    )
    to_down = pltpu.make_async_remote_copy(
        src_ref=bottom_stage, dst_ref=above_ref, send_sem=halo_send.at[1], recv_sem=halo_recv.at[1],
        device_id=down, device_id_type=MESH_ID,
    )

    @pl.when(has_up)
    def _():
        to_up.start()

    @pl.when(has_down)
    def _():
        to_down.start()

    store = pltpu.make_async_copy(landed, field_ref, store_sem.at[0])
    store.start()
    fill_low = pltpu.make_async_copy(zero_low, below_ref, store_sem.at[1])
    fill_high = pltpu.make_async_copy(zero_high, above_ref, store_sem.at[2])

    @pl.when(jnp.logical_not(has_down))
    def _():
        zero_low[...] = jnp.zeros(zero_low.shape, zero_low.dtype)
        fill_low.start()
        fill_low.wait()

    @pl.when(jnp.logical_not(has_up))
    def _():
        zero_high[...] = jnp.zeros(zero_high.shape, zero_high.dtype)
        fill_high.start()
        fill_high.wait()

    store.wait()

    for copy in copies:
        copy.wait_send()

    @pl.when(has_up)
    def _():
        to_up.wait_send()
        to_down.wait_recv()

    @pl.when(has_down)
    def _():
        to_down.wait_send()
        to_up.wait_recv()


def exit_kernel(src_ref, matrix_ref, out_ref, landed, send_sem, recv_sem, local_sem, *, src_at, dst_at):
    count = lax.axis_size("lon")
    me = lax.axis_index("lon")
    lat = lax.axis_index("lat")
    levels = out_ref.shape[0]
    per = levels // CHUNKS
    barrier = greet(count, me, lat)
    pl.semaphore_wait(barrier, count - 1)
    copies = []
    locals_ = []
    for chunk in range(CHUNKS):
        part = pl.ds(chunk * per, per)
        row = []
        for offset in range(1, count):
            peer = lax.rem(me + offset, count)
            copy = pltpu.make_async_remote_copy(
                src_ref=src_at(src_ref, peer, part),
                dst_ref=dst_at(landed, me, part),
                send_sem=send_sem.at[chunk, offset],
                recv_sem=recv_sem.at[chunk, offset],
                device_id=(peer, lat),
                device_id_type=MESH_ID,
            )
            copy.start()
            row.append(copy)
        copies.append(row)
        local = pltpu.make_async_copy(src_at(src_ref, me, part), dst_at(landed, me, part), local_sem.at[chunk])
        local.start()
        locals_.append(local)
    for chunk in range(CHUNKS):
        for copy in copies[chunk]:
            copy.wait_recv()
        locals_[chunk].wait()

        def body(k, carry):
            out_ref[k] = permute_block(landed[k], matrix_ref[...])
            return carry

        lax.fori_loop(chunk * per, (chunk + 1) * per, body, 0)
    for row in copies:
        for copy in row:
            copy.wait_send()


def run_exchange(kernel, operand, matrix, out_shape, src_spec, out_spec, scratch, src_at, dst_at, ident):
    count = lax.axis_size("lon")
    return pl.pallas_call(
        functools.partial(kernel, src_at=src_at, dst_at=dst_at),
        out_shape=jax.ShapeDtypeStruct(out_shape, operand.dtype),
        in_specs=[src_spec, pl.BlockSpec(memory_space=pltpu.VMEM)],
        out_specs=out_spec,
        scratch_shapes=[
            pltpu.VMEM(scratch, operand.dtype),
            pltpu.SemaphoreType.DMA((CHUNKS, count)),
            pltpu.SemaphoreType.DMA((CHUNKS, count)),
            pltpu.SemaphoreType.DMA((CHUNKS,)),
        ],
        compiler_params=pltpu.CompilerParams(collective_id=ident, has_side_effects=True),
    )(operand, matrix)


def to_columns(block):
    levels, rows, width = block.shape
    cells = width // NTR
    devices = lax.axis_size("lon")
    parts = devices // (NTR // PAIR)
    count = rows // parts
    lane = cells * PAIR

    def src_at(ref, peer, part):
        return ref.at[part, pl.ds((peer % parts) * count, count), pl.ds((peer // parts) * lane, lane)]

    def dst_at(ref, sender, part):
        return ref.at[part, :, pl.ds(sender * lane, lane)]

    vmem = pl.BlockSpec(memory_space=pltpu.VMEM)
    hbm = pl.BlockSpec(memory_space=pl.ANY)
    field_shape = (levels, count, devices * lane)
    below_shape = (levels, 2, devices * lane)
    above_shape = (levels, 3, devices * lane)
    return pl.pallas_call(
        functools.partial(entry_kernel, src_at=src_at, dst_at=dst_at, parts=parts),
        out_shape=tuple(jax.ShapeDtypeStruct(shape, block.dtype) for shape in (field_shape, below_shape, above_shape)),
        in_specs=[vmem, vmem],
        out_specs=(hbm, hbm, hbm),
        scratch_shapes=[
            pltpu.VMEM(block.shape, block.dtype),
            pltpu.VMEM(field_shape, block.dtype),
            pltpu.VMEM(below_shape, block.dtype),
            pltpu.VMEM(above_shape, block.dtype),
            pltpu.VMEM(below_shape, block.dtype),
            pltpu.VMEM(above_shape, block.dtype),
            pltpu.SemaphoreType.DMA((CHUNKS, devices)),
            pltpu.SemaphoreType.DMA((CHUNKS, devices)),
            pltpu.SemaphoreType.DMA((CHUNKS,)),
            pltpu.SemaphoreType.DMA((2,)),
            pltpu.SemaphoreType.DMA((2,)),
            pltpu.SemaphoreType.DMA((3,)),
        ],
        compiler_params=pltpu.CompilerParams(collective_id=0, has_side_effects=True),
    )(block, permutation(pair_order(cells), False))


def from_columns(field, rows):
    levels, count, width = field.shape
    devices = lax.axis_size("lon")
    parts = devices // (NTR // PAIR)
    lane = width // devices
    cells = lane // PAIR

    def src_at(ref, peer, part):
        return ref.at[part, :, pl.ds(peer * lane, lane)]

    def dst_at(ref, sender, part):
        return ref.at[part, pl.ds((sender % parts) * count, count), pl.ds((sender // parts) * lane, lane)]

    shape = (levels, rows, cells * NTR)
    return run_exchange(
        exit_kernel, field, permutation(pair_order(cells), True), shape,
        pl.BlockSpec(memory_space=pl.ANY), pl.BlockSpec(memory_space=pltpu.VMEM), shape,
        src_at, dst_at, 1,
    )


def lat_halo(field, width):
    lon_n = lax.axis_size("lon")
    lat_n = lax.axis_size("lat")
    parts = lon_n // (NTR // PAIR)
    up = []
    for b in range(lat_n):
        for l in range(lon_n):
            t, h = l // parts, l % parts
            g = b * parts + h
            if g + 1 < lat_n * parts:
                nb, nh = (g + 1) // parts, (g + 1) % parts
                up.append((l * lat_n + b, (t * parts + nh) * lat_n + nb))
    down = [(d, s) for s, d in up]
    rows = field.shape[1]
    below = lax.ppermute(field[:, rows - width + 1 :], ("lon", "lat"), up)
    above = lax.ppermute(field[:, :width], ("lon", "lat"), down)
    return jnp.concatenate([below[:, :1], below, field, above], axis=1)


def roll_rows(field, amount):
    cells = field.shape[2] // PAIR
    current = field
    for position in range(cells.bit_length() - 1):
        moved = jnp.roll(current, PAIR * 2**position, axis=2)
        current = jnp.where(bit_mask(amount, position), moved, current)
    return current


def lon_cubic(shifted, fraction):
    weights = cubic_weights(fraction)
    taps = [jnp.roll(shifted, PAIR * (1 - p), axis=2) for p in range(4)]
    summed = None
    for p in range(4):
        addend = weights[p][:, :, None] * taps[p]
        summed = addend if summed is None else summed + addend
    return summed


def own_rows(values, count):
    parts = lax.axis_size("lon") // (NTR // PAIR)
    start = (lax.axis_index("lon") % parts) * count
    return lax.dynamic_slice_in_dim(values, start, count, axis=values.ndim - 1)


def per_device(tracers, lon_shift, lon_frac, lat_shift, lat_frac, remap_frac, diffusivity):
    rows = tracers.shape[1]
    field, below, above = to_columns(tracers)
    count = field.shape[1]
    width = field.shape[2]
    lon_shift, lon_frac, lat_shift, lat_frac, remap_frac, diffusivity = (
        own_rows(v, count) for v in (lon_shift, lon_frac, lat_shift, lat_frac, remap_frac, diffusivity)
    )
    for time_step in range(STEPS):
        if time_step == 0:
            padded = jnp.concatenate([below[:, :1], below, field, above], axis=1)
        else:
            padded = lat_halo(field, 3)
        field = lat_step(padded, lat_shift[time_step], lat_frac[time_step], count)
        amount = jnp.remainder(lon_shift[time_step], width // PAIR)
        field = lon_cubic(roll_rows(field, amount), lon_frac[time_step])
        field = remap(field, remap_frac[time_step])
        field = diffuse(field, diffusivity)
    return from_columns(field, rows)


def solution(mesh):
    in_specs = (
        P(None, "lat", "lon"),
        P(None, None, "lat"),
        P(None, None, "lat"),
        P(None, None, "lat"),
        P(None, None, "lat"),
        P(None, None, "lat"),
        P(None, "lat"),
    )
    out_specs = P(None, "lat", "lon")
    return jax.shard_map(
        per_device, mesh=mesh, in_specs=in_specs, out_specs=out_specs, check_vma=False
    )
```

```python
import functools

import jax
import numpy as np
import jax.numpy as jnp
from jax import lax
from jax.experimental import pallas as pl
from jax.experimental.pallas import tpu as pltpu
from jax.sharding import PartitionSpec as P

NTR = 8
STEPS = 2


def from_behind(x, axis, by):
    peers = lax.axis_size(axis)
    return lax.ppermute(x, axis, [(i, (i + by) % peers) for i in range(peers)])


def with_halo(block, sides, width, periodic):
    for axis, dim in sides:
        count = lax.axis_size(axis)
        forward = [(i, i + 1) for i in range(count - 1)]
        if periodic:
            forward.append((count - 1, 0))
        backward = [(target, source) for source, target in forward]
        low = lax.ppermute(
            lax.slice_in_dim(block, block.shape[dim] - width, None, axis=dim), axis, forward
        )
        high = lax.ppermute(lax.slice_in_dim(block, 0, width, axis=dim), axis, backward)
        block = jnp.concatenate([low, block, high], axis=dim)
    return block


def cubic_weights(fraction):
    w_zero = -fraction * (fraction - 1.0) * (fraction - 2.0) / 6.0
    w_one = (fraction + 1.0) * (fraction - 1.0) * (fraction - 2.0) / 2.0
    w_two = -(fraction + 1.0) * fraction * (fraction - 2.0) / 2.0
    w_three = (fraction + 1.0) * fraction * (fraction - 1.0) / 6.0
    return (w_zero, w_one, w_two, w_three)


def lat_step(padded, offset, fraction, row_count):
    weights = cubic_weights(fraction)
    summed = None
    for place_index in range(6):
        row_delta = place_index - 2
        coeff = jnp.zeros_like(fraction)
        for tap_index in range(4):
            coeff = coeff + jnp.where(offset == tap_index - 1 - row_delta, weights[tap_index], 0.0)
        addend = coeff[:, :, None] * padded[:, 1 + place_index : 1 + place_index + row_count, :]
        summed = addend if summed is None else summed + addend
    return summed


def lon_step(wrapped, fraction, tracer_count):
    weights = cubic_weights(fraction)
    width_cols = wrapped.shape[2] - 4 * tracer_count
    summed = None
    for tap_index in range(4):
        offset_cols = (1 + tap_index) * tracer_count
        addend = (
            weights[tap_index][:, :, None] * wrapped[:, :, offset_cols : offset_cols + width_cols]
        )
        summed = addend if summed is None else summed + addend
    return summed


def remap(tracer_field, fraction):
    level_above = jnp.concatenate([tracer_field[1:], tracer_field[-1:]], axis=0)
    return (1.0 - fraction)[:, :, None] * tracer_field + fraction[:, :, None] * level_above


def diffuse(tracer_field, kappa):
    levels = tracer_field.shape[0]
    face_kappa = 0.5 * (kappa[:-1] + kappa[1:])
    zero_face = jnp.zeros_like(kappa[:1])
    face_below = jnp.concatenate([zero_face, face_kappa], axis=0)
    face_above = jnp.concatenate([face_kappa, zero_face], axis=0)
    ratio_prev = jnp.zeros_like(kappa[0])
    solved_prev = jnp.zeros_like(tracer_field[0])
    ratios = []
    solveds = []
    for level_index in range(levels):
        below = face_below[level_index]
        above = face_above[level_index]
        pivot_value = 1.0 + below + above + below * ratio_prev
        ratio_now = -above / pivot_value
        solved_now = (tracer_field[level_index] + below[:, None] * solved_prev) / pivot_value[
            :, None
        ]
        ratios.append(ratio_now)
        solveds.append(solved_now)
        ratio_prev = ratio_now
        solved_prev = solved_now
    results = [None] * levels
    results[levels - 1] = solveds[levels - 1]
    for level_index in range(levels - 2, -1, -1):
        results[level_index] = (
            solveds[level_index] - ratios[level_index][:, None] * results[level_index + 1]
        )
    return jnp.stack(results, axis=0)


def bit_mask(amount, position):
    return (amount // 2**position % 2 == 1)[:, :, None]


PAIR = 2


def pair_order(cells):
    cols = np.arange(cells * NTR)
    cell, tracer = cols // NTR, cols % NTR
    return (tracer // PAIR) * cells * PAIR + cell * PAIR + tracer % PAIR


def permutation(target, inverse):
    cols = np.arange(target.shape[0])
    if inverse:
        matrix = cols[:, None] == target[None, :]
    else:
        matrix = cols[None, :] == target[:, None]
    return jnp.asarray(matrix.astype(np.float32), dtype=jnp.bfloat16)


def permute_block(block, matrix):
    high = block.astype(jnp.bfloat16)
    rest = block - high.astype(jnp.float32)
    middle = rest.astype(jnp.bfloat16)
    low = (rest - middle.astype(jnp.float32)).astype(jnp.bfloat16)
    total = jnp.dot(high, matrix, preferred_element_type=jnp.float32)
    total = total + jnp.dot(middle, matrix, preferred_element_type=jnp.float32)
    return total + jnp.dot(low, matrix, preferred_element_type=jnp.float32)


CHUNKS = 4
MESH_ID = pl.DeviceIdType.MESH


def greet(count, me, lat):
    barrier = pltpu.get_barrier_semaphore()
    for offset in range(1, count):
        peer = lax.rem(me + offset, count)
        pl.semaphore_signal(barrier, 1, device_id=(peer, lat), device_id_type=MESH_ID)
    return barrier


def neighbours(parts):
    lon = lax.axis_index("lon")
    lat = lax.axis_index("lat")
    bands = lax.axis_size("lat")
    quarter = lon % parts
    inside_up = quarter < parts - 1
    inside_down = quarter > 0
    has_up = jnp.logical_or(inside_up, lat < bands - 1)
    has_down = jnp.logical_or(inside_down, lat > 0)
    up = (jnp.where(inside_up, lon + 1, lon + 1 - parts), jnp.where(inside_up, lat, lat + 1))
    down = (jnp.where(inside_down, lon - 1, lon + parts - 1), jnp.where(inside_down, lat, lat - 1))
    return has_up, up, has_down, down


def entry_kernel(x_ref, matrix_ref, field_ref, below_ref, above_ref, moved, landed, top_stage, bottom_stage,
                 zero_low, zero_high, send_sem, recv_sem, local_sem, halo_send, halo_recv, store_sem,
                 *, src_at, dst_at, parts):
    count = lax.axis_size("lon")
    me = lax.axis_index("lon")
    lat = lax.axis_index("lat")
    levels = x_ref.shape[0]
    rows = landed.shape[1]
    per = levels // CHUNKS
    has_up, up, has_down, down = neighbours(parts)
    barrier = greet(count, me, lat)

    @pl.when(has_up)
    def _():
        pl.semaphore_signal(barrier, 1, device_id=up, device_id_type=MESH_ID)

    @pl.when(has_down)
    def _():
        pl.semaphore_signal(barrier, 1, device_id=down, device_id_type=MESH_ID)

    copies = []
    locals_ = []
    for chunk in range(CHUNKS):
        def body(k, carry):
            moved[k] = permute_block(x_ref[k], matrix_ref[...])
            return carry

        lax.fori_loop(chunk * per, (chunk + 1) * per, body, 0)
        if chunk == 0:
            pl.semaphore_wait(barrier, count - 1 + has_up.astype(jnp.int32) + has_down.astype(jnp.int32))
        part = pl.ds(chunk * per, per)
        for offset in range(1, count):
            peer = lax.rem(me + offset, count)
            copy = pltpu.make_async_remote_copy(
                src_ref=src_at(moved, peer, part),
                dst_ref=dst_at(landed, me, part),
                send_sem=send_sem.at[chunk, offset],
                recv_sem=recv_sem.at[chunk, offset],
                device_id=(peer, lat),
                device_id_type=MESH_ID,
            )
            copy.start()
            copies.append(copy)
        local = pltpu.make_async_copy(src_at(moved, me, part), dst_at(landed, me, part), local_sem.at[chunk])
        local.start()
        locals_.append(local)
    for copy in copies:
        copy.wait_recv()
    for local in locals_:
        local.wait()
    top_stage[...] = landed[:, rows - top_stage.shape[1] :, :]
    bottom_stage[...] = landed[:, : bottom_stage.shape[1], :]
    to_up = pltpu.make_async_remote_copy(
        src_ref=top_stage, dst_ref=below_ref, send_sem=halo_send.at[0], recv_sem=halo_recv.at[0],
        device_id=up, device_id_type=MESH_ID,
    )
    to_down = pltpu.make_async_remote_copy(
        src_ref=bottom_stage, dst_ref=above_ref, send_sem=halo_send.at[1], recv_sem=halo_recv.at[1],
        device_id=down, device_id_type=MESH_ID,
    )

    @pl.when(has_up)
    def _():
        to_up.start()

    @pl.when(has_down)
    def _():
        to_down.start()

    store = pltpu.make_async_copy(landed, field_ref, store_sem.at[0])
    store.start()
    fill_low = pltpu.make_async_copy(zero_low, below_ref, store_sem.at[1])
    fill_high = pltpu.make_async_copy(zero_high, above_ref, store_sem.at[2])

    @pl.when(jnp.logical_not(has_down))
    def _():
        zero_low[...] = jnp.zeros(zero_low.shape, zero_low.dtype)
        fill_low.start()
        fill_low.wait()

    @pl.when(jnp.logical_not(has_up))
    def _():
        zero_high[...] = jnp.zeros(zero_high.shape, zero_high.dtype)
        fill_high.start()
        fill_high.wait()

    store.wait()

    for copy in copies:
        copy.wait_send()

    @pl.when(has_up)
    def _():
        to_up.wait_send()
        to_down.wait_recv()

    @pl.when(has_down)
    def _():
        to_down.wait_send()
        to_up.wait_recv()


def exit_kernel(src_ref, matrix_ref, out_ref, landed, send_sem, recv_sem, local_sem, *, src_at, dst_at):
    count = lax.axis_size("lon")
    me = lax.axis_index("lon")
    lat = lax.axis_index("lat")
    levels = out_ref.shape[0]
    per = levels // CHUNKS
    barrier = greet(count, me, lat)
    pl.semaphore_wait(barrier, count - 1)
    copies = []
    locals_ = []
    for chunk in range(CHUNKS):
        part = pl.ds(chunk * per, per)
        row = []
        for offset in range(1, count):
            peer = lax.rem(me + offset, count)
            copy = pltpu.make_async_remote_copy(
                src_ref=src_at(src_ref, peer, part),
                dst_ref=dst_at(landed, me, part),
                send_sem=send_sem.at[chunk, offset],
                recv_sem=recv_sem.at[chunk, offset],
                device_id=(peer, lat),
                device_id_type=MESH_ID,
            )
            copy.start()
            row.append(copy)
        copies.append(row)
        local = pltpu.make_async_copy(src_at(src_ref, me, part), dst_at(landed, me, part), local_sem.at[chunk])
        local.start()
        locals_.append(local)
    for chunk in range(CHUNKS):
        for copy in copies[chunk]:
            copy.wait_recv()
        locals_[chunk].wait()

        def body(k, carry):
            out_ref[k] = permute_block(landed[k], matrix_ref[...])
            return carry

        lax.fori_loop(chunk * per, (chunk + 1) * per, body, 0)
    for row in copies:
        for copy in row:
            copy.wait_send()


def run_exchange(kernel, operand, matrix, out_shape, src_spec, out_spec, scratch, src_at, dst_at, ident):
    count = lax.axis_size("lon")
    return pl.pallas_call(
        functools.partial(kernel, src_at=src_at, dst_at=dst_at),
        out_shape=jax.ShapeDtypeStruct(out_shape, operand.dtype),
        in_specs=[src_spec, pl.BlockSpec(memory_space=pltpu.VMEM)],
        out_specs=out_spec,
        scratch_shapes=[
            pltpu.VMEM(scratch, operand.dtype),
            pltpu.SemaphoreType.DMA((CHUNKS, count)),
            pltpu.SemaphoreType.DMA((CHUNKS, count)),
            pltpu.SemaphoreType.DMA((CHUNKS,)),
        ],
        compiler_params=pltpu.CompilerParams(collective_id=ident, has_side_effects=True),
    )(operand, matrix)


def to_columns(block):
    levels, rows, width = block.shape
    cells = width // NTR
    devices = lax.axis_size("lon")
    parts = devices // (NTR // PAIR)
    count = rows // parts
    lane = cells * PAIR

    def src_at(ref, peer, part):
        return ref.at[part, pl.ds((peer % parts) * count, count), pl.ds((peer // parts) * lane, lane)]

    def dst_at(ref, sender, part):
        return ref.at[part, :, pl.ds(sender * lane, lane)]

    vmem = pl.BlockSpec(memory_space=pltpu.VMEM)
    hbm = pl.BlockSpec(memory_space=pl.ANY)
    field_shape = (levels, count, devices * lane)
    below_shape = (levels, 2, devices * lane)
    above_shape = (levels, 3, devices * lane)
    return pl.pallas_call(
        functools.partial(entry_kernel, src_at=src_at, dst_at=dst_at, parts=parts),
        out_shape=tuple(jax.ShapeDtypeStruct(shape, block.dtype) for shape in (field_shape, below_shape, above_shape)),
        in_specs=[vmem, vmem],
        out_specs=(hbm, hbm, hbm),
        scratch_shapes=[
            pltpu.VMEM(block.shape, block.dtype),
            pltpu.VMEM(field_shape, block.dtype),
            pltpu.VMEM(below_shape, block.dtype),
            pltpu.VMEM(above_shape, block.dtype),
            pltpu.VMEM(below_shape, block.dtype),
            pltpu.VMEM(above_shape, block.dtype),
            pltpu.SemaphoreType.DMA((CHUNKS, devices)),
            pltpu.SemaphoreType.DMA((CHUNKS, devices)),
            pltpu.SemaphoreType.DMA((CHUNKS,)),
            pltpu.SemaphoreType.DMA((2,)),
            pltpu.SemaphoreType.DMA((2,)),
            pltpu.SemaphoreType.DMA((3,)),
        ],
        compiler_params=pltpu.CompilerParams(collective_id=0, has_side_effects=True),
    )(block, permutation(pair_order(cells), False))


def from_columns(field, rows):
    levels, count, width = field.shape
    devices = lax.axis_size("lon")
    parts = devices // (NTR // PAIR)
    lane = width // devices
    cells = lane // PAIR

    def src_at(ref, peer, part):
        return ref.at[part, :, pl.ds(peer * lane, lane)]

    def dst_at(ref, sender, part):
        return ref.at[part, pl.ds((sender % parts) * count, count), pl.ds((sender // parts) * lane, lane)]

    shape = (levels, rows, cells * NTR)
    return run_exchange(
        exit_kernel, field, permutation(pair_order(cells), True), shape,
        pl.BlockSpec(memory_space=pl.ANY), pl.BlockSpec(memory_space=pltpu.VMEM), shape,
        src_at, dst_at, 1,
    )


def lat_halo(field, width):
    lon_n = lax.axis_size("lon")
    lat_n = lax.axis_size("lat")
    parts = lon_n // (NTR // PAIR)
    up = []
    for b in range(lat_n):
        for l in range(lon_n):
            t, h = l // parts, l % parts
            g = b * parts + h
            if g + 1 < lat_n * parts:
                nb, nh = (g + 1) // parts, (g + 1) % parts
                up.append((l * lat_n + b, (t * parts + nh) * lat_n + nb))
    down = [(d, s) for s, d in up]
    rows = field.shape[1]
    below = lax.ppermute(field[:, rows - width + 1 :], ("lon", "lat"), up)
    above = lax.ppermute(field[:, :width], ("lon", "lat"), down)
    return jnp.concatenate([below[:, :1], below, field, above], axis=1)


def roll_rows(field, shift):
    cells = field.shape[2] // PAIR
    reach = cells // 4
    amount = shift + reach
    current = jnp.roll(field, -PAIR * reach, axis=2)
    for position in range((2 * reach - 1).bit_length()):
        moved = jnp.roll(current, PAIR * 2**position, axis=2)
        current = jnp.where(bit_mask(amount, position), moved, current)
    return current


def lon_cubic(shifted, fraction):
    weights = cubic_weights(fraction)
    taps = [jnp.roll(shifted, PAIR * (1 - p), axis=2) for p in range(4)]
    summed = None
    for p in range(4):
        addend = weights[p][:, :, None] * taps[p]
        summed = addend if summed is None else summed + addend
    return summed


def own_rows(values, count):
    parts = lax.axis_size("lon") // (NTR // PAIR)
    start = (lax.axis_index("lon") % parts) * count
    return lax.dynamic_slice_in_dim(values, start, count, axis=values.ndim - 1)


def per_device(tracers, lon_shift, lon_frac, lat_shift, lat_frac, remap_frac, diffusivity):
    rows = tracers.shape[1]
    field, below, above = to_columns(tracers)
    count = field.shape[1]
    width = field.shape[2]
    lon_shift, lon_frac, lat_shift, lat_frac, remap_frac, diffusivity = (
        own_rows(v, count) for v in (lon_shift, lon_frac, lat_shift, lat_frac, remap_frac, diffusivity)
    )
    for time_step in range(STEPS):
        if time_step == 0:
            padded = jnp.concatenate([below[:, :1], below, field, above], axis=1)
        else:
            padded = lat_halo(field, 3)
        field = lat_step(padded, lat_shift[time_step], lat_frac[time_step], count)
        field = lon_cubic(roll_rows(field, lon_shift[time_step]), lon_frac[time_step])
        field = remap(field, remap_frac[time_step])
        field = diffuse(field, diffusivity)
    return from_columns(field, rows)


def solution(mesh):
    in_specs = (
        P(None, "lat", "lon"),
        P(None, None, "lat"),
        P(None, None, "lat"),
        P(None, None, "lat"),
        P(None, None, "lat"),
        P(None, None, "lat"),
        P(None, "lat"),
    )
    out_specs = P(None, "lat", "lon")
    return jax.shard_map(
        per_device, mesh=mesh, in_specs=in_specs, out_specs=out_specs, check_vma=False
    )
```

```python
import functools

import jax
import numpy as np
import jax.numpy as jnp
from jax import lax
from jax.experimental import pallas as pl
from jax.experimental.pallas import tpu as pltpu
from jax.sharding import PartitionSpec as P

NTR = 8
STEPS = 2


def from_behind(x, axis, by):
    peers = lax.axis_size(axis)
    return lax.ppermute(x, axis, [(i, (i + by) % peers) for i in range(peers)])


def with_halo(block, sides, width, periodic):
    for axis, dim in sides:
        count = lax.axis_size(axis)
        forward = [(i, i + 1) for i in range(count - 1)]
        if periodic:
            forward.append((count - 1, 0))
        backward = [(target, source) for source, target in forward]
        low = lax.ppermute(
            lax.slice_in_dim(block, block.shape[dim] - width, None, axis=dim), axis, forward
        )
        high = lax.ppermute(lax.slice_in_dim(block, 0, width, axis=dim), axis, backward)
        block = jnp.concatenate([low, block, high], axis=dim)
    return block


def cubic_weights(fraction):
    w_zero = -fraction * (fraction - 1.0) * (fraction - 2.0) / 6.0
    w_one = (fraction + 1.0) * (fraction - 1.0) * (fraction - 2.0) / 2.0
    w_two = -(fraction + 1.0) * fraction * (fraction - 2.0) / 2.0
    w_three = (fraction + 1.0) * fraction * (fraction - 1.0) / 6.0
    return (w_zero, w_one, w_two, w_three)


def lat_step(padded, offset, fraction, row_count):
    weights = cubic_weights(fraction)
    summed = None
    for place_index in range(6):
        row_delta = place_index - 2
        coeff = jnp.zeros_like(fraction)
        for tap_index in range(4):
            coeff = coeff + jnp.where(offset == tap_index - 1 - row_delta, weights[tap_index], 0.0)
        addend = coeff[:, :, None] * padded[:, 1 + place_index : 1 + place_index + row_count, :]
        summed = addend if summed is None else summed + addend
    return summed


def lon_step(wrapped, fraction, tracer_count):
    weights = cubic_weights(fraction)
    width_cols = wrapped.shape[2] - 4 * tracer_count
    summed = None
    for tap_index in range(4):
        offset_cols = (1 + tap_index) * tracer_count
        addend = (
            weights[tap_index][:, :, None] * wrapped[:, :, offset_cols : offset_cols + width_cols]
        )
        summed = addend if summed is None else summed + addend
    return summed


def remap(tracer_field, fraction):
    level_above = jnp.concatenate([tracer_field[1:], tracer_field[-1:]], axis=0)
    return (1.0 - fraction)[:, :, None] * tracer_field + fraction[:, :, None] * level_above


def diffuse(tracer_field, kappa):
    levels = tracer_field.shape[0]
    face_kappa = 0.5 * (kappa[:-1] + kappa[1:])
    zero_face = jnp.zeros_like(kappa[:1])
    face_below = jnp.concatenate([zero_face, face_kappa], axis=0)
    face_above = jnp.concatenate([face_kappa, zero_face], axis=0)
    ratio_prev = jnp.zeros_like(kappa[0])
    solved_prev = jnp.zeros_like(tracer_field[0])
    ratios = []
    solveds = []
    for level_index in range(levels):
        below = face_below[level_index]
        above = face_above[level_index]
        pivot_value = 1.0 + below + above + below * ratio_prev
        ratio_now = -above / pivot_value
        solved_now = (tracer_field[level_index] + below[:, None] * solved_prev) / pivot_value[
            :, None
        ]
        ratios.append(ratio_now)
        solveds.append(solved_now)
        ratio_prev = ratio_now
        solved_prev = solved_now
    results = [None] * levels
    results[levels - 1] = solveds[levels - 1]
    for level_index in range(levels - 2, -1, -1):
        results[level_index] = (
            solveds[level_index] - ratios[level_index][:, None] * results[level_index + 1]
        )
    return jnp.stack(results, axis=0)


def bit_mask(amount, position):
    return (amount // 2**position % 2 == 1)[:, :, None]


PAIR = 2


def pair_order(cells):
    cols = np.arange(cells * NTR)
    cell, tracer = cols // NTR, cols % NTR
    return (tracer // PAIR) * cells * PAIR + cell * PAIR + tracer % PAIR


def permutation(target, inverse):
    cols = np.arange(target.shape[0])
    if inverse:
        matrix = cols[:, None] == target[None, :]
    else:
        matrix = cols[None, :] == target[:, None]
    return jnp.asarray(matrix.astype(np.float32), dtype=jnp.bfloat16)


def permute_block(block, matrix):
    high = block.astype(jnp.bfloat16)
    rest = block - high.astype(jnp.float32)
    middle = rest.astype(jnp.bfloat16)
    low = (rest - middle.astype(jnp.float32)).astype(jnp.bfloat16)
    total = jnp.dot(high, matrix, preferred_element_type=jnp.float32)
    total = total + jnp.dot(middle, matrix, preferred_element_type=jnp.float32)
    return total + jnp.dot(low, matrix, preferred_element_type=jnp.float32)


CHUNKS = 4
MESH_ID = pl.DeviceIdType.MESH


def greet(count, me, lat):
    barrier = pltpu.get_barrier_semaphore()
    for offset in range(1, count):
        peer = lax.rem(me + offset, count)
        pl.semaphore_signal(barrier, 1, device_id=(peer, lat), device_id_type=MESH_ID)
    return barrier


def neighbours(parts):
    lon = lax.axis_index("lon")
    lat = lax.axis_index("lat")
    bands = lax.axis_size("lat")
    quarter = lon % parts
    inside_up = quarter < parts - 1
    inside_down = quarter > 0
    has_up = jnp.logical_or(inside_up, lat < bands - 1)
    has_down = jnp.logical_or(inside_down, lat > 0)
    up = (jnp.where(inside_up, lon + 1, lon + 1 - parts), jnp.where(inside_up, lat, lat + 1))
    down = (jnp.where(inside_down, lon - 1, lon + parts - 1), jnp.where(inside_down, lat, lat - 1))
    return has_up, up, has_down, down


def entry_kernel(x_ref, matrix_ref, field_ref, below_ref, above_ref, moved, landed, top_stage, bottom_stage,
                 zero_low, zero_high, send_sem, recv_sem, local_sem, halo_send, halo_recv, store_sem,
                 *, src_at, dst_at, parts):
    count = lax.axis_size("lon")
    me = lax.axis_index("lon")
    lat = lax.axis_index("lat")
    levels = x_ref.shape[0]
    rows = landed.shape[1]
    per = levels // CHUNKS
    has_up, up, has_down, down = neighbours(parts)
    barrier = greet(count, me, lat)

    @pl.when(has_up)
    def _():
        pl.semaphore_signal(barrier, 1, device_id=up, device_id_type=MESH_ID)

    @pl.when(has_down)
    def _():
        pl.semaphore_signal(barrier, 1, device_id=down, device_id_type=MESH_ID)

    copies = []
    locals_ = []
    for chunk in range(CHUNKS):
        def body(k, carry):
            moved[k] = permute_block(x_ref[k], matrix_ref[...])
            return carry

        lax.fori_loop(chunk * per, (chunk + 1) * per, body, 0)
        if chunk == 0:
            pl.semaphore_wait(barrier, count - 1 + has_up.astype(jnp.int32) + has_down.astype(jnp.int32))
        part = pl.ds(chunk * per, per)
        for offset in range(1, count):
            peer = lax.rem(me + offset, count)
            copy = pltpu.make_async_remote_copy(
                src_ref=src_at(moved, peer, part),
                dst_ref=dst_at(landed, me, part),
                send_sem=send_sem.at[chunk, offset],
                recv_sem=recv_sem.at[chunk, offset],
                device_id=(peer, lat),
                device_id_type=MESH_ID,
            )
            copy.start()
            copies.append(copy)
        local = pltpu.make_async_copy(src_at(moved, me, part), dst_at(landed, me, part), local_sem.at[chunk])
        local.start()
        locals_.append(local)
    for copy in copies:
        copy.wait_recv()
    for local in locals_:
        local.wait()
    top_stage[...] = landed[:, rows - top_stage.shape[1] :, :]
    bottom_stage[...] = landed[:, : bottom_stage.shape[1], :]
    to_up = pltpu.make_async_remote_copy(
        src_ref=top_stage, dst_ref=below_ref, send_sem=halo_send.at[0], recv_sem=halo_recv.at[0],
        device_id=up, device_id_type=MESH_ID,
    )
    to_down = pltpu.make_async_remote_copy(
        src_ref=bottom_stage, dst_ref=above_ref, send_sem=halo_send.at[1], recv_sem=halo_recv.at[1],
        device_id=down, device_id_type=MESH_ID,
    )

    @pl.when(has_up)
    def _():
        to_up.start()

    @pl.when(has_down)
    def _():
        to_down.start()

    store = pltpu.make_async_copy(landed, field_ref, store_sem.at[0])
    store.start()
    fill_low = pltpu.make_async_copy(zero_low, below_ref, store_sem.at[1])
    fill_high = pltpu.make_async_copy(zero_high, above_ref, store_sem.at[2])

    @pl.when(jnp.logical_not(has_down))
    def _():
        zero_low[...] = jnp.zeros(zero_low.shape, zero_low.dtype)
        fill_low.start()
        fill_low.wait()

    @pl.when(jnp.logical_not(has_up))
    def _():
        zero_high[...] = jnp.zeros(zero_high.shape, zero_high.dtype)
        fill_high.start()
        fill_high.wait()

    store.wait()

    for copy in copies:
        copy.wait_send()

    @pl.when(has_up)
    def _():
        to_up.wait_send()
        to_down.wait_recv()

    @pl.when(has_down)
    def _():
        to_down.wait_send()
        to_up.wait_recv()


def exit_kernel(src_ref, matrix_ref, out_ref, landed, send_sem, recv_sem, local_sem, *, src_at, dst_at):
    count = lax.axis_size("lon")
    me = lax.axis_index("lon")
    lat = lax.axis_index("lat")
    levels = out_ref.shape[0]
    per = levels // CHUNKS
    barrier = greet(count, me, lat)
    pl.semaphore_wait(barrier, count - 1)
    copies = []
    locals_ = []
    for chunk in range(CHUNKS):
        part = pl.ds(chunk * per, per)
        row = []
        for offset in range(1, count):
            peer = lax.rem(me + offset, count)
            copy = pltpu.make_async_remote_copy(
                src_ref=src_at(src_ref, peer, part),
                dst_ref=dst_at(landed, me, part),
                send_sem=send_sem.at[chunk, offset],
                recv_sem=recv_sem.at[chunk, offset],
                device_id=(peer, lat),
                device_id_type=MESH_ID,
            )
            copy.start()
            row.append(copy)
        copies.append(row)
        local = pltpu.make_async_copy(src_at(src_ref, me, part), dst_at(landed, me, part), local_sem.at[chunk])
        local.start()
        locals_.append(local)
    for chunk in range(CHUNKS):
        for copy in copies[chunk]:
            copy.wait_recv()
        locals_[chunk].wait()

        def body(k, carry):
            out_ref[k] = permute_block(landed[k], matrix_ref[...])
            return carry

        lax.fori_loop(chunk * per, (chunk + 1) * per, body, 0)
    for row in copies:
        for copy in row:
            copy.wait_send()


def run_exchange(kernel, operand, matrix, out_shape, src_spec, out_spec, scratch, src_at, dst_at, ident):
    count = lax.axis_size("lon")
    return pl.pallas_call(
        functools.partial(kernel, src_at=src_at, dst_at=dst_at),
        out_shape=jax.ShapeDtypeStruct(out_shape, operand.dtype),
        in_specs=[src_spec, pl.BlockSpec(memory_space=pltpu.VMEM)],
        out_specs=out_spec,
        scratch_shapes=[
            pltpu.VMEM(scratch, operand.dtype),
            pltpu.SemaphoreType.DMA((CHUNKS, count)),
            pltpu.SemaphoreType.DMA((CHUNKS, count)),
            pltpu.SemaphoreType.DMA((CHUNKS,)),
        ],
        compiler_params=pltpu.CompilerParams(collective_id=ident, has_side_effects=True),
    )(operand, matrix)


def to_columns(block):
    levels, rows, width = block.shape
    cells = width // NTR
    devices = lax.axis_size("lon")
    parts = devices // (NTR // PAIR)
    count = rows // parts
    lane = cells * PAIR

    def src_at(ref, peer, part):
        return ref.at[part, pl.ds((peer % parts) * count, count), pl.ds((peer // parts) * lane, lane)]

    def dst_at(ref, sender, part):
        return ref.at[part, :, pl.ds(sender * lane, lane)]

    vmem = pl.BlockSpec(memory_space=pltpu.VMEM)
    hbm = pl.BlockSpec(memory_space=pl.ANY)
    field_shape = (levels, count, devices * lane)
    below_shape = (levels, 2, devices * lane)
    above_shape = (levels, 3, devices * lane)
    return pl.pallas_call(
        functools.partial(entry_kernel, src_at=src_at, dst_at=dst_at, parts=parts),
        out_shape=tuple(jax.ShapeDtypeStruct(shape, block.dtype) for shape in (field_shape, below_shape, above_shape)),
        in_specs=[vmem, vmem],
        out_specs=(hbm, hbm, hbm),
        scratch_shapes=[
            pltpu.VMEM(block.shape, block.dtype),
            pltpu.VMEM(field_shape, block.dtype),
            pltpu.VMEM(below_shape, block.dtype),
            pltpu.VMEM(above_shape, block.dtype),
            pltpu.VMEM(below_shape, block.dtype),
            pltpu.VMEM(above_shape, block.dtype),
            pltpu.SemaphoreType.DMA((CHUNKS, devices)),
            pltpu.SemaphoreType.DMA((CHUNKS, devices)),
            pltpu.SemaphoreType.DMA((CHUNKS,)),
            pltpu.SemaphoreType.DMA((2,)),
            pltpu.SemaphoreType.DMA((2,)),
            pltpu.SemaphoreType.DMA((3,)),
        ],
        compiler_params=pltpu.CompilerParams(collective_id=0, has_side_effects=True),
    )(block, permutation(pair_order(cells), False))


def from_columns(field, rows):
    levels, count, width = field.shape
    devices = lax.axis_size("lon")
    parts = devices // (NTR // PAIR)
    lane = width // devices
    cells = lane // PAIR

    def src_at(ref, peer, part):
        return ref.at[part, :, pl.ds(peer * lane, lane)]

    def dst_at(ref, sender, part):
        return ref.at[part, pl.ds((sender % parts) * count, count), pl.ds((sender // parts) * lane, lane)]

    shape = (levels, rows, cells * NTR)
    return run_exchange(
        exit_kernel, field, permutation(pair_order(cells), True), shape,
        pl.BlockSpec(memory_space=pltpu.VMEM), pl.BlockSpec(memory_space=pltpu.VMEM), shape,
        src_at, dst_at, 1,
    )


def lat_halo(field, width):
    lon_n = lax.axis_size("lon")
    lat_n = lax.axis_size("lat")
    parts = lon_n // (NTR // PAIR)
    up = []
    for b in range(lat_n):
        for l in range(lon_n):
            t, h = l // parts, l % parts
            g = b * parts + h
            if g + 1 < lat_n * parts:
                nb, nh = (g + 1) // parts, (g + 1) % parts
                up.append((l * lat_n + b, (t * parts + nh) * lat_n + nb))
    down = [(d, s) for s, d in up]
    rows = field.shape[1]
    below = lax.ppermute(field[:, rows - width + 1 :], ("lon", "lat"), up)
    above = lax.ppermute(field[:, :width], ("lon", "lat"), down)
    return jnp.concatenate([below[:, :1], below, field, above], axis=1)


def roll_rows(field, shift):
    cells = field.shape[2] // PAIR
    reach = cells // 4
    amount = shift + reach
    current = jnp.roll(field, -PAIR * reach, axis=2)
    for position in range((2 * reach - 1).bit_length()):
        moved = jnp.roll(current, PAIR * 2**position, axis=2)
        current = jnp.where(bit_mask(amount, position), moved, current)
    return current


def lon_cubic(shifted, fraction):
    weights = cubic_weights(fraction)
    taps = [jnp.roll(shifted, PAIR * (1 - p), axis=2) for p in range(4)]
    summed = None
    for p in range(4):
        addend = weights[p][:, :, None] * taps[p]
        summed = addend if summed is None else summed + addend
    return summed


def own_rows(values, count):
    parts = lax.axis_size("lon") // (NTR // PAIR)
    start = (lax.axis_index("lon") % parts) * count
    return lax.dynamic_slice_in_dim(values, start, count, axis=values.ndim - 1)


def per_device(tracers, lon_shift, lon_frac, lat_shift, lat_frac, remap_frac, diffusivity):
    rows = tracers.shape[1]
    field, below, above = to_columns(tracers)
    count = field.shape[1]
    width = field.shape[2]
    lon_shift, lon_frac, lat_shift, lat_frac, remap_frac, diffusivity = (
        own_rows(v, count) for v in (lon_shift, lon_frac, lat_shift, lat_frac, remap_frac, diffusivity)
    )
    for time_step in range(STEPS):
        if time_step == 0:
            padded = jnp.concatenate([below[:, :1], below, field, above], axis=1)
        else:
            padded = lat_halo(field, 3)
        field = lat_step(padded, lat_shift[time_step], lat_frac[time_step], count)
        field = lon_cubic(roll_rows(field, lon_shift[time_step]), lon_frac[time_step])
        field = remap(field, remap_frac[time_step])
        field = diffuse(field, diffusivity)
    return from_columns(field, rows)


def solution(mesh):
    in_specs = (
        P(None, "lat", "lon"),
        P(None, None, "lat"),
        P(None, None, "lat"),
        P(None, None, "lat"),
        P(None, None, "lat"),
        P(None, None, "lat"),
        P(None, "lat"),
    )
    out_specs = P(None, "lat", "lon")
    return jax.shard_map(
        per_device, mesh=mesh, in_specs=in_specs, out_specs=out_specs, check_vma=False
    )
```

```python
import functools

import jax
import numpy as np
import jax.numpy as jnp
from jax import lax
from jax.experimental import pallas as pl
from jax.experimental.pallas import tpu as pltpu
from jax.sharding import PartitionSpec as P

NTR = 8
STEPS = 2


def from_behind(x, axis, by):
    peers = lax.axis_size(axis)
    return lax.ppermute(x, axis, [(i, (i + by) % peers) for i in range(peers)])


def with_halo(block, sides, width, periodic):
    for axis, dim in sides:
        count = lax.axis_size(axis)
        forward = [(i, i + 1) for i in range(count - 1)]
        if periodic:
            forward.append((count - 1, 0))
        backward = [(target, source) for source, target in forward]
        low = lax.ppermute(
            lax.slice_in_dim(block, block.shape[dim] - width, None, axis=dim), axis, forward
        )
        high = lax.ppermute(lax.slice_in_dim(block, 0, width, axis=dim), axis, backward)
        block = jnp.concatenate([low, block, high], axis=dim)
    return block


def cubic_weights(fraction):
    w_zero = -fraction * (fraction - 1.0) * (fraction - 2.0) / 6.0
    w_one = (fraction + 1.0) * (fraction - 1.0) * (fraction - 2.0) / 2.0
    w_two = -(fraction + 1.0) * fraction * (fraction - 2.0) / 2.0
    w_three = (fraction + 1.0) * fraction * (fraction - 1.0) / 6.0
    return (w_zero, w_one, w_two, w_three)


def lat_step(padded, offset, fraction, row_count, first=1):
    weights = cubic_weights(fraction)
    summed = None
    for place_index in range(6):
        row_delta = place_index - 2
        coeff = jnp.zeros_like(fraction)
        for tap_index in range(4):
            coeff = coeff + jnp.where(offset == tap_index - 1 - row_delta, weights[tap_index], 0.0)
        addend = coeff[:, :, None] * padded[:, first + place_index : first + place_index + row_count, :]
        summed = addend if summed is None else summed + addend
    return summed


def lon_step(wrapped, fraction, tracer_count):
    weights = cubic_weights(fraction)
    width_cols = wrapped.shape[2] - 4 * tracer_count
    summed = None
    for tap_index in range(4):
        offset_cols = (1 + tap_index) * tracer_count
        addend = (
            weights[tap_index][:, :, None] * wrapped[:, :, offset_cols : offset_cols + width_cols]
        )
        summed = addend if summed is None else summed + addend
    return summed


def remap(tracer_field, fraction):
    level_above = jnp.concatenate([tracer_field[1:], tracer_field[-1:]], axis=0)
    return (1.0 - fraction)[:, :, None] * tracer_field + fraction[:, :, None] * level_above


def diffuse(tracer_field, kappa):
    levels = tracer_field.shape[0]
    face_kappa = 0.5 * (kappa[:-1] + kappa[1:])
    zero_face = jnp.zeros_like(kappa[:1])
    face_below = jnp.concatenate([zero_face, face_kappa], axis=0)
    face_above = jnp.concatenate([face_kappa, zero_face], axis=0)
    ratio_prev = jnp.zeros_like(kappa[0])
    solved_prev = jnp.zeros_like(tracer_field[0])
    ratios = []
    solveds = []
    for level_index in range(levels):
        below = face_below[level_index]
        above = face_above[level_index]
        pivot_value = 1.0 + below + above + below * ratio_prev
        ratio_now = -above / pivot_value
        solved_now = (tracer_field[level_index] + below[:, None] * solved_prev) / pivot_value[
            :, None
        ]
        ratios.append(ratio_now)
        solveds.append(solved_now)
        ratio_prev = ratio_now
        solved_prev = solved_now
    results = [None] * levels
    results[levels - 1] = solveds[levels - 1]
    for level_index in range(levels - 2, -1, -1):
        results[level_index] = (
            solveds[level_index] - ratios[level_index][:, None] * results[level_index + 1]
        )
    return jnp.stack(results, axis=0)


def bit_mask(amount, position):
    return (amount // 2**position % 2 == 1)[:, :, None]


PAIR = 2


def pair_order(cells):
    cols = np.arange(cells * NTR)
    cell, tracer = cols // NTR, cols % NTR
    return (tracer // PAIR) * cells * PAIR + cell * PAIR + tracer % PAIR


def permutation(target, inverse):
    cols = np.arange(target.shape[0])
    if inverse:
        matrix = cols[:, None] == target[None, :]
    else:
        matrix = cols[None, :] == target[:, None]
    return jnp.asarray(matrix.astype(np.float32), dtype=jnp.bfloat16)


def permute_block(block, matrix):
    high = block.astype(jnp.bfloat16)
    rest = block - high.astype(jnp.float32)
    middle = rest.astype(jnp.bfloat16)
    low = (rest - middle.astype(jnp.float32)).astype(jnp.bfloat16)
    total = jnp.dot(high, matrix, preferred_element_type=jnp.float32)
    total = total + jnp.dot(middle, matrix, preferred_element_type=jnp.float32)
    return total + jnp.dot(low, matrix, preferred_element_type=jnp.float32)


CHUNKS = 4
MESH_ID = pl.DeviceIdType.MESH


def greet(count, me, lat):
    barrier = pltpu.get_barrier_semaphore()
    for offset in range(1, count):
        peer = lax.rem(me + offset, count)
        pl.semaphore_signal(barrier, 1, device_id=(peer, lat), device_id_type=MESH_ID)
    return barrier


def neighbours(parts):
    lon = lax.axis_index("lon")
    lat = lax.axis_index("lat")
    bands = lax.axis_size("lat")
    quarter = lon % parts
    inside_up = quarter < parts - 1
    inside_down = quarter > 0
    has_up = jnp.logical_or(inside_up, lat < bands - 1)
    has_down = jnp.logical_or(inside_down, lat > 0)
    up = (jnp.where(inside_up, lon + 1, lon + 1 - parts), jnp.where(inside_up, lat, lat + 1))
    down = (jnp.where(inside_down, lon - 1, lon + parts - 1), jnp.where(inside_down, lat, lat - 1))
    return has_up, up, has_down, down


TOP = 8


def entry_padded(x_ref, matrix_ref, padded_ref, *scratch, **kw):
    rows = scratch[1].shape[1]
    low, high = scratch[4].shape[1], scratch[5].shape[1]
    entry_kernel(
        x_ref, matrix_ref,
        padded_ref.at[:, pl.ds(TOP, rows), :],
        padded_ref.at[:, pl.ds(TOP - low, low), :],
        padded_ref.at[:, pl.ds(TOP + rows, high), :],
        *scratch, **kw,
    )


def entry_kernel(x_ref, matrix_ref, field_ref, below_ref, above_ref, moved, landed, top_stage, bottom_stage,
                 zero_low, zero_high, send_sem, recv_sem, local_sem, halo_send, halo_recv, store_sem,
                 *, src_at, dst_at, parts):
    count = lax.axis_size("lon")
    me = lax.axis_index("lon")
    lat = lax.axis_index("lat")
    levels = x_ref.shape[0]
    rows = landed.shape[1]
    per = levels // CHUNKS
    has_up, up, has_down, down = neighbours(parts)
    barrier = greet(count, me, lat)

    @pl.when(has_up)
    def _():
        pl.semaphore_signal(barrier, 1, device_id=up, device_id_type=MESH_ID)

    @pl.when(has_down)
    def _():
        pl.semaphore_signal(barrier, 1, device_id=down, device_id_type=MESH_ID)

    copies = []
    locals_ = []
    for chunk in range(CHUNKS):
        def body(k, carry):
            moved[k] = permute_block(x_ref[k], matrix_ref[...])
            return carry

        lax.fori_loop(chunk * per, (chunk + 1) * per, body, 0)
        if chunk == 0:
            pl.semaphore_wait(barrier, count - 1 + has_up.astype(jnp.int32) + has_down.astype(jnp.int32))
        part = pl.ds(chunk * per, per)
        for offset in range(1, count):
            peer = lax.rem(me + offset, count)
            copy = pltpu.make_async_remote_copy(
                src_ref=src_at(moved, peer, part),
                dst_ref=dst_at(landed, me, part),
                send_sem=send_sem.at[chunk, offset],
                recv_sem=recv_sem.at[chunk, offset],
                device_id=(peer, lat),
                device_id_type=MESH_ID,
            )
            copy.start()
            copies.append(copy)
        local = pltpu.make_async_copy(src_at(moved, me, part), dst_at(landed, me, part), local_sem.at[chunk])
        local.start()
        locals_.append(local)
    for copy in copies:
        copy.wait_recv()
    for local in locals_:
        local.wait()
    top_stage[...] = landed[:, rows - top_stage.shape[1] :, :]
    bottom_stage[...] = landed[:, : bottom_stage.shape[1], :]
    to_up = pltpu.make_async_remote_copy(
        src_ref=top_stage, dst_ref=below_ref, send_sem=halo_send.at[0], recv_sem=halo_recv.at[0],
        device_id=up, device_id_type=MESH_ID,
    )
    to_down = pltpu.make_async_remote_copy(
        src_ref=bottom_stage, dst_ref=above_ref, send_sem=halo_send.at[1], recv_sem=halo_recv.at[1],
        device_id=down, device_id_type=MESH_ID,
    )

    @pl.when(has_up)
    def _():
        to_up.start()

    @pl.when(has_down)
    def _():
        to_down.start()

    store = pltpu.make_async_copy(landed, field_ref, store_sem.at[0])
    store.start()
    fill_low = pltpu.make_async_copy(zero_low, below_ref, store_sem.at[1])
    fill_high = pltpu.make_async_copy(zero_high, above_ref, store_sem.at[2])

    @pl.when(jnp.logical_not(has_down))
    def _():
        zero_low[...] = jnp.zeros(zero_low.shape, zero_low.dtype)
        fill_low.start()
        fill_low.wait()

    @pl.when(jnp.logical_not(has_up))
    def _():
        zero_high[...] = jnp.zeros(zero_high.shape, zero_high.dtype)
        fill_high.start()
        fill_high.wait()

    store.wait()

    for copy in copies:
        copy.wait_send()

    @pl.when(has_up)
    def _():
        to_up.wait_send()
        to_down.wait_recv()

    @pl.when(has_down)
    def _():
        to_down.wait_send()
        to_up.wait_recv()


def exit_kernel(src_ref, matrix_ref, out_ref, landed, send_sem, recv_sem, local_sem, *, src_at, dst_at):
    count = lax.axis_size("lon")
    me = lax.axis_index("lon")
    lat = lax.axis_index("lat")
    levels = out_ref.shape[0]
    per = levels // CHUNKS
    barrier = greet(count, me, lat)
    pl.semaphore_wait(barrier, count - 1)
    copies = []
    locals_ = []
    for chunk in range(CHUNKS):
        part = pl.ds(chunk * per, per)
        row = []
        for offset in range(1, count):
            peer = lax.rem(me + offset, count)
            copy = pltpu.make_async_remote_copy(
                src_ref=src_at(src_ref, peer, part),
                dst_ref=dst_at(landed, me, part),
                send_sem=send_sem.at[chunk, offset],
                recv_sem=recv_sem.at[chunk, offset],
                device_id=(peer, lat),
                device_id_type=MESH_ID,
            )
            copy.start()
            row.append(copy)
        copies.append(row)
        local = pltpu.make_async_copy(src_at(src_ref, me, part), dst_at(landed, me, part), local_sem.at[chunk])
        local.start()
        locals_.append(local)
    for chunk in range(CHUNKS):
        for copy in copies[chunk]:
            copy.wait_recv()
        locals_[chunk].wait()

        def body(k, carry):
            out_ref[k] = permute_block(landed[k], matrix_ref[...])
            return carry

        lax.fori_loop(chunk * per, (chunk + 1) * per, body, 0)
    for row in copies:
        for copy in row:
            copy.wait_send()


def run_exchange(kernel, operand, matrix, out_shape, src_spec, out_spec, scratch, src_at, dst_at, ident):
    count = lax.axis_size("lon")
    return pl.pallas_call(
        functools.partial(kernel, src_at=src_at, dst_at=dst_at),
        out_shape=jax.ShapeDtypeStruct(out_shape, operand.dtype),
        in_specs=[src_spec, pl.BlockSpec(memory_space=pltpu.VMEM)],
        out_specs=out_spec,
        scratch_shapes=[
            pltpu.VMEM(scratch, operand.dtype),
            pltpu.SemaphoreType.DMA((CHUNKS, count)),
            pltpu.SemaphoreType.DMA((CHUNKS, count)),
            pltpu.SemaphoreType.DMA((CHUNKS,)),
        ],
        compiler_params=pltpu.CompilerParams(collective_id=ident, has_side_effects=True),
    )(operand, matrix)


def to_columns(block):
    levels, rows, width = block.shape
    cells = width // NTR
    devices = lax.axis_size("lon")
    parts = devices // (NTR // PAIR)
    count = rows // parts
    lane = cells * PAIR

    def src_at(ref, peer, part):
        return ref.at[part, pl.ds((peer % parts) * count, count), pl.ds((peer // parts) * lane, lane)]

    def dst_at(ref, sender, part):
        return ref.at[part, :, pl.ds(sender * lane, lane)]

    vmem = pl.BlockSpec(memory_space=pltpu.VMEM)
    hbm = pl.BlockSpec(memory_space=pl.ANY)
    field_shape = (levels, count, devices * lane)
    below_shape = (levels, 2, devices * lane)
    above_shape = (levels, 3, devices * lane)
    return pl.pallas_call(
        functools.partial(entry_padded, src_at=src_at, dst_at=dst_at, parts=parts),
        out_shape=jax.ShapeDtypeStruct((levels, 2 * TOP + count, devices * lane), block.dtype),
        in_specs=[vmem, vmem],
        out_specs=hbm,
        scratch_shapes=[
            pltpu.VMEM(block.shape, block.dtype),
            pltpu.VMEM(field_shape, block.dtype),
            pltpu.VMEM(below_shape, block.dtype),
            pltpu.VMEM(above_shape, block.dtype),
            pltpu.VMEM(below_shape, block.dtype),
            pltpu.VMEM(above_shape, block.dtype),
            pltpu.SemaphoreType.DMA((CHUNKS, devices)),
            pltpu.SemaphoreType.DMA((CHUNKS, devices)),
            pltpu.SemaphoreType.DMA((CHUNKS,)),
            pltpu.SemaphoreType.DMA((2,)),
            pltpu.SemaphoreType.DMA((2,)),
            pltpu.SemaphoreType.DMA((3,)),
        ],
        compiler_params=pltpu.CompilerParams(collective_id=0, has_side_effects=True),
    )(block, permutation(pair_order(cells), False))


def from_columns(field, rows):
    levels, count, width = field.shape
    devices = lax.axis_size("lon")
    parts = devices // (NTR // PAIR)
    lane = width // devices
    cells = lane // PAIR

    def src_at(ref, peer, part):
        return ref.at[part, :, pl.ds(peer * lane, lane)]

    def dst_at(ref, sender, part):
        return ref.at[part, pl.ds((sender % parts) * count, count), pl.ds((sender // parts) * lane, lane)]

    shape = (levels, rows, cells * NTR)
    return run_exchange(
        exit_kernel, field, permutation(pair_order(cells), True), shape,
        pl.BlockSpec(memory_space=pl.ANY), pl.BlockSpec(memory_space=pltpu.VMEM), shape,
        src_at, dst_at, 1,
    )


def lat_halo(field, width):
    lon_n = lax.axis_size("lon")
    lat_n = lax.axis_size("lat")
    parts = lon_n // (NTR // PAIR)
    up = []
    for b in range(lat_n):
        for l in range(lon_n):
            t, h = l // parts, l % parts
            g = b * parts + h
            if g + 1 < lat_n * parts:
                nb, nh = (g + 1) // parts, (g + 1) % parts
                up.append((l * lat_n + b, (t * parts + nh) * lat_n + nb))
    down = [(d, s) for s, d in up]
    rows = field.shape[1]
    below = lax.ppermute(field[:, rows - width + 1 :], ("lon", "lat"), up)
    above = lax.ppermute(field[:, :width], ("lon", "lat"), down)
    return jnp.concatenate([below[:, :1], below, field, above], axis=1)


def roll_rows(field, shift):
    cells = field.shape[2] // PAIR
    reach = cells // 4
    amount = shift + reach
    current = jnp.roll(field, -PAIR * reach, axis=2)
    for position in range((2 * reach - 1).bit_length()):
        moved = jnp.roll(current, PAIR * 2**position, axis=2)
        current = jnp.where(bit_mask(amount, position), moved, current)
    return current


def lon_cubic(shifted, fraction):
    weights = cubic_weights(fraction)
    taps = [jnp.roll(shifted, PAIR * (1 - p), axis=2) for p in range(4)]
    summed = None
    for p in range(4):
        addend = weights[p][:, :, None] * taps[p]
        summed = addend if summed is None else summed + addend
    return summed


def own_rows(values, count):
    parts = lax.axis_size("lon") // (NTR // PAIR)
    start = (lax.axis_index("lon") % parts) * count
    return lax.dynamic_slice_in_dim(values, start, count, axis=values.ndim - 1)


def per_device(tracers, lon_shift, lon_frac, lat_shift, lat_frac, remap_frac, diffusivity):
    rows = tracers.shape[1]
    first = to_columns(tracers)
    count = first.shape[1] - 2 * TOP
    field = first[:, TOP : TOP + count]
    width = field.shape[2]
    lon_shift, lon_frac, lat_shift, lat_frac, remap_frac, diffusivity = (
        own_rows(v, count) for v in (lon_shift, lon_frac, lat_shift, lat_frac, remap_frac, diffusivity)
    )
    for time_step in range(STEPS):
        if time_step == 0:
            padded, start = first, TOP - 2
        else:
            padded, start = lat_halo(field, 3), 1
        field = lat_step(padded, lat_shift[time_step], lat_frac[time_step], count, start)
        field = lon_cubic(roll_rows(field, lon_shift[time_step]), lon_frac[time_step])
        field = remap(field, remap_frac[time_step])
        field = diffuse(field, diffusivity)
    return from_columns(field, rows)


def solution(mesh):
    in_specs = (
        P(None, "lat", "lon"),
        P(None, None, "lat"),
        P(None, None, "lat"),
        P(None, None, "lat"),
        P(None, None, "lat"),
        P(None, None, "lat"),
        P(None, "lat"),
    )
    out_specs = P(None, "lat", "lon")
    return jax.shard_map(
        per_device, mesh=mesh, in_specs=in_specs, out_specs=out_specs, check_vma=False
    )
```

```python
import functools

import jax
import numpy as np
import jax.numpy as jnp
from jax import lax
from jax.experimental import pallas as pl
from jax.experimental.pallas import tpu as pltpu
from jax.sharding import PartitionSpec as P

NTR = 8
STEPS = 2


def from_behind(x, axis, by):
    peers = lax.axis_size(axis)
    return lax.ppermute(x, axis, [(i, (i + by) % peers) for i in range(peers)])


def with_halo(block, sides, width, periodic):
    for axis, dim in sides:
        count = lax.axis_size(axis)
        forward = [(i, i + 1) for i in range(count - 1)]
        if periodic:
            forward.append((count - 1, 0))
        backward = [(target, source) for source, target in forward]
        low = lax.ppermute(
            lax.slice_in_dim(block, block.shape[dim] - width, None, axis=dim), axis, forward
        )
        high = lax.ppermute(lax.slice_in_dim(block, 0, width, axis=dim), axis, backward)
        block = jnp.concatenate([low, block, high], axis=dim)
    return block


def cubic_weights(fraction):
    w_zero = -fraction * (fraction - 1.0) * (fraction - 2.0) / 6.0
    w_one = (fraction + 1.0) * (fraction - 1.0) * (fraction - 2.0) / 2.0
    w_two = -(fraction + 1.0) * fraction * (fraction - 2.0) / 2.0
    w_three = (fraction + 1.0) * fraction * (fraction - 1.0) / 6.0
    return (w_zero, w_one, w_two, w_three)


def lat_step(padded, offset, fraction, row_count):
    weights = cubic_weights(fraction)
    summed = None
    for place_index in range(6):
        row_delta = place_index - 2
        coeff = jnp.zeros_like(fraction)
        for tap_index in range(4):
            coeff = coeff + jnp.where(offset == tap_index - 1 - row_delta, weights[tap_index], 0.0)
        addend = coeff[:, :, None] * padded[:, 1 + place_index : 1 + place_index + row_count, :]
        summed = addend if summed is None else summed + addend
    return summed


def lat_split(field, below, above, offset, fraction):
    rows = field.shape[1]
    low, high = below.shape[1], above.shape[1]
    weights = cubic_weights(fraction)
    coeffs = []
    for place_index in range(6):
        row_delta = place_index - 2
        coeff = jnp.zeros_like(fraction)
        for tap_index in range(4):
            coeff = coeff + jnp.where(offset == tap_index - 1 - row_delta, weights[tap_index], 0.0)
        coeffs.append(coeff)
    padded = jnp.pad(field, ((0, 0), (low, high), (0, 0)))
    summed = None
    for place_index in range(6):
        addend = coeffs[place_index][:, :, None] * padded[:, place_index : place_index + rows, :]
        summed = addend if summed is None else summed + addend
    low_fix = []
    for row in range(low):
        total = None
        for place_index in range(low - row):
            term = coeffs[place_index][:, row, None] * below[:, row + place_index]
            total = term if total is None else total + term
        low_fix.append(total)
    high_fix = []
    for row in range(rows - high, rows):
        total = None
        for place_index in range(6):
            source = row + place_index - low - rows
            if 0 <= source < high:
                term = coeffs[place_index][:, row, None] * above[:, source]
                total = term if total is None else total + term
        high_fix.append(total)
    summed = summed.at[:, :low].add(jnp.stack(low_fix, axis=1))
    return summed.at[:, rows - high :].add(jnp.stack(high_fix, axis=1))


def lon_step(wrapped, fraction, tracer_count):
    weights = cubic_weights(fraction)
    width_cols = wrapped.shape[2] - 4 * tracer_count
    summed = None
    for tap_index in range(4):
        offset_cols = (1 + tap_index) * tracer_count
        addend = (
            weights[tap_index][:, :, None] * wrapped[:, :, offset_cols : offset_cols + width_cols]
        )
        summed = addend if summed is None else summed + addend
    return summed


def remap(tracer_field, fraction):
    level_above = jnp.concatenate([tracer_field[1:], tracer_field[-1:]], axis=0)
    return (1.0 - fraction)[:, :, None] * tracer_field + fraction[:, :, None] * level_above


def diffuse(tracer_field, kappa):
    levels = tracer_field.shape[0]
    face_kappa = 0.5 * (kappa[:-1] + kappa[1:])
    zero_face = jnp.zeros_like(kappa[:1])
    face_below = jnp.concatenate([zero_face, face_kappa], axis=0)
    face_above = jnp.concatenate([face_kappa, zero_face], axis=0)
    ratio_prev = jnp.zeros_like(kappa[0])
    solved_prev = jnp.zeros_like(tracer_field[0])
    ratios = []
    solveds = []
    for level_index in range(levels):
        below = face_below[level_index]
        above = face_above[level_index]
        pivot_value = 1.0 + below + above + below * ratio_prev
        ratio_now = -above / pivot_value
        solved_now = (tracer_field[level_index] + below[:, None] * solved_prev) / pivot_value[
            :, None
        ]
        ratios.append(ratio_now)
        solveds.append(solved_now)
        ratio_prev = ratio_now
        solved_prev = solved_now
    results = [None] * levels
    results[levels - 1] = solveds[levels - 1]
    for level_index in range(levels - 2, -1, -1):
        results[level_index] = (
            solveds[level_index] - ratios[level_index][:, None] * results[level_index + 1]
        )
    return jnp.stack(results, axis=0)


def bit_mask(amount, position):
    return (amount // 2**position % 2 == 1)[:, :, None]


PAIR = 2


def pair_order(cells):
    cols = np.arange(cells * NTR)
    cell, tracer = cols // NTR, cols % NTR
    return (tracer // PAIR) * cells * PAIR + cell * PAIR + tracer % PAIR


def permutation(target, inverse):
    cols = np.arange(target.shape[0])
    if inverse:
        matrix = cols[:, None] == target[None, :]
    else:
        matrix = cols[None, :] == target[:, None]
    return jnp.asarray(matrix.astype(np.float32), dtype=jnp.bfloat16)


def permute_block(block, matrix):
    high = block.astype(jnp.bfloat16)
    rest = block - high.astype(jnp.float32)
    middle = rest.astype(jnp.bfloat16)
    low = (rest - middle.astype(jnp.float32)).astype(jnp.bfloat16)
    total = jnp.dot(high, matrix, preferred_element_type=jnp.float32)
    total = total + jnp.dot(middle, matrix, preferred_element_type=jnp.float32)
    return total + jnp.dot(low, matrix, preferred_element_type=jnp.float32)


CHUNKS = 4
MESH_ID = pl.DeviceIdType.MESH


def greet(count, me, lat):
    barrier = pltpu.get_barrier_semaphore()
    for offset in range(1, count):
        peer = lax.rem(me + offset, count)
        pl.semaphore_signal(barrier, 1, device_id=(peer, lat), device_id_type=MESH_ID)
    return barrier


def neighbours(parts):
    lon = lax.axis_index("lon")
    lat = lax.axis_index("lat")
    bands = lax.axis_size("lat")
    quarter = lon % parts
    inside_up = quarter < parts - 1
    inside_down = quarter > 0
    has_up = jnp.logical_or(inside_up, lat < bands - 1)
    has_down = jnp.logical_or(inside_down, lat > 0)
    up = (jnp.where(inside_up, lon + 1, lon + 1 - parts), jnp.where(inside_up, lat, lat + 1))
    down = (jnp.where(inside_down, lon - 1, lon + parts - 1), jnp.where(inside_down, lat, lat - 1))
    return has_up, up, has_down, down


def entry_kernel(x_ref, matrix_ref, field_ref, below_ref, above_ref, moved, landed, top_stage, bottom_stage,
                 zero_low, zero_high, send_sem, recv_sem, local_sem, halo_send, halo_recv, store_sem,
                 *, src_at, dst_at, parts):
    count = lax.axis_size("lon")
    me = lax.axis_index("lon")
    lat = lax.axis_index("lat")
    levels = x_ref.shape[0]
    rows = landed.shape[1]
    per = levels // CHUNKS
    has_up, up, has_down, down = neighbours(parts)
    barrier = greet(count, me, lat)

    @pl.when(has_up)
    def _():
        pl.semaphore_signal(barrier, 1, device_id=up, device_id_type=MESH_ID)

    @pl.when(has_down)
    def _():
        pl.semaphore_signal(barrier, 1, device_id=down, device_id_type=MESH_ID)

    copies = []
    locals_ = []
    for chunk in range(CHUNKS):
        def body(k, carry):
            moved[k] = permute_block(x_ref[k], matrix_ref[...])
            return carry

        lax.fori_loop(chunk * per, (chunk + 1) * per, body, 0)
        if chunk == 0:
            pl.semaphore_wait(barrier, count - 1 + has_up.astype(jnp.int32) + has_down.astype(jnp.int32))
        part = pl.ds(chunk * per, per)
        for offset in range(1, count):
            peer = lax.rem(me + offset, count)
            copy = pltpu.make_async_remote_copy(
                src_ref=src_at(moved, peer, part),
                dst_ref=dst_at(landed, me, part),
                send_sem=send_sem.at[chunk, offset],
                recv_sem=recv_sem.at[chunk, offset],
                device_id=(peer, lat),
                device_id_type=MESH_ID,
            )
            copy.start()
            copies.append(copy)
        local = pltpu.make_async_copy(src_at(moved, me, part), dst_at(landed, me, part), local_sem.at[chunk])
        local.start()
        locals_.append(local)
    for copy in copies:
        copy.wait_recv()
    for local in locals_:
        local.wait()
    top_stage[...] = landed[:, rows - top_stage.shape[1] :, :]
    bottom_stage[...] = landed[:, : bottom_stage.shape[1], :]
    to_up = pltpu.make_async_remote_copy(
        src_ref=top_stage, dst_ref=below_ref, send_sem=halo_send.at[0], recv_sem=halo_recv.at[0],
        device_id=up, device_id_type=MESH_ID,
    )
    to_down = pltpu.make_async_remote_copy(
        src_ref=bottom_stage, dst_ref=above_ref, send_sem=halo_send.at[1], recv_sem=halo_recv.at[1],
        device_id=down, device_id_type=MESH_ID,
    )

    @pl.when(has_up)
    def _():
        to_up.start()

    @pl.when(has_down)
    def _():
        to_down.start()

    store = pltpu.make_async_copy(landed, field_ref, store_sem.at[0])
    store.start()
    fill_low = pltpu.make_async_copy(zero_low, below_ref, store_sem.at[1])
    fill_high = pltpu.make_async_copy(zero_high, above_ref, store_sem.at[2])

    @pl.when(jnp.logical_not(has_down))
    def _():
        zero_low[...] = jnp.zeros(zero_low.shape, zero_low.dtype)
        fill_low.start()
        fill_low.wait()

    @pl.when(jnp.logical_not(has_up))
    def _():
        zero_high[...] = jnp.zeros(zero_high.shape, zero_high.dtype)
        fill_high.start()
        fill_high.wait()

    store.wait()

    for copy in copies:
        copy.wait_send()

    @pl.when(has_up)
    def _():
        to_up.wait_send()
        to_down.wait_recv()

    @pl.when(has_down)
    def _():
        to_down.wait_send()
        to_up.wait_recv()


def exit_kernel(src_ref, matrix_ref, out_ref, landed, send_sem, recv_sem, local_sem, *, src_at, dst_at):
    count = lax.axis_size("lon")
    me = lax.axis_index("lon")
    lat = lax.axis_index("lat")
    levels = out_ref.shape[0]
    per = levels // CHUNKS
    barrier = greet(count, me, lat)
    pl.semaphore_wait(barrier, count - 1)
    copies = []
    locals_ = []
    for chunk in range(CHUNKS):
        part = pl.ds(chunk * per, per)
        row = []
        for offset in range(1, count):
            peer = lax.rem(me + offset, count)
            copy = pltpu.make_async_remote_copy(
                src_ref=src_at(src_ref, peer, part),
                dst_ref=dst_at(landed, me, part),
                send_sem=send_sem.at[chunk, offset],
                recv_sem=recv_sem.at[chunk, offset],
                device_id=(peer, lat),
                device_id_type=MESH_ID,
            )
            copy.start()
            row.append(copy)
        copies.append(row)
        local = pltpu.make_async_copy(src_at(src_ref, me, part), dst_at(landed, me, part), local_sem.at[chunk])
        local.start()
        locals_.append(local)
    for chunk in range(CHUNKS):
        for copy in copies[chunk]:
            copy.wait_recv()
        locals_[chunk].wait()

        def body(k, carry):
            out_ref[k] = permute_block(landed[k], matrix_ref[...])
            return carry

        lax.fori_loop(chunk * per, (chunk + 1) * per, body, 0)
    for row in copies:
        for copy in row:
            copy.wait_send()


def run_exchange(kernel, operand, matrix, out_shape, src_spec, out_spec, scratch, src_at, dst_at, ident):
    count = lax.axis_size("lon")
    return pl.pallas_call(
        functools.partial(kernel, src_at=src_at, dst_at=dst_at),
        out_shape=jax.ShapeDtypeStruct(out_shape, operand.dtype),
        in_specs=[src_spec, pl.BlockSpec(memory_space=pltpu.VMEM)],
        out_specs=out_spec,
        scratch_shapes=[
            pltpu.VMEM(scratch, operand.dtype),
            pltpu.SemaphoreType.DMA((CHUNKS, count)),
            pltpu.SemaphoreType.DMA((CHUNKS, count)),
            pltpu.SemaphoreType.DMA((CHUNKS,)),
        ],
        compiler_params=pltpu.CompilerParams(collective_id=ident, has_side_effects=True),
    )(operand, matrix)


def to_columns(block):
    levels, rows, width = block.shape
    cells = width // NTR
    devices = lax.axis_size("lon")
    parts = devices // (NTR // PAIR)
    count = rows // parts
    lane = cells * PAIR

    def src_at(ref, peer, part):
        return ref.at[part, pl.ds((peer % parts) * count, count), pl.ds((peer // parts) * lane, lane)]

    def dst_at(ref, sender, part):
        return ref.at[part, :, pl.ds(sender * lane, lane)]

    vmem = pl.BlockSpec(memory_space=pltpu.VMEM)
    hbm = pl.BlockSpec(memory_space=pl.ANY)
    field_shape = (levels, count, devices * lane)
    below_shape = (levels, 2, devices * lane)
    above_shape = (levels, 3, devices * lane)
    return pl.pallas_call(
        functools.partial(entry_kernel, src_at=src_at, dst_at=dst_at, parts=parts),
        out_shape=tuple(jax.ShapeDtypeStruct(shape, block.dtype) for shape in (field_shape, below_shape, above_shape)),
        in_specs=[vmem, vmem],
        out_specs=(hbm, hbm, hbm),
        scratch_shapes=[
            pltpu.VMEM(block.shape, block.dtype),
            pltpu.VMEM(field_shape, block.dtype),
            pltpu.VMEM(below_shape, block.dtype),
            pltpu.VMEM(above_shape, block.dtype),
            pltpu.VMEM(below_shape, block.dtype),
            pltpu.VMEM(above_shape, block.dtype),
            pltpu.SemaphoreType.DMA((CHUNKS, devices)),
            pltpu.SemaphoreType.DMA((CHUNKS, devices)),
            pltpu.SemaphoreType.DMA((CHUNKS,)),
            pltpu.SemaphoreType.DMA((2,)),
            pltpu.SemaphoreType.DMA((2,)),
            pltpu.SemaphoreType.DMA((3,)),
        ],
        compiler_params=pltpu.CompilerParams(collective_id=0, has_side_effects=True),
    )(block, permutation(pair_order(cells), False))


def from_columns(field, rows):
    levels, count, width = field.shape
    devices = lax.axis_size("lon")
    parts = devices // (NTR // PAIR)
    lane = width // devices
    cells = lane // PAIR

    def src_at(ref, peer, part):
        return ref.at[part, :, pl.ds(peer * lane, lane)]

    def dst_at(ref, sender, part):
        return ref.at[part, pl.ds((sender % parts) * count, count), pl.ds((sender // parts) * lane, lane)]

    shape = (levels, rows, cells * NTR)
    return run_exchange(
        exit_kernel, field, permutation(pair_order(cells), True), shape,
        pl.BlockSpec(memory_space=pl.ANY), pl.BlockSpec(memory_space=pltpu.VMEM), shape,
        src_at, dst_at, 1,
    )


def lat_halo(field, width):
    lon_n = lax.axis_size("lon")
    lat_n = lax.axis_size("lat")
    parts = lon_n // (NTR // PAIR)
    up = []
    for b in range(lat_n):
        for l in range(lon_n):
            t, h = l // parts, l % parts
            g = b * parts + h
            if g + 1 < lat_n * parts:
                nb, nh = (g + 1) // parts, (g + 1) % parts
                up.append((l * lat_n + b, (t * parts + nh) * lat_n + nb))
    down = [(d, s) for s, d in up]
    rows = field.shape[1]
    below = lax.ppermute(field[:, rows - width + 1 :], ("lon", "lat"), up)
    above = lax.ppermute(field[:, :width], ("lon", "lat"), down)
    return jnp.concatenate([below[:, :1], below, field, above], axis=1)


def roll_rows(field, shift):
    cells = field.shape[2] // PAIR
    reach = cells // 4
    amount = shift + reach
    current = jnp.roll(field, -PAIR * reach, axis=2)
    for position in range((2 * reach - 1).bit_length()):
        moved = jnp.roll(current, PAIR * 2**position, axis=2)
        current = jnp.where(bit_mask(amount, position), moved, current)
    return current


def lon_cubic(shifted, fraction):
    weights = cubic_weights(fraction)
    taps = [jnp.roll(shifted, PAIR * (1 - p), axis=2) for p in range(4)]
    summed = None
    for p in range(4):
        addend = weights[p][:, :, None] * taps[p]
        summed = addend if summed is None else summed + addend
    return summed


def own_rows(values, count):
    parts = lax.axis_size("lon") // (NTR // PAIR)
    start = (lax.axis_index("lon") % parts) * count
    return lax.dynamic_slice_in_dim(values, start, count, axis=values.ndim - 1)


def per_device(tracers, lon_shift, lon_frac, lat_shift, lat_frac, remap_frac, diffusivity):
    rows = tracers.shape[1]
    field, below, above = to_columns(tracers)
    count = field.shape[1]
    width = field.shape[2]
    lon_shift, lon_frac, lat_shift, lat_frac, remap_frac, diffusivity = (
        own_rows(v, count) for v in (lon_shift, lon_frac, lat_shift, lat_frac, remap_frac, diffusivity)
    )
    for time_step in range(STEPS):
        if time_step == 0:
            field = lat_split(field, below, above, lat_shift[time_step], lat_frac[time_step])
        else:
            padded = lat_halo(field, 3)
            field = lat_step(padded, lat_shift[time_step], lat_frac[time_step], count)
        field = lon_cubic(roll_rows(field, lon_shift[time_step]), lon_frac[time_step])
        field = remap(field, remap_frac[time_step])
        field = diffuse(field, diffusivity)
    return from_columns(field, rows)


def solution(mesh):
    in_specs = (
        P(None, "lat", "lon"),
        P(None, None, "lat"),
        P(None, None, "lat"),
        P(None, None, "lat"),
        P(None, None, "lat"),
        P(None, None, "lat"),
        P(None, "lat"),
    )
    out_specs = P(None, "lat", "lon")
    return jax.shard_map(
        per_device, mesh=mesh, in_specs=in_specs, out_specs=out_specs, check_vma=False
    )
```

```python
import functools

import jax
import numpy as np
import jax.numpy as jnp
from jax import lax
from jax.experimental import pallas as pl
from jax.experimental.pallas import tpu as pltpu
from jax.sharding import PartitionSpec as P

NTR = 8
STEPS = 2


def from_behind(x, axis, by):
    peers = lax.axis_size(axis)
    return lax.ppermute(x, axis, [(i, (i + by) % peers) for i in range(peers)])


def with_halo(block, sides, width, periodic):
    for axis, dim in sides:
        count = lax.axis_size(axis)
        forward = [(i, i + 1) for i in range(count - 1)]
        if periodic:
            forward.append((count - 1, 0))
        backward = [(target, source) for source, target in forward]
        low = lax.ppermute(
            lax.slice_in_dim(block, block.shape[dim] - width, None, axis=dim), axis, forward
        )
        high = lax.ppermute(lax.slice_in_dim(block, 0, width, axis=dim), axis, backward)
        block = jnp.concatenate([low, block, high], axis=dim)
    return block


def cubic_weights(fraction):
    w_zero = -fraction * (fraction - 1.0) * (fraction - 2.0) / 6.0
    w_one = (fraction + 1.0) * (fraction - 1.0) * (fraction - 2.0) / 2.0
    w_two = -(fraction + 1.0) * fraction * (fraction - 2.0) / 2.0
    w_three = (fraction + 1.0) * fraction * (fraction - 1.0) / 6.0
    return (w_zero, w_one, w_two, w_three)


def lat_step(padded, offset, fraction, row_count, first=1):
    weights = cubic_weights(fraction)
    summed = None
    for place_index in range(6):
        row_delta = place_index - 2
        coeff = jnp.zeros_like(fraction)
        for tap_index in range(4):
            coeff = coeff + jnp.where(offset == tap_index - 1 - row_delta, weights[tap_index], 0.0)
        addend = coeff[:, :, None] * padded[:, first + place_index : first + place_index + row_count, :]
        summed = addend if summed is None else summed + addend
    return summed


def lon_step(wrapped, fraction, tracer_count):
    weights = cubic_weights(fraction)
    width_cols = wrapped.shape[2] - 4 * tracer_count
    summed = None
    for tap_index in range(4):
        offset_cols = (1 + tap_index) * tracer_count
        addend = (
            weights[tap_index][:, :, None] * wrapped[:, :, offset_cols : offset_cols + width_cols]
        )
        summed = addend if summed is None else summed + addend
    return summed


def remap(tracer_field, fraction):
    level_above = jnp.concatenate([tracer_field[1:], tracer_field[-1:]], axis=0)
    return (1.0 - fraction)[:, :, None] * tracer_field + fraction[:, :, None] * level_above


def diffuse(tracer_field, kappa):
    levels = tracer_field.shape[0]
    face_kappa = 0.5 * (kappa[:-1] + kappa[1:])
    zero_face = jnp.zeros_like(kappa[:1])
    face_below = jnp.concatenate([zero_face, face_kappa], axis=0)
    face_above = jnp.concatenate([face_kappa, zero_face], axis=0)
    ratio_prev = jnp.zeros_like(kappa[0])
    solved_prev = jnp.zeros_like(tracer_field[0])
    ratios = []
    solveds = []
    for level_index in range(levels):
        below = face_below[level_index]
        above = face_above[level_index]
        pivot_value = 1.0 + below + above + below * ratio_prev
        ratio_now = -above / pivot_value
        solved_now = (tracer_field[level_index] + below[:, None] * solved_prev) / pivot_value[
            :, None
        ]
        ratios.append(ratio_now)
        solveds.append(solved_now)
        ratio_prev = ratio_now
        solved_prev = solved_now
    results = [None] * levels
    results[levels - 1] = solveds[levels - 1]
    for level_index in range(levels - 2, -1, -1):
        results[level_index] = (
            solveds[level_index] - ratios[level_index][:, None] * results[level_index + 1]
        )
    return jnp.stack(results, axis=0)


def bit_mask(amount, position):
    return (amount // 2**position % 2 == 1)[:, :, None]


PAIR = 2


def pair_order(cells):
    cols = np.arange(cells * NTR)
    cell, tracer = cols // NTR, cols % NTR
    return (tracer // PAIR) * cells * PAIR + cell * PAIR + tracer % PAIR


def permutation(target, inverse):
    cols = np.arange(target.shape[0])
    if inverse:
        matrix = cols[:, None] == target[None, :]
    else:
        matrix = cols[None, :] == target[:, None]
    return jnp.asarray(matrix.astype(np.float32), dtype=jnp.bfloat16)


def permute_block(block, matrix):
    high = block.astype(jnp.bfloat16)
    rest = block - high.astype(jnp.float32)
    middle = rest.astype(jnp.bfloat16)
    low = (rest - middle.astype(jnp.float32)).astype(jnp.bfloat16)
    total = jnp.dot(high, matrix, preferred_element_type=jnp.float32)
    total = total + jnp.dot(middle, matrix, preferred_element_type=jnp.float32)
    return total + jnp.dot(low, matrix, preferred_element_type=jnp.float32)


CHUNKS = 4
MESH_ID = pl.DeviceIdType.MESH


def greet(count, me, lat):
    barrier = pltpu.get_barrier_semaphore()
    for offset in range(1, count):
        peer = lax.rem(me + offset, count)
        pl.semaphore_signal(barrier, 1, device_id=(peer, lat), device_id_type=MESH_ID)
    return barrier


def neighbours(parts):
    lon = lax.axis_index("lon")
    lat = lax.axis_index("lat")
    bands = lax.axis_size("lat")
    quarter = lon % parts
    inside_up = quarter < parts - 1
    inside_down = quarter > 0
    has_up = jnp.logical_or(inside_up, lat < bands - 1)
    has_down = jnp.logical_or(inside_down, lat > 0)
    up = (jnp.where(inside_up, lon + 1, lon + 1 - parts), jnp.where(inside_up, lat, lat + 1))
    down = (jnp.where(inside_down, lon - 1, lon + parts - 1), jnp.where(inside_down, lat, lat - 1))
    return has_up, up, has_down, down


def entry_kernel(x_ref, matrix_ref, field_ref, below_ref, above_ref, moved, landed, top_stage, bottom_stage,
                 zero_low, zero_high, send_sem, recv_sem, local_sem, halo_send, halo_recv, store_sem,
                 *, src_at, dst_at, parts):
    count = lax.axis_size("lon")
    me = lax.axis_index("lon")
    lat = lax.axis_index("lat")
    levels = x_ref.shape[0]
    rows = landed.shape[1]
    per = levels // CHUNKS
    has_up, up, has_down, down = neighbours(parts)
    barrier = greet(count, me, lat)

    @pl.when(has_up)
    def _():
        pl.semaphore_signal(barrier, 1, device_id=up, device_id_type=MESH_ID)

    @pl.when(has_down)
    def _():
        pl.semaphore_signal(barrier, 1, device_id=down, device_id_type=MESH_ID)

    copies = []
    locals_ = []
    for chunk in range(CHUNKS):
        def body(k, carry):
            moved[k] = permute_block(x_ref[k], matrix_ref[...])
            return carry

        lax.fori_loop(chunk * per, (chunk + 1) * per, body, 0)
        if chunk == 0:
            pl.semaphore_wait(barrier, count - 1 + has_up.astype(jnp.int32) + has_down.astype(jnp.int32))
        part = pl.ds(chunk * per, per)
        for offset in range(1, count):
            peer = lax.rem(me + offset, count)
            copy = pltpu.make_async_remote_copy(
                src_ref=src_at(moved, peer, part),
                dst_ref=dst_at(landed, me, part),
                send_sem=send_sem.at[chunk, offset],
                recv_sem=recv_sem.at[chunk, offset],
                device_id=(peer, lat),
                device_id_type=MESH_ID,
            )
            copy.start()
            copies.append(copy)
        local = pltpu.make_async_copy(src_at(moved, me, part), dst_at(landed, me, part), local_sem.at[chunk])
        local.start()
        locals_.append(local)
    for copy in copies:
        copy.wait_recv()
    for local in locals_:
        local.wait()
    top_stage[...] = landed[:, rows - top_stage.shape[1] :, :]
    bottom_stage[...] = landed[:, : bottom_stage.shape[1], :]
    to_up = pltpu.make_async_remote_copy(
        src_ref=top_stage, dst_ref=below_ref, send_sem=halo_send.at[0], recv_sem=halo_recv.at[0],
        device_id=up, device_id_type=MESH_ID,
    )
    to_down = pltpu.make_async_remote_copy(
        src_ref=bottom_stage, dst_ref=above_ref, send_sem=halo_send.at[1], recv_sem=halo_recv.at[1],
        device_id=down, device_id_type=MESH_ID,
    )

    @pl.when(has_up)
    def _():
        to_up.start()

    @pl.when(has_down)
    def _():
        to_down.start()

    store = pltpu.make_async_copy(landed, field_ref, store_sem.at[0])
    store.start()
    fill_low = pltpu.make_async_copy(zero_low, below_ref, store_sem.at[1])
    fill_high = pltpu.make_async_copy(zero_high, above_ref, store_sem.at[2])

    @pl.when(jnp.logical_not(has_down))
    def _():
        zero_low[...] = jnp.zeros(zero_low.shape, zero_low.dtype)
        fill_low.start()
        fill_low.wait()

    @pl.when(jnp.logical_not(has_up))
    def _():
        zero_high[...] = jnp.zeros(zero_high.shape, zero_high.dtype)
        fill_high.start()
        fill_high.wait()

    store.wait()

    for copy in copies:
        copy.wait_send()

    @pl.when(has_up)
    def _():
        to_up.wait_send()
        to_down.wait_recv()

    @pl.when(has_down)
    def _():
        to_down.wait_send()
        to_up.wait_recv()


def exit_kernel(src_ref, matrix_ref, out_ref, landed, send_sem, recv_sem, local_sem, *, src_at, dst_at):
    count = lax.axis_size("lon")
    me = lax.axis_index("lon")
    lat = lax.axis_index("lat")
    levels = out_ref.shape[0]
    per = levels // CHUNKS
    barrier = greet(count, me, lat)
    pl.semaphore_wait(barrier, count - 1)
    copies = []
    locals_ = []
    for chunk in range(CHUNKS):
        part = pl.ds(chunk * per, per)
        row = []
        for offset in range(1, count):
            peer = lax.rem(me + offset, count)
            copy = pltpu.make_async_remote_copy(
                src_ref=src_at(src_ref, peer, part),
                dst_ref=dst_at(landed, me, part),
                send_sem=send_sem.at[chunk, offset],
                recv_sem=recv_sem.at[chunk, offset],
                device_id=(peer, lat),
                device_id_type=MESH_ID,
            )
            copy.start()
            row.append(copy)
        copies.append(row)
        local = pltpu.make_async_copy(src_at(src_ref, me, part), dst_at(landed, me, part), local_sem.at[chunk])
        local.start()
        locals_.append(local)
    for chunk in range(CHUNKS):
        for copy in copies[chunk]:
            copy.wait_recv()
        locals_[chunk].wait()

        def body(k, carry):
            out_ref[k] = permute_block(landed[k], matrix_ref[...])
            return carry

        lax.fori_loop(chunk * per, (chunk + 1) * per, body, 0)
    for row in copies:
        for copy in row:
            copy.wait_send()


def run_exchange(kernel, operand, matrix, out_shape, src_spec, out_spec, scratch, src_at, dst_at, ident):
    count = lax.axis_size("lon")
    return pl.pallas_call(
        functools.partial(kernel, src_at=src_at, dst_at=dst_at),
        out_shape=jax.ShapeDtypeStruct(out_shape, operand.dtype),
        in_specs=[src_spec, pl.BlockSpec(memory_space=pltpu.VMEM)],
        out_specs=out_spec,
        scratch_shapes=[
            pltpu.VMEM(scratch, operand.dtype),
            pltpu.SemaphoreType.DMA((CHUNKS, count)),
            pltpu.SemaphoreType.DMA((CHUNKS, count)),
            pltpu.SemaphoreType.DMA((CHUNKS,)),
        ],
        compiler_params=pltpu.CompilerParams(collective_id=ident, has_side_effects=True),
    )(operand, matrix)


def to_columns(block):
    levels, rows, width = block.shape
    cells = width // NTR
    devices = lax.axis_size("lon")
    parts = devices // (NTR // PAIR)
    count = rows // parts
    lane = cells * PAIR

    def src_at(ref, peer, part):
        return ref.at[part, pl.ds((peer % parts) * count, count), pl.ds((peer // parts) * lane, lane)]

    def dst_at(ref, sender, part):
        return ref.at[part, :, pl.ds(sender * lane, lane)]

    vmem = pl.BlockSpec(memory_space=pltpu.VMEM)
    hbm = pl.BlockSpec(memory_space=pl.ANY)
    field_shape = (levels, count, devices * lane)
    below_shape = (levels, 2, devices * lane)
    above_shape = (levels, 3, devices * lane)
    return pl.pallas_call(
        functools.partial(entry_kernel, src_at=src_at, dst_at=dst_at, parts=parts),
        out_shape=tuple(jax.ShapeDtypeStruct(shape, block.dtype) for shape in (field_shape, below_shape, above_shape)),
        in_specs=[vmem, vmem],
        out_specs=(hbm, hbm, hbm),
        scratch_shapes=[
            pltpu.VMEM(block.shape, block.dtype),
            pltpu.VMEM(field_shape, block.dtype),
            pltpu.VMEM(below_shape, block.dtype),
            pltpu.VMEM(above_shape, block.dtype),
            pltpu.VMEM(below_shape, block.dtype),
            pltpu.VMEM(above_shape, block.dtype),
            pltpu.SemaphoreType.DMA((CHUNKS, devices)),
            pltpu.SemaphoreType.DMA((CHUNKS, devices)),
            pltpu.SemaphoreType.DMA((CHUNKS,)),
            pltpu.SemaphoreType.DMA((2,)),
            pltpu.SemaphoreType.DMA((2,)),
            pltpu.SemaphoreType.DMA((3,)),
        ],
        compiler_params=pltpu.CompilerParams(collective_id=0, has_side_effects=True),
    )(block, permutation(pair_order(cells), False))


def from_columns(field, rows):
    levels, count, width = field.shape
    devices = lax.axis_size("lon")
    parts = devices // (NTR // PAIR)
    lane = width // devices
    cells = lane // PAIR

    def src_at(ref, peer, part):
        return ref.at[part, :, pl.ds(peer * lane, lane)]

    def dst_at(ref, sender, part):
        return ref.at[part, pl.ds((sender % parts) * count, count), pl.ds((sender // parts) * lane, lane)]

    shape = (levels, rows, cells * NTR)
    return run_exchange(
        exit_kernel, field, permutation(pair_order(cells), True), shape,
        pl.BlockSpec(memory_space=pl.ANY), pl.BlockSpec(memory_space=pltpu.VMEM), shape,
        src_at, dst_at, 1,
    )


def lat_halo(field, width):
    lon_n = lax.axis_size("lon")
    lat_n = lax.axis_size("lat")
    parts = lon_n // (NTR // PAIR)
    up = []
    for b in range(lat_n):
        for l in range(lon_n):
            t, h = l // parts, l % parts
            g = b * parts + h
            if g + 1 < lat_n * parts:
                nb, nh = (g + 1) // parts, (g + 1) % parts
                up.append((l * lat_n + b, (t * parts + nh) * lat_n + nb))
    down = [(d, s) for s, d in up]
    rows = field.shape[1]
    below = lax.ppermute(field[:, rows - width + 1 :], ("lon", "lat"), up)
    above = lax.ppermute(field[:, :width], ("lon", "lat"), down)
    return jnp.concatenate([below, field, above], axis=1)


def roll_rows(field, shift):
    cells = field.shape[2] // PAIR
    reach = cells // 4
    amount = shift + reach
    current = jnp.roll(field, -PAIR * reach, axis=2)
    for position in range((2 * reach - 1).bit_length()):
        moved = jnp.roll(current, PAIR * 2**position, axis=2)
        current = jnp.where(bit_mask(amount, position), moved, current)
    return current


def lon_cubic(shifted, fraction):
    weights = cubic_weights(fraction)
    taps = [jnp.roll(shifted, PAIR * (1 - p), axis=2) for p in range(4)]
    summed = None
    for p in range(4):
        addend = weights[p][:, :, None] * taps[p]
        summed = addend if summed is None else summed + addend
    return summed


def own_rows(values, count):
    parts = lax.axis_size("lon") // (NTR // PAIR)
    start = (lax.axis_index("lon") % parts) * count
    return lax.dynamic_slice_in_dim(values, start, count, axis=values.ndim - 1)


def per_device(tracers, lon_shift, lon_frac, lat_shift, lat_frac, remap_frac, diffusivity):
    rows = tracers.shape[1]
    field, below, above = to_columns(tracers)
    count = field.shape[1]
    width = field.shape[2]
    lon_shift, lon_frac, lat_shift, lat_frac, remap_frac, diffusivity = (
        own_rows(v, count) for v in (lon_shift, lon_frac, lat_shift, lat_frac, remap_frac, diffusivity)
    )
    for time_step in range(STEPS):
        if time_step == 0:
            padded = jnp.concatenate([below[:, :1], below, field, above], axis=1)
        else:
            padded = lat_halo(field, 3)
        field = lat_step(padded, lat_shift[time_step], lat_frac[time_step], count, padded.shape[1] - count - 5)
        field = lon_cubic(roll_rows(field, lon_shift[time_step]), lon_frac[time_step])
        field = remap(field, remap_frac[time_step])
        field = diffuse(field, diffusivity)
    return from_columns(field, rows)


def solution(mesh):
    in_specs = (
        P(None, "lat", "lon"),
        P(None, None, "lat"),
        P(None, None, "lat"),
        P(None, None, "lat"),
        P(None, None, "lat"),
        P(None, None, "lat"),
        P(None, "lat"),
    )
    out_specs = P(None, "lat", "lon")
    return jax.shard_map(
        per_device, mesh=mesh, in_specs=in_specs, out_specs=out_specs, check_vma=False
    )
```

```python
import functools

import jax
import numpy as np
import jax.numpy as jnp
from jax import lax
from jax.experimental import pallas as pl
from jax.experimental.pallas import tpu as pltpu
from jax.sharding import PartitionSpec as P

NTR = 8
STEPS = 2


def from_behind(x, axis, by):
    peers = lax.axis_size(axis)
    return lax.ppermute(x, axis, [(i, (i + by) % peers) for i in range(peers)])


def with_halo(block, sides, width, periodic):
    for axis, dim in sides:
        count = lax.axis_size(axis)
        forward = [(i, i + 1) for i in range(count - 1)]
        if periodic:
            forward.append((count - 1, 0))
        backward = [(target, source) for source, target in forward]
        low = lax.ppermute(
            lax.slice_in_dim(block, block.shape[dim] - width, None, axis=dim), axis, forward
        )
        high = lax.ppermute(lax.slice_in_dim(block, 0, width, axis=dim), axis, backward)
        block = jnp.concatenate([low, block, high], axis=dim)
    return block


def cubic_weights(fraction):
    w_zero = -fraction * (fraction - 1.0) * (fraction - 2.0) / 6.0
    w_one = (fraction + 1.0) * (fraction - 1.0) * (fraction - 2.0) / 2.0
    w_two = -(fraction + 1.0) * fraction * (fraction - 2.0) / 2.0
    w_three = (fraction + 1.0) * fraction * (fraction - 1.0) / 6.0
    return (w_zero, w_one, w_two, w_three)


def lat_step(padded, offset, fraction, row_count):
    weights = cubic_weights(fraction)
    summed = None
    for place_index in range(6):
        row_delta = place_index - 2
        coeff = jnp.zeros_like(fraction)
        for tap_index in range(4):
            coeff = coeff + jnp.where(offset == tap_index - 1 - row_delta, weights[tap_index], 0.0)
        addend = coeff[:, :, None] * padded[:, 1 + place_index : 1 + place_index + row_count, :]
        summed = addend if summed is None else summed + addend
    return summed


def lon_step(wrapped, fraction, tracer_count):
    weights = cubic_weights(fraction)
    width_cols = wrapped.shape[2] - 4 * tracer_count
    summed = None
    for tap_index in range(4):
        offset_cols = (1 + tap_index) * tracer_count
        addend = (
            weights[tap_index][:, :, None] * wrapped[:, :, offset_cols : offset_cols + width_cols]
        )
        summed = addend if summed is None else summed + addend
    return summed


def remap(tracer_field, fraction):
    level_above = jnp.concatenate([tracer_field[1:], tracer_field[-1:]], axis=0)
    return (1.0 - fraction)[:, :, None] * tracer_field + fraction[:, :, None] * level_above


def diffuse(tracer_field, kappa):
    levels = tracer_field.shape[0]
    face_kappa = 0.5 * (kappa[:-1] + kappa[1:])
    zero_face = jnp.zeros_like(kappa[:1])
    face_below = jnp.concatenate([zero_face, face_kappa], axis=0)
    face_above = jnp.concatenate([face_kappa, zero_face], axis=0)
    ratio_prev = jnp.zeros_like(kappa[0])
    solved_prev = jnp.zeros_like(tracer_field[0])
    ratios = []
    solveds = []
    for level_index in range(levels):
        below = face_below[level_index]
        above = face_above[level_index]
        pivot_value = 1.0 + below + above + below * ratio_prev
        ratio_now = -above / pivot_value
        solved_now = (tracer_field[level_index] + below[:, None] * solved_prev) / pivot_value[
            :, None
        ]
        ratios.append(ratio_now)
        solveds.append(solved_now)
        ratio_prev = ratio_now
        solved_prev = solved_now
    results = [None] * levels
    results[levels - 1] = solveds[levels - 1]
    for level_index in range(levels - 2, -1, -1):
        results[level_index] = (
            solveds[level_index] - ratios[level_index][:, None] * results[level_index + 1]
        )
    return jnp.stack(results, axis=0)


def bit_mask(amount, position):
    return (amount // 2**position % 2 == 1)[:, :, None]


PAIR = 2


def pair_order(cells):
    cols = np.arange(cells * NTR)
    cell, tracer = cols // NTR, cols % NTR
    return (tracer // PAIR) * cells * PAIR + cell * PAIR + tracer % PAIR


def permutation(target, inverse):
    cols = np.arange(target.shape[0])
    if inverse:
        matrix = cols[:, None] == target[None, :]
    else:
        matrix = cols[None, :] == target[:, None]
    return jnp.asarray(matrix.astype(np.float32), dtype=jnp.bfloat16)


def permute_block(block, matrix):
    high = block.astype(jnp.bfloat16)
    rest = block - high.astype(jnp.float32)
    middle = rest.astype(jnp.bfloat16)
    low = (rest - middle.astype(jnp.float32)).astype(jnp.bfloat16)
    total = jnp.dot(high, matrix, preferred_element_type=jnp.float32)
    total = total + jnp.dot(middle, matrix, preferred_element_type=jnp.float32)
    return total + jnp.dot(low, matrix, preferred_element_type=jnp.float32)


CHUNKS = 4
MESH_ID = pl.DeviceIdType.MESH


def greet(count, me, lat):
    barrier = pltpu.get_barrier_semaphore()
    for offset in range(1, count):
        peer = lax.rem(me + offset, count)
        pl.semaphore_signal(barrier, 1, device_id=(peer, lat), device_id_type=MESH_ID)
    return barrier


def neighbours(parts):
    lon = lax.axis_index("lon")
    lat = lax.axis_index("lat")
    bands = lax.axis_size("lat")
    quarter = lon % parts
    inside_up = quarter < parts - 1
    inside_down = quarter > 0
    has_up = jnp.logical_or(inside_up, lat < bands - 1)
    has_down = jnp.logical_or(inside_down, lat > 0)
    up = (jnp.where(inside_up, lon + 1, lon + 1 - parts), jnp.where(inside_up, lat, lat + 1))
    down = (jnp.where(inside_down, lon - 1, lon + parts - 1), jnp.where(inside_down, lat, lat - 1))
    return has_up, up, has_down, down


def entry_kernel(x_ref, matrix_ref, field_ref, below_ref, above_ref, moved, landed, top_stage, bottom_stage,
                 zero_low, zero_high, send_sem, recv_sem, local_sem, halo_send, halo_recv, store_sem,
                 *, src_at, dst_at, parts):
    count = lax.axis_size("lon")
    me = lax.axis_index("lon")
    lat = lax.axis_index("lat")
    levels = x_ref.shape[0]
    rows = landed.shape[1]
    per = levels // CHUNKS
    has_up, up, has_down, down = neighbours(parts)
    barrier = greet(count, me, lat)

    @pl.when(has_up)
    def _():
        pl.semaphore_signal(barrier, 1, device_id=up, device_id_type=MESH_ID)

    @pl.when(has_down)
    def _():
        pl.semaphore_signal(barrier, 1, device_id=down, device_id_type=MESH_ID)

    copies = []
    locals_ = []
    for chunk in range(CHUNKS):
        def body(k, carry):
            moved[k] = permute_block(x_ref[k], matrix_ref[...])
            return carry

        lax.fori_loop(chunk * per, (chunk + 1) * per, body, 0)
        if chunk == 0:
            pl.semaphore_wait(barrier, count - 1 + has_up.astype(jnp.int32) + has_down.astype(jnp.int32))
        part = pl.ds(chunk * per, per)
        for offset in range(1, count):
            peer = lax.rem(me + offset, count)
            copy = pltpu.make_async_remote_copy(
                src_ref=src_at(moved, peer, part),
                dst_ref=dst_at(landed, me, part),
                send_sem=send_sem.at[chunk, offset],
                recv_sem=recv_sem.at[chunk, offset],
                device_id=(peer, lat),
                device_id_type=MESH_ID,
            )
            copy.start()
            copies.append(copy)
        local = pltpu.make_async_copy(src_at(moved, me, part), dst_at(landed, me, part), local_sem.at[chunk])
        local.start()
        locals_.append(local)
    for copy in copies:
        copy.wait_recv()
    for local in locals_:
        local.wait()
    top_stage[...] = landed[:, rows - top_stage.shape[1] :, :]
    bottom_stage[...] = landed[:, : bottom_stage.shape[1], :]
    to_up = pltpu.make_async_remote_copy(
        src_ref=top_stage, dst_ref=below_ref, send_sem=halo_send.at[0], recv_sem=halo_recv.at[0],
        device_id=up, device_id_type=MESH_ID,
    )
    to_down = pltpu.make_async_remote_copy(
        src_ref=bottom_stage, dst_ref=above_ref, send_sem=halo_send.at[1], recv_sem=halo_recv.at[1],
        device_id=down, device_id_type=MESH_ID,
    )

    @pl.when(has_up)
    def _():
        to_up.start()

    @pl.when(has_down)
    def _():
        to_down.start()

    store = pltpu.make_async_copy(landed, field_ref, store_sem.at[0])
    store.start()
    fill_low = pltpu.make_async_copy(zero_low, below_ref, store_sem.at[1])
    fill_high = pltpu.make_async_copy(zero_high, above_ref, store_sem.at[2])

    @pl.when(jnp.logical_not(has_down))
    def _():
        zero_low[...] = jnp.zeros(zero_low.shape, zero_low.dtype)
        fill_low.start()
        fill_low.wait()

    @pl.when(jnp.logical_not(has_up))
    def _():
        zero_high[...] = jnp.zeros(zero_high.shape, zero_high.dtype)
        fill_high.start()
        fill_high.wait()

    store.wait()

    for copy in copies:
        copy.wait_send()

    @pl.when(has_up)
    def _():
        to_up.wait_send()
        to_down.wait_recv()

    @pl.when(has_down)
    def _():
        to_down.wait_send()
        to_up.wait_recv()


def exit_kernel(src_ref, matrix_ref, out_ref, landed, result, send_sem, recv_sem, local_sem, store_sem, *, src_at, dst_at):
    count = lax.axis_size("lon")
    me = lax.axis_index("lon")
    lat = lax.axis_index("lat")
    levels = out_ref.shape[0]
    per = levels // CHUNKS
    barrier = greet(count, me, lat)
    pl.semaphore_wait(barrier, count - 1)
    copies = []
    locals_ = []
    stores = []
    for chunk in range(CHUNKS):
        part = pl.ds(chunk * per, per)
        row = []
        for offset in range(1, count):
            peer = lax.rem(me + offset, count)
            copy = pltpu.make_async_remote_copy(
                src_ref=src_at(src_ref, peer, part),
                dst_ref=dst_at(landed, me, part),
                send_sem=send_sem.at[chunk, offset],
                recv_sem=recv_sem.at[chunk, offset],
                device_id=(peer, lat),
                device_id_type=MESH_ID,
            )
            copy.start()
            row.append(copy)
        copies.append(row)
        local = pltpu.make_async_copy(src_at(src_ref, me, part), dst_at(landed, me, part), local_sem.at[chunk])
        local.start()
        locals_.append(local)
    for chunk in range(CHUNKS):
        for copy in copies[chunk]:
            copy.wait_recv()
        locals_[chunk].wait()

        def body(k, carry):
            result[k] = permute_block(landed[k], matrix_ref[...])
            return carry

        lax.fori_loop(chunk * per, (chunk + 1) * per, body, 0)
        part = pl.ds(chunk * per, per)
        store = pltpu.make_async_copy(result.at[part], out_ref.at[part], store_sem.at[chunk])
        store.start()
        stores.append(store)
    for store in stores:
        store.wait()
    for row in copies:
        for copy in row:
            copy.wait_send()


def run_exchange(kernel, operand, matrix, out_shape, src_spec, out_spec, scratch, src_at, dst_at, ident, extra=()):
    count = lax.axis_size("lon")
    return pl.pallas_call(
        functools.partial(kernel, src_at=src_at, dst_at=dst_at),
        out_shape=jax.ShapeDtypeStruct(out_shape, operand.dtype),
        in_specs=[src_spec, pl.BlockSpec(memory_space=pltpu.VMEM)],
        out_specs=out_spec,
        scratch_shapes=[pltpu.VMEM(scratch, operand.dtype)] * (1 + len(extra)) + [
            pltpu.SemaphoreType.DMA((CHUNKS, count)),
            pltpu.SemaphoreType.DMA((CHUNKS, count)),
            pltpu.SemaphoreType.DMA((CHUNKS,)),
        ] + [pltpu.SemaphoreType.DMA((CHUNKS,)) for _ in extra],
        compiler_params=pltpu.CompilerParams(collective_id=ident, has_side_effects=True),
    )(operand, matrix)


def to_columns(block):
    levels, rows, width = block.shape
    cells = width // NTR
    devices = lax.axis_size("lon")
    parts = devices // (NTR // PAIR)
    count = rows // parts
    lane = cells * PAIR

    def src_at(ref, peer, part):
        return ref.at[part, pl.ds((peer % parts) * count, count), pl.ds((peer // parts) * lane, lane)]

    def dst_at(ref, sender, part):
        return ref.at[part, :, pl.ds(sender * lane, lane)]

    vmem = pl.BlockSpec(memory_space=pltpu.VMEM)
    hbm = pl.BlockSpec(memory_space=pl.ANY)
    field_shape = (levels, count, devices * lane)
    below_shape = (levels, 2, devices * lane)
    above_shape = (levels, 3, devices * lane)
    return pl.pallas_call(
        functools.partial(entry_kernel, src_at=src_at, dst_at=dst_at, parts=parts),
        out_shape=tuple(jax.ShapeDtypeStruct(shape, block.dtype) for shape in (field_shape, below_shape, above_shape)),
        in_specs=[vmem, vmem],
        out_specs=(hbm, hbm, hbm),
        scratch_shapes=[
            pltpu.VMEM(block.shape, block.dtype),
            pltpu.VMEM(field_shape, block.dtype),
            pltpu.VMEM(below_shape, block.dtype),
            pltpu.VMEM(above_shape, block.dtype),
            pltpu.VMEM(below_shape, block.dtype),
            pltpu.VMEM(above_shape, block.dtype),
            pltpu.SemaphoreType.DMA((CHUNKS, devices)),
            pltpu.SemaphoreType.DMA((CHUNKS, devices)),
            pltpu.SemaphoreType.DMA((CHUNKS,)),
            pltpu.SemaphoreType.DMA((2,)),
            pltpu.SemaphoreType.DMA((2,)),
            pltpu.SemaphoreType.DMA((3,)),
        ],
        compiler_params=pltpu.CompilerParams(collective_id=0, has_side_effects=True),
    )(block, permutation(pair_order(cells), False))


def from_columns(field, rows):
    levels, count, width = field.shape
    devices = lax.axis_size("lon")
    parts = devices // (NTR // PAIR)
    lane = width // devices
    cells = lane // PAIR

    def src_at(ref, peer, part):
        return ref.at[part, :, pl.ds(peer * lane, lane)]

    def dst_at(ref, sender, part):
        return ref.at[part, pl.ds((sender % parts) * count, count), pl.ds((sender // parts) * lane, lane)]

    shape = (levels, rows, cells * NTR)
    return run_exchange(
        exit_kernel, field, permutation(pair_order(cells), True), shape,
        pl.BlockSpec(memory_space=pl.ANY), pl.BlockSpec(memory_space=pl.ANY), shape,
        src_at, dst_at, 1, extra=("result",),
    )


def lat_halo(field, width):
    lon_n = lax.axis_size("lon")
    lat_n = lax.axis_size("lat")
    parts = lon_n // (NTR // PAIR)
    up = []
    for b in range(lat_n):
        for l in range(lon_n):
            t, h = l // parts, l % parts
            g = b * parts + h
            if g + 1 < lat_n * parts:
                nb, nh = (g + 1) // parts, (g + 1) % parts
                up.append((l * lat_n + b, (t * parts + nh) * lat_n + nb))
    down = [(d, s) for s, d in up]
    rows = field.shape[1]
    below = lax.ppermute(field[:, rows - width + 1 :], ("lon", "lat"), up)
    above = lax.ppermute(field[:, :width], ("lon", "lat"), down)
    return jnp.concatenate([below[:, :1], below, field, above], axis=1)


def roll_rows(field, shift):
    cells = field.shape[2] // PAIR
    reach = cells // 4
    amount = shift + reach
    current = jnp.roll(field, -PAIR * reach, axis=2)
    for position in range((2 * reach - 1).bit_length()):
        moved = jnp.roll(current, PAIR * 2**position, axis=2)
        current = jnp.where(bit_mask(amount, position), moved, current)
    return current


def lon_cubic(shifted, fraction):
    weights = cubic_weights(fraction)
    taps = [jnp.roll(shifted, PAIR * (1 - p), axis=2) for p in range(4)]
    summed = None
    for p in range(4):
        addend = weights[p][:, :, None] * taps[p]
        summed = addend if summed is None else summed + addend
    return summed


def own_rows(values, count):
    parts = lax.axis_size("lon") // (NTR // PAIR)
    start = (lax.axis_index("lon") % parts) * count
    return lax.dynamic_slice_in_dim(values, start, count, axis=values.ndim - 1)


def per_device(tracers, lon_shift, lon_frac, lat_shift, lat_frac, remap_frac, diffusivity):
    rows = tracers.shape[1]
    field, below, above = to_columns(tracers)
    count = field.shape[1]
    width = field.shape[2]
    lon_shift, lon_frac, lat_shift, lat_frac, remap_frac, diffusivity = (
        own_rows(v, count) for v in (lon_shift, lon_frac, lat_shift, lat_frac, remap_frac, diffusivity)
    )
    for time_step in range(STEPS):
        if time_step == 0:
            padded = jnp.concatenate([below[:, :1], below, field, above], axis=1)
        else:
            padded = lat_halo(field, 3)
        field = lat_step(padded, lat_shift[time_step], lat_frac[time_step], count)
        field = lon_cubic(roll_rows(field, lon_shift[time_step]), lon_frac[time_step])
        field = remap(field, remap_frac[time_step])
        field = diffuse(field, diffusivity)
    return from_columns(field, rows)


def solution(mesh):
    in_specs = (
        P(None, "lat", "lon"),
        P(None, None, "lat"),
        P(None, None, "lat"),
        P(None, None, "lat"),
        P(None, None, "lat"),
        P(None, None, "lat"),
        P(None, "lat"),
    )
    out_specs = P(None, "lat", "lon")
    return jax.shard_map(
        per_device, mesh=mesh, in_specs=in_specs, out_specs=out_specs, check_vma=False
    )
```

```python
import functools

import jax
import numpy as np
import jax.numpy as jnp
from jax import lax
from jax.experimental import pallas as pl
from jax.experimental.pallas import tpu as pltpu
from jax.sharding import PartitionSpec as P

NTR = 8
STEPS = 2


def from_behind(x, axis, by):
    peers = lax.axis_size(axis)
    return lax.ppermute(x, axis, [(i, (i + by) % peers) for i in range(peers)])


def with_halo(block, sides, width, periodic):
    for axis, dim in sides:
        count = lax.axis_size(axis)
        forward = [(i, i + 1) for i in range(count - 1)]
        if periodic:
            forward.append((count - 1, 0))
        backward = [(target, source) for source, target in forward]
        low = lax.ppermute(
            lax.slice_in_dim(block, block.shape[dim] - width, None, axis=dim), axis, forward
        )
        high = lax.ppermute(lax.slice_in_dim(block, 0, width, axis=dim), axis, backward)
        block = jnp.concatenate([low, block, high], axis=dim)
    return block


def cubic_weights(fraction):
    w_zero = -fraction * (fraction - 1.0) * (fraction - 2.0) / 6.0
    w_one = (fraction + 1.0) * (fraction - 1.0) * (fraction - 2.0) / 2.0
    w_two = -(fraction + 1.0) * fraction * (fraction - 2.0) / 2.0
    w_three = (fraction + 1.0) * fraction * (fraction - 1.0) / 6.0
    return (w_zero, w_one, w_two, w_three)


def lat_step(padded, offset, fraction, row_count):
    weights = cubic_weights(fraction)
    summed = None
    for place_index in range(6):
        row_delta = place_index - 2
        coeff = jnp.zeros_like(fraction)
        for tap_index in range(4):
            coeff = coeff + jnp.where(offset == tap_index - 1 - row_delta, weights[tap_index], 0.0)
        addend = coeff[:, :, None] * padded[:, 1 + place_index : 1 + place_index + row_count, :]
        summed = addend if summed is None else summed + addend
    return summed


def lon_step(wrapped, fraction, tracer_count):
    weights = cubic_weights(fraction)
    width_cols = wrapped.shape[2] - 4 * tracer_count
    summed = None
    for tap_index in range(4):
        offset_cols = (1 + tap_index) * tracer_count
        addend = (
            weights[tap_index][:, :, None] * wrapped[:, :, offset_cols : offset_cols + width_cols]
        )
        summed = addend if summed is None else summed + addend
    return summed


def remap(tracer_field, fraction):
    level_above = jnp.concatenate([tracer_field[1:], tracer_field[-1:]], axis=0)
    return (1.0 - fraction)[:, :, None] * tracer_field + fraction[:, :, None] * level_above


def diffuse(tracer_field, kappa):
    levels = tracer_field.shape[0]
    face_kappa = 0.5 * (kappa[:-1] + kappa[1:])
    zero_face = jnp.zeros_like(kappa[:1])
    face_below = jnp.concatenate([zero_face, face_kappa], axis=0)
    face_above = jnp.concatenate([face_kappa, zero_face], axis=0)
    ratio_prev = jnp.zeros_like(kappa[0])
    solved_prev = jnp.zeros_like(tracer_field[0])
    ratios = []
    solveds = []
    for level_index in range(levels):
        below = face_below[level_index]
        above = face_above[level_index]
        pivot_value = 1.0 + below + above + below * ratio_prev
        ratio_now = -above / pivot_value
        solved_now = (tracer_field[level_index] + below[:, None] * solved_prev) / pivot_value[
            :, None
        ]
        ratios.append(ratio_now)
        solveds.append(solved_now)
        ratio_prev = ratio_now
        solved_prev = solved_now
    results = [None] * levels
    results[levels - 1] = solveds[levels - 1]
    for level_index in range(levels - 2, -1, -1):
        results[level_index] = (
            solveds[level_index] - ratios[level_index][:, None] * results[level_index + 1]
        )
    return jnp.stack(results, axis=0)


def bit_mask(amount, position):
    return (amount // 2**position % 2 == 1)[:, :, None]


PAIR = 2


def pair_order(cells):
    cols = np.arange(cells * NTR)
    cell, tracer = cols // NTR, cols % NTR
    return (tracer // PAIR) * cells * PAIR + cell * PAIR + tracer % PAIR


def permutation(target, inverse):
    cols = np.arange(target.shape[0])
    if inverse:
        matrix = cols[:, None] == target[None, :]
    else:
        matrix = cols[None, :] == target[:, None]
    return jnp.asarray(matrix.astype(np.float32), dtype=jnp.bfloat16)


def permute_block(block, matrix):
    high = block.astype(jnp.bfloat16)
    rest = block - high.astype(jnp.float32)
    middle = rest.astype(jnp.bfloat16)
    low = (rest - middle.astype(jnp.float32)).astype(jnp.bfloat16)
    total = jnp.dot(high, matrix, preferred_element_type=jnp.float32)
    total = total + jnp.dot(middle, matrix, preferred_element_type=jnp.float32)
    return total + jnp.dot(low, matrix, preferred_element_type=jnp.float32)


CHUNKS = 4
MESH_ID = pl.DeviceIdType.MESH


def greet(count, me, lat):
    barrier = pltpu.get_barrier_semaphore()
    for offset in range(1, count):
        peer = lax.rem(me + offset, count)
        pl.semaphore_signal(barrier, 1, device_id=(peer, lat), device_id_type=MESH_ID)
    return barrier


def neighbours(parts):
    lon = lax.axis_index("lon")
    lat = lax.axis_index("lat")
    bands = lax.axis_size("lat")
    quarter = lon % parts
    inside_up = quarter < parts - 1
    inside_down = quarter > 0
    has_up = jnp.logical_or(inside_up, lat < bands - 1)
    has_down = jnp.logical_or(inside_down, lat > 0)
    up = (jnp.where(inside_up, lon + 1, lon + 1 - parts), jnp.where(inside_up, lat, lat + 1))
    down = (jnp.where(inside_down, lon - 1, lon + parts - 1), jnp.where(inside_down, lat, lat - 1))
    return has_up, up, has_down, down


def entry_kernel(x_ref, matrix_ref, field_ref, below_ref, above_ref, moved, landed, top_stage, bottom_stage,
                 zero_low, zero_high, send_sem, recv_sem, local_sem, halo_send, halo_recv, store_sem,
                 *, src_at, dst_at, parts):
    count = lax.axis_size("lon")
    me = lax.axis_index("lon")
    lat = lax.axis_index("lat")
    levels = x_ref.shape[0]
    rows = landed.shape[1]
    per = levels // CHUNKS
    has_up, up, has_down, down = neighbours(parts)
    barrier = greet(count, me, lat)

    @pl.when(has_up)
    def _():
        pl.semaphore_signal(barrier, 1, device_id=up, device_id_type=MESH_ID)

    @pl.when(has_down)
    def _():
        pl.semaphore_signal(barrier, 1, device_id=down, device_id_type=MESH_ID)

    copies = []
    locals_ = []
    for chunk in range(CHUNKS):
        def body(k, carry):
            moved[k] = permute_block(x_ref[k], matrix_ref[...])
            return carry

        lax.fori_loop(chunk * per, (chunk + 1) * per, body, 0)
        if chunk == 0:
            pl.semaphore_wait(barrier, count - 1 + has_up.astype(jnp.int32) + has_down.astype(jnp.int32))
        part = pl.ds(chunk * per, per)
        for offset in range(1, count):
            peer = lax.rem(me + offset, count)
            copy = pltpu.make_async_remote_copy(
                src_ref=src_at(moved, peer, part),
                dst_ref=dst_at(landed, me, part),
                send_sem=send_sem.at[chunk, offset],
                recv_sem=recv_sem.at[chunk, offset],
                device_id=(peer, lat),
                device_id_type=MESH_ID,
            )
            copy.start()
            copies.append(copy)
        local = pltpu.make_async_copy(src_at(moved, me, part), dst_at(landed, me, part), local_sem.at[chunk])
        local.start()
        locals_.append(local)
    for copy in copies:
        copy.wait_recv()
    for local in locals_:
        local.wait()
    top_stage[...] = landed[:, rows - top_stage.shape[1] :, :]
    bottom_stage[...] = landed[:, : bottom_stage.shape[1], :]
    to_up = pltpu.make_async_remote_copy(
        src_ref=top_stage, dst_ref=below_ref, send_sem=halo_send.at[0], recv_sem=halo_recv.at[0],
        device_id=up, device_id_type=MESH_ID,
    )
    to_down = pltpu.make_async_remote_copy(
        src_ref=bottom_stage, dst_ref=above_ref, send_sem=halo_send.at[1], recv_sem=halo_recv.at[1],
        device_id=down, device_id_type=MESH_ID,
    )

    @pl.when(has_up)
    def _():
        to_up.start()

    @pl.when(has_down)
    def _():
        to_down.start()

    store = pltpu.make_async_copy(landed, field_ref, store_sem.at[0])
    store.start()
    fill_low = pltpu.make_async_copy(zero_low, below_ref, store_sem.at[1])
    fill_high = pltpu.make_async_copy(zero_high, above_ref, store_sem.at[2])

    @pl.when(jnp.logical_not(has_down))
    def _():
        zero_low[...] = jnp.zeros(zero_low.shape, zero_low.dtype)
        fill_low.start()
        fill_low.wait()

    @pl.when(jnp.logical_not(has_up))
    def _():
        zero_high[...] = jnp.zeros(zero_high.shape, zero_high.dtype)
        fill_high.start()
        fill_high.wait()

    store.wait()

    for copy in copies:
        copy.wait_send()

    @pl.when(has_up)
    def _():
        to_up.wait_send()
        to_down.wait_recv()

    @pl.when(has_down)
    def _():
        to_down.wait_send()
        to_up.wait_recv()


def exit_kernel(src_ref, matrix_ref, out_ref, landed, send_sem, recv_sem, local_sem, *, src_at, dst_at):
    count = lax.axis_size("lon")
    me = lax.axis_index("lon")
    lat = lax.axis_index("lat")
    levels = out_ref.shape[0]
    per = levels // CHUNKS
    barrier = greet(count, me, lat)
    pl.semaphore_wait(barrier, count - 1)
    copies = []
    locals_ = []
    for chunk in range(CHUNKS):
        part = pl.ds(chunk * per, per)
        row = []
        for offset in range(1, count):
            peer = lax.rem(me + offset, count)
            copy = pltpu.make_async_remote_copy(
                src_ref=src_at(src_ref, peer, part),
                dst_ref=dst_at(landed, me, part),
                send_sem=send_sem.at[chunk, offset],
                recv_sem=recv_sem.at[chunk, offset],
                device_id=(peer, lat),
                device_id_type=MESH_ID,
            )
            copy.start()
            row.append(copy)
        copies.append(row)
        local = pltpu.make_async_copy(src_at(src_ref, me, part), dst_at(landed, me, part), local_sem.at[chunk])
        local.start()
        locals_.append(local)
    for chunk in range(CHUNKS):
        for copy in copies[chunk]:
            copy.wait_recv()
        locals_[chunk].wait()

        def body(k, carry):
            out_ref[k] = permute_block(landed[k], matrix_ref[...])
            return carry

        lax.fori_loop(chunk * per, (chunk + 1) * per, body, 0)
    for row in copies:
        for copy in row:
            copy.wait_send()


def run_exchange(kernel, operand, matrix, out_shape, src_spec, out_spec, scratch, src_at, dst_at, ident):
    count = lax.axis_size("lon")
    return pl.pallas_call(
        functools.partial(kernel, src_at=src_at, dst_at=dst_at),
        out_shape=jax.ShapeDtypeStruct(out_shape, operand.dtype),
        in_specs=[src_spec, pl.BlockSpec(memory_space=pltpu.VMEM)],
        out_specs=out_spec,
        scratch_shapes=[
            pltpu.VMEM(scratch, operand.dtype),
            pltpu.SemaphoreType.DMA((CHUNKS, count)),
            pltpu.SemaphoreType.DMA((CHUNKS, count)),
            pltpu.SemaphoreType.DMA((CHUNKS,)),
        ],
        compiler_params=pltpu.CompilerParams(collective_id=ident, has_side_effects=True),
    )(operand, matrix)


def to_columns(block):
    levels, rows, width = block.shape
    cells = width // NTR
    devices = lax.axis_size("lon")
    parts = devices // (NTR // PAIR)
    count = rows // parts
    lane = cells * PAIR

    def src_at(ref, peer, part):
        return ref.at[part, pl.ds((peer % parts) * count, count), pl.ds((peer // parts) * lane, lane)]

    def dst_at(ref, sender, part):
        return ref.at[part, :, pl.ds(sender * lane, lane)]

    vmem = pl.BlockSpec(memory_space=pltpu.VMEM)
    hbm = pl.BlockSpec(memory_space=pl.ANY)
    field_shape = (levels, count, devices * lane)
    below_shape = (levels, 2, devices * lane)
    above_shape = (levels, 3, devices * lane)
    return pl.pallas_call(
        functools.partial(entry_kernel, src_at=src_at, dst_at=dst_at, parts=parts),
        out_shape=tuple(jax.ShapeDtypeStruct(shape, block.dtype) for shape in (field_shape, below_shape, above_shape)),
        in_specs=[vmem, vmem],
        out_specs=(hbm, hbm, hbm),
        scratch_shapes=[
            pltpu.VMEM(block.shape, block.dtype),
            pltpu.VMEM(field_shape, block.dtype),
            pltpu.VMEM(below_shape, block.dtype),
            pltpu.VMEM(above_shape, block.dtype),
            pltpu.VMEM(below_shape, block.dtype),
            pltpu.VMEM(above_shape, block.dtype),
            pltpu.SemaphoreType.DMA((CHUNKS, devices)),
            pltpu.SemaphoreType.DMA((CHUNKS, devices)),
            pltpu.SemaphoreType.DMA((CHUNKS,)),
            pltpu.SemaphoreType.DMA((2,)),
            pltpu.SemaphoreType.DMA((2,)),
            pltpu.SemaphoreType.DMA((3,)),
        ],
        compiler_params=pltpu.CompilerParams(collective_id=0, has_side_effects=True),
    )(block, permutation(pair_order(cells), False))


def from_columns(field, rows):
    levels, count, width = field.shape
    devices = lax.axis_size("lon")
    parts = devices // (NTR // PAIR)
    lane = width // devices
    cells = lane // PAIR

    def src_at(ref, peer, part):
        return ref.at[part, :, pl.ds(peer * lane, lane)]

    def dst_at(ref, sender, part):
        return ref.at[part, pl.ds((sender % parts) * count, count), pl.ds((sender // parts) * lane, lane)]

    shape = (levels, rows, cells * NTR)
    return run_exchange(
        exit_kernel, field, permutation(pair_order(cells), True), shape,
        pl.BlockSpec(memory_space=pl.ANY), pl.BlockSpec(memory_space=pltpu.VMEM), shape,
        src_at, dst_at, 1,
    )


def lat_halo(field, width):
    lon_n = lax.axis_size("lon")
    lat_n = lax.axis_size("lat")
    parts = lon_n // (NTR // PAIR)
    up = []
    for b in range(lat_n):
        for l in range(lon_n):
            t, h = l // parts, l % parts
            g = b * parts + h
            if g + 1 < lat_n * parts:
                nb, nh = (g + 1) // parts, (g + 1) % parts
                up.append((l * lat_n + b, (t * parts + nh) * lat_n + nb))
    down = [(d, s) for s, d in up]
    rows = field.shape[1]
    below = lax.ppermute(field[:, rows - width + 1 :], ("lon", "lat"), up)
    above = lax.ppermute(field[:, :width], ("lon", "lat"), down)
    return jnp.concatenate([below[:, :1], below, field, above], axis=1)


def roll_rows(field, shift):
    cells = field.shape[2] // PAIR
    reach = cells // 4
    amount = shift + reach
    current = jnp.roll(field, -PAIR * reach, axis=2)
    stages = (2 * reach - 1).bit_length()
    position = 0
    while position < stages:
        step = PAIR * 2**position
        if position + 1 < stages and step < 128:
            one = jnp.roll(current, step, axis=2)
            two = jnp.roll(current, 2 * step, axis=2)
            three = jnp.roll(current, 3 * step, axis=2)
            low, high = bit_mask(amount, position), bit_mask(amount, position + 1)
            current = jnp.where(high, jnp.where(low, three, two), jnp.where(low, one, current))
            position += 2
        else:
            moved = jnp.roll(current, step, axis=2)
            current = jnp.where(bit_mask(amount, position), moved, current)
            position += 1
    return current


def lon_cubic(shifted, fraction):
    weights = cubic_weights(fraction)
    taps = [jnp.roll(shifted, PAIR * (1 - p), axis=2) for p in range(4)]
    summed = None
    for p in range(4):
        addend = weights[p][:, :, None] * taps[p]
        summed = addend if summed is None else summed + addend
    return summed


def own_rows(values, count):
    parts = lax.axis_size("lon") // (NTR // PAIR)
    start = (lax.axis_index("lon") % parts) * count
    return lax.dynamic_slice_in_dim(values, start, count, axis=values.ndim - 1)


def per_device(tracers, lon_shift, lon_frac, lat_shift, lat_frac, remap_frac, diffusivity):
    rows = tracers.shape[1]
    field, below, above = to_columns(tracers)
    count = field.shape[1]
    width = field.shape[2]
    lon_shift, lon_frac, lat_shift, lat_frac, remap_frac, diffusivity = (
        own_rows(v, count) for v in (lon_shift, lon_frac, lat_shift, lat_frac, remap_frac, diffusivity)
    )
    for time_step in range(STEPS):
        if time_step == 0:
            padded = jnp.concatenate([below[:, :1], below, field, above], axis=1)
        else:
            padded = lat_halo(field, 3)
        field = lat_step(padded, lat_shift[time_step], lat_frac[time_step], count)
        field = lon_cubic(roll_rows(field, lon_shift[time_step]), lon_frac[time_step])
        field = remap(field, remap_frac[time_step])
        field = diffuse(field, diffusivity)
    return from_columns(field, rows)


def solution(mesh):
    in_specs = (
        P(None, "lat", "lon"),
        P(None, None, "lat"),
        P(None, None, "lat"),
        P(None, None, "lat"),
        P(None, None, "lat"),
        P(None, None, "lat"),
        P(None, "lat"),
    )
    out_specs = P(None, "lat", "lon")
    return jax.shard_map(
        per_device, mesh=mesh, in_specs=in_specs, out_specs=out_specs, check_vma=False
    )
```

```python
import functools

import jax
import numpy as np
import jax.numpy as jnp
from jax import lax
from jax.experimental import pallas as pl
from jax.experimental.pallas import tpu as pltpu
from jax.sharding import PartitionSpec as P

NTR = 8
STEPS = 2


def from_behind(x, axis, by):
    peers = lax.axis_size(axis)
    return lax.ppermute(x, axis, [(i, (i + by) % peers) for i in range(peers)])


def with_halo(block, sides, width, periodic):
    for axis, dim in sides:
        count = lax.axis_size(axis)
        forward = [(i, i + 1) for i in range(count - 1)]
        if periodic:
            forward.append((count - 1, 0))
        backward = [(target, source) for source, target in forward]
        low = lax.ppermute(
            lax.slice_in_dim(block, block.shape[dim] - width, None, axis=dim), axis, forward
        )
        high = lax.ppermute(lax.slice_in_dim(block, 0, width, axis=dim), axis, backward)
        block = jnp.concatenate([low, block, high], axis=dim)
    return block


def cubic_weights(fraction):
    w_zero = -fraction * (fraction - 1.0) * (fraction - 2.0) / 6.0
    w_one = (fraction + 1.0) * (fraction - 1.0) * (fraction - 2.0) / 2.0
    w_two = -(fraction + 1.0) * fraction * (fraction - 2.0) / 2.0
    w_three = (fraction + 1.0) * fraction * (fraction - 1.0) / 6.0
    return (w_zero, w_one, w_two, w_three)


def lat_step(padded, offset, fraction, row_count):
    weights = cubic_weights(fraction)
    summed = None
    for place_index in range(6):
        row_delta = place_index - 2
        coeff = jnp.zeros_like(fraction)
        for tap_index in range(4):
            coeff = coeff + jnp.where(offset == tap_index - 1 - row_delta, weights[tap_index], 0.0)
        addend = coeff[:, :, None] * padded[:, 1 + place_index : 1 + place_index + row_count, :]
        summed = addend if summed is None else summed + addend
    return summed


def lon_step(wrapped, fraction, tracer_count):
    weights = cubic_weights(fraction)
    width_cols = wrapped.shape[2] - 4 * tracer_count
    summed = None
    for tap_index in range(4):
        offset_cols = (1 + tap_index) * tracer_count
        addend = (
            weights[tap_index][:, :, None] * wrapped[:, :, offset_cols : offset_cols + width_cols]
        )
        summed = addend if summed is None else summed + addend
    return summed


def remap(tracer_field, fraction):
    level_above = jnp.concatenate([tracer_field[1:], tracer_field[-1:]], axis=0)
    return (1.0 - fraction)[:, :, None] * tracer_field + fraction[:, :, None] * level_above


def diffuse(tracer_field, kappa):
    levels = tracer_field.shape[0]
    face_kappa = 0.5 * (kappa[:-1] + kappa[1:])
    zero_face = jnp.zeros_like(kappa[:1])
    face_below = jnp.concatenate([zero_face, face_kappa], axis=0)
    face_above = jnp.concatenate([face_kappa, zero_face], axis=0)
    ratio_prev = jnp.zeros_like(kappa[0])
    solved_prev = jnp.zeros_like(tracer_field[0])
    ratios = []
    solveds = []
    for level_index in range(levels):
        below = face_below[level_index]
        above = face_above[level_index]
        pivot_value = 1.0 + below + above + below * ratio_prev
        ratio_now = -above / pivot_value
        solved_now = (tracer_field[level_index] + below[:, None] * solved_prev) / pivot_value[
            :, None
        ]
        ratios.append(ratio_now)
        solveds.append(solved_now)
        ratio_prev = ratio_now
        solved_prev = solved_now
    results = [None] * levels
    results[levels - 1] = solveds[levels - 1]
    for level_index in range(levels - 2, -1, -1):
        results[level_index] = (
            solveds[level_index] - ratios[level_index][:, None] * results[level_index + 1]
        )
    return jnp.stack(results, axis=0)


def bit_mask(amount, position):
    return (amount // 2**position % 2 == 1)[:, :, None]


PAIR = 2


def pair_order(cells):
    cols = np.arange(cells * NTR)
    cell, tracer = cols // NTR, cols % NTR
    return (tracer // PAIR) * cells * PAIR + cell * PAIR + tracer % PAIR


def permutation(target, inverse):
    cols = np.arange(target.shape[0])
    if inverse:
        matrix = cols[:, None] == target[None, :]
    else:
        matrix = cols[None, :] == target[:, None]
    return jnp.asarray(matrix.astype(np.float32), dtype=jnp.bfloat16)


def permute_block(block, matrix):
    high = block.astype(jnp.bfloat16)
    rest = block - high.astype(jnp.float32)
    middle = rest.astype(jnp.bfloat16)
    low = (rest - middle.astype(jnp.float32)).astype(jnp.bfloat16)
    total = jnp.dot(high, matrix, preferred_element_type=jnp.float32)
    total = total + jnp.dot(middle, matrix, preferred_element_type=jnp.float32)
    return total + jnp.dot(low, matrix, preferred_element_type=jnp.float32)


CHUNKS = 4
MESH_ID = pl.DeviceIdType.MESH


def greet(count, me, lat):
    barrier = pltpu.get_barrier_semaphore()
    for offset in range(1, count):
        peer = lax.rem(me + offset, count)
        pl.semaphore_signal(barrier, 1, device_id=(peer, lat), device_id_type=MESH_ID)
    return barrier


def neighbours(parts):
    lon = lax.axis_index("lon")
    lat = lax.axis_index("lat")
    bands = lax.axis_size("lat")
    quarter = lon % parts
    inside_up = quarter < parts - 1
    inside_down = quarter > 0
    has_up = jnp.logical_or(inside_up, lat < bands - 1)
    has_down = jnp.logical_or(inside_down, lat > 0)
    up = (jnp.where(inside_up, lon + 1, lon + 1 - parts), jnp.where(inside_up, lat, lat + 1))
    down = (jnp.where(inside_down, lon - 1, lon + parts - 1), jnp.where(inside_down, lat, lat - 1))
    return has_up, up, has_down, down


def entry_kernel(x_ref, matrix_ref, field_ref, below_ref, above_ref, moved, landed, top_stage, bottom_stage,
                 zero_low, zero_high, send_sem, recv_sem, local_sem, halo_send, halo_recv, store_sem,
                 *, src_at, dst_at, parts):
    count = lax.axis_size("lon")
    me = lax.axis_index("lon")
    lat = lax.axis_index("lat")
    levels = x_ref.shape[0]
    rows = landed.shape[1]
    per = levels // CHUNKS
    has_up, up, has_down, down = neighbours(parts)
    barrier = greet(count, me, lat)

    @pl.when(has_up)
    def _():
        pl.semaphore_signal(barrier, 1, device_id=up, device_id_type=MESH_ID)

    @pl.when(has_down)
    def _():
        pl.semaphore_signal(barrier, 1, device_id=down, device_id_type=MESH_ID)

    copies = []
    locals_ = []
    for chunk in range(CHUNKS):
        def body(k, carry):
            moved[k] = permute_block(x_ref[k], matrix_ref[...])
            return carry

        lax.fori_loop(chunk * per, (chunk + 1) * per, body, 0)
        if chunk == 0:
            pl.semaphore_wait(barrier, count - 1 + has_up.astype(jnp.int32) + has_down.astype(jnp.int32))
        part = pl.ds(chunk * per, per)
        for offset in range(1, count):
            peer = lax.rem(me + offset, count)
            copy = pltpu.make_async_remote_copy(
                src_ref=src_at(moved, peer, part),
                dst_ref=dst_at(landed, me, part),
                send_sem=send_sem.at[chunk, offset],
                recv_sem=recv_sem.at[chunk, offset],
                device_id=(peer, lat),
                device_id_type=MESH_ID,
            )
            copy.start()
            copies.append(copy)
        local = pltpu.make_async_copy(src_at(moved, me, part), dst_at(landed, me, part), local_sem.at[chunk])
        local.start()
        locals_.append(local)
    for copy in copies:
        copy.wait_recv()
    for local in locals_:
        local.wait()
    top_stage[...] = landed[:, rows - top_stage.shape[1] :, :]
    bottom_stage[...] = landed[:, : bottom_stage.shape[1], :]
    to_up = pltpu.make_async_remote_copy(
        src_ref=top_stage, dst_ref=below_ref, send_sem=halo_send.at[0], recv_sem=halo_recv.at[0],
        device_id=up, device_id_type=MESH_ID,
    )
    to_down = pltpu.make_async_remote_copy(
        src_ref=bottom_stage, dst_ref=above_ref, send_sem=halo_send.at[1], recv_sem=halo_recv.at[1],
        device_id=down, device_id_type=MESH_ID,
    )

    @pl.when(has_up)
    def _():
        to_up.start()

    @pl.when(has_down)
    def _():
        to_down.start()

    store = pltpu.make_async_copy(landed, field_ref, store_sem.at[0])
    store.start()
    fill_low = pltpu.make_async_copy(zero_low, below_ref, store_sem.at[1])
    fill_high = pltpu.make_async_copy(zero_high, above_ref, store_sem.at[2])

    @pl.when(jnp.logical_not(has_down))
    def _():
        zero_low[...] = jnp.zeros(zero_low.shape, zero_low.dtype)
        fill_low.start()
        fill_low.wait()

    @pl.when(jnp.logical_not(has_up))
    def _():
        zero_high[...] = jnp.zeros(zero_high.shape, zero_high.dtype)
        fill_high.start()
        fill_high.wait()

    store.wait()

    for copy in copies:
        copy.wait_send()

    @pl.when(has_up)
    def _():
        to_up.wait_send()
        to_down.wait_recv()

    @pl.when(has_down)
    def _():
        to_down.wait_send()
        to_up.wait_recv()


def exit_kernel(src_ref, matrix_ref, out_ref, landed, send_sem, recv_sem, local_sem, *, src_at, dst_at):
    count = lax.axis_size("lon")
    me = lax.axis_index("lon")
    lat = lax.axis_index("lat")
    levels = out_ref.shape[0]
    per = levels // CHUNKS
    barrier = greet(count, me, lat)
    pl.semaphore_wait(barrier, count - 1)
    copies = []
    locals_ = []
    for chunk in range(CHUNKS):
        part = pl.ds(chunk * per, per)
        row = []
        for offset in range(1, count):
            peer = lax.rem(me + offset, count)
            copy = pltpu.make_async_remote_copy(
                src_ref=src_at(src_ref, peer, part),
                dst_ref=dst_at(landed, me, part),
                send_sem=send_sem.at[chunk, offset],
                recv_sem=recv_sem.at[chunk, offset],
                device_id=(peer, lat),
                device_id_type=MESH_ID,
            )
            copy.start()
            row.append(copy)
        copies.append(row)
        local = pltpu.make_async_copy(src_at(src_ref, me, part), dst_at(landed, me, part), local_sem.at[chunk])
        local.start()
        locals_.append(local)
    for chunk in range(CHUNKS):
        for copy in copies[chunk]:
            copy.wait_recv()
        locals_[chunk].wait()

        def body(k, carry):
            out_ref[k] = permute_block(landed[k], matrix_ref[...])
            return carry

        lax.fori_loop(chunk * per, (chunk + 1) * per, body, 0)
    for row in copies:
        for copy in row:
            copy.wait_send()


def run_exchange(kernel, operand, matrix, out_shape, src_spec, out_spec, scratch, src_at, dst_at, ident):
    count = lax.axis_size("lon")
    return pl.pallas_call(
        functools.partial(kernel, src_at=src_at, dst_at=dst_at),
        out_shape=jax.ShapeDtypeStruct(out_shape, operand.dtype),
        in_specs=[src_spec, pl.BlockSpec(memory_space=pltpu.VMEM)],
        out_specs=out_spec,
        scratch_shapes=[
            pltpu.VMEM(scratch, operand.dtype),
            pltpu.SemaphoreType.DMA((CHUNKS, count)),
            pltpu.SemaphoreType.DMA((CHUNKS, count)),
            pltpu.SemaphoreType.DMA((CHUNKS,)),
        ],
        compiler_params=pltpu.CompilerParams(collective_id=ident, has_side_effects=True),
    )(operand, matrix)


def to_columns(block):
    levels, rows, width = block.shape
    cells = width // NTR
    devices = lax.axis_size("lon")
    parts = devices // (NTR // PAIR)
    count = rows // parts
    lane = cells * PAIR

    def src_at(ref, peer, part):
        return ref.at[part, pl.ds((peer % parts) * count, count), pl.ds((peer // parts) * lane, lane)]

    def dst_at(ref, sender, part):
        return ref.at[part, :, pl.ds(sender * lane, lane)]

    vmem = pl.BlockSpec(memory_space=pltpu.VMEM)
    hbm = pl.BlockSpec(memory_space=pl.ANY)
    field_shape = (levels, count, devices * lane)
    below_shape = (levels, 2, devices * lane)
    above_shape = (levels, 3, devices * lane)
    return pl.pallas_call(
        functools.partial(entry_kernel, src_at=src_at, dst_at=dst_at, parts=parts),
        out_shape=tuple(jax.ShapeDtypeStruct(shape, block.dtype) for shape in (field_shape, below_shape, above_shape)),
        in_specs=[vmem, vmem],
        out_specs=(hbm, hbm, hbm),
        scratch_shapes=[
            pltpu.VMEM(block.shape, block.dtype),
            pltpu.VMEM(field_shape, block.dtype),
            pltpu.VMEM(below_shape, block.dtype),
            pltpu.VMEM(above_shape, block.dtype),
            pltpu.VMEM(below_shape, block.dtype),
            pltpu.VMEM(above_shape, block.dtype),
            pltpu.SemaphoreType.DMA((CHUNKS, devices)),
            pltpu.SemaphoreType.DMA((CHUNKS, devices)),
            pltpu.SemaphoreType.DMA((CHUNKS,)),
            pltpu.SemaphoreType.DMA((2,)),
            pltpu.SemaphoreType.DMA((2,)),
            pltpu.SemaphoreType.DMA((3,)),
        ],
        compiler_params=pltpu.CompilerParams(collective_id=0, has_side_effects=True),
    )(block, permutation(pair_order(cells), False))


def from_columns(field, rows):
    levels, count, width = field.shape
    devices = lax.axis_size("lon")
    parts = devices // (NTR // PAIR)
    lane = width // devices
    cells = lane // PAIR

    def src_at(ref, peer, part):
        return ref.at[part, :, pl.ds(peer * lane, lane)]

    def dst_at(ref, sender, part):
        return ref.at[part, pl.ds((sender % parts) * count, count), pl.ds((sender // parts) * lane, lane)]

    shape = (levels, rows, cells * NTR)
    return run_exchange(
        exit_kernel, field, permutation(pair_order(cells), True), shape,
        pl.BlockSpec(memory_space=pl.ANY), pl.BlockSpec(memory_space=pltpu.VMEM), shape,
        src_at, dst_at, 1,
    )


def lat_halo(field, width):
    lon_n = lax.axis_size("lon")
    lat_n = lax.axis_size("lat")
    parts = lon_n // (NTR // PAIR)
    up = []
    for b in range(lat_n):
        for l in range(lon_n):
            t, h = l // parts, l % parts
            g = b * parts + h
            if g + 1 < lat_n * parts:
                nb, nh = (g + 1) // parts, (g + 1) % parts
                up.append((l * lat_n + b, (t * parts + nh) * lat_n + nb))
    down = [(d, s) for s, d in up]
    rows = field.shape[1]
    below = lax.ppermute(field[:, rows - width + 1 :], ("lon", "lat"), up)
    above = lax.ppermute(field[:, :width], ("lon", "lat"), down)
    return jnp.concatenate([below[:, :1], below, field, above], axis=1)


def roll_rows(field, shift):
    cells = field.shape[2] // PAIR
    reach = cells // 4
    amount = shift + reach
    current = jnp.roll(field, -PAIR * reach, axis=2)
    stages = (2 * reach - 1).bit_length()
    position = 0
    while position < stages:
        step = PAIR * 2**position
        if position + 1 < stages and step >= 128:
            one = jnp.roll(current, step, axis=2)
            two = jnp.roll(current, 2 * step, axis=2)
            three = jnp.roll(current, 3 * step, axis=2)
            low, high = bit_mask(amount, position), bit_mask(amount, position + 1)
            current = jnp.where(high, jnp.where(low, three, two), jnp.where(low, one, current))
            position += 2
        else:
            moved = jnp.roll(current, step, axis=2)
            current = jnp.where(bit_mask(amount, position), moved, current)
            position += 1
    return current


def lon_cubic(shifted, fraction):
    weights = cubic_weights(fraction)
    taps = [jnp.roll(shifted, PAIR * (1 - p), axis=2) for p in range(4)]
    summed = None
    for p in range(4):
        addend = weights[p][:, :, None] * taps[p]
        summed = addend if summed is None else summed + addend
    return summed


def own_rows(values, count):
    parts = lax.axis_size("lon") // (NTR // PAIR)
    start = (lax.axis_index("lon") % parts) * count
    return lax.dynamic_slice_in_dim(values, start, count, axis=values.ndim - 1)


def per_device(tracers, lon_shift, lon_frac, lat_shift, lat_frac, remap_frac, diffusivity):
    rows = tracers.shape[1]
    field, below, above = to_columns(tracers)
    count = field.shape[1]
    width = field.shape[2]
    lon_shift, lon_frac, lat_shift, lat_frac, remap_frac, diffusivity = (
        own_rows(v, count) for v in (lon_shift, lon_frac, lat_shift, lat_frac, remap_frac, diffusivity)
    )
    for time_step in range(STEPS):
        if time_step == 0:
            padded = jnp.concatenate([below[:, :1], below, field, above], axis=1)
        else:
            padded = lat_halo(field, 3)
        field = lat_step(padded, lat_shift[time_step], lat_frac[time_step], count)
        field = lon_cubic(roll_rows(field, lon_shift[time_step]), lon_frac[time_step])
        field = remap(field, remap_frac[time_step])
        field = diffuse(field, diffusivity)
    return from_columns(field, rows)


def solution(mesh):
    in_specs = (
        P(None, "lat", "lon"),
        P(None, None, "lat"),
        P(None, None, "lat"),
        P(None, None, "lat"),
        P(None, None, "lat"),
        P(None, None, "lat"),
        P(None, "lat"),
    )
    out_specs = P(None, "lat", "lon")
    return jax.shard_map(
        per_device, mesh=mesh, in_specs=in_specs, out_specs=out_specs, check_vma=False
    )
```
